256 devices in a mesh: snp: 16 (over z, y_hi), samp: 16 (over y_lo, x, core).
Axes of the slice: x: 4, y: 4 (y_hi: 2, y_lo: 2; y = y_hi * 2 + y_lo), z: 8, core: 2. Of those that a mesh axis runs over, the one named last changes fastest.
Arguments:
- dosage: bfloat16 [20480, 16384], P('samp', 'snp'), may hold values from 0 to 2, as said below
- observed: int32 [20480, 16384], P('samp', 'snp'), may hold values 0 or 1
- band: int32 [16], replicated, may hold values from 1 to 2
Outputs:
- linkage: float32 [16384, 5120], P(('snp', 'samp'))
The draws below stay inside these ranges and needn't reach their ends.
Inputs may be any that keep to these rules, and one draw needn't show every extreme that they name: `dosage`: real-valued dosages.
All inputs are finite; a program needn't handle non-finite values. No bound on the sum of `observed` on one device may be relied on, other than what follows from the above.
Results may differ from the reference program's by a relative error of at most 0.00055.
Values may be sent and summed in bfloat16 or wider, within the bound.
No kernel may reach another device: no remote copies, remote signals or barrier semaphores. Data moves between devices by JAX's collectives and lax.ppermute only.
A program may use at most 128 MiB of HBM per device.

```python
import jax
import jax.numpy as jnp
from jax import lax

B = 1024
NBLK = 16
NSNP = 16384
SAMPLES = 20480


def draw_dosage(key, part):
    keys = jax.random.split(key, 10)
    count = max(B // 4, 4)
    shape = (NBLK + 2, count)
    factors = jax.random.normal(keys[0], (SAMPLES, NBLK + 2, count), jnp.float32)
    starts = (jnp.arange(NBLK + 2, dtype=jnp.int32)[:, None] - 2) * B + jax.random.randint(keys[1], shape, 0, B)
    top = (2 * B).bit_length() - 1
    exponent = jax.random.randint(keys[2], shape, 4, top)
    powers = jnp.left_shift(jnp.ones_like(exponent), exponent)
    lengths = powers + jax.random.randint(keys[3], shape, 0, 1048576) % powers
    signs = (2 * jax.random.randint(keys[4], shape, 0, 2) - 1).astype(jnp.float32)

    def one_block(blk):
        near = lax.dynamic_slice_in_dim(factors, blk, 3, 1).reshape(SAMPLES, 3 * count)
        first = lax.dynamic_slice_in_dim(starts, blk, 3, 0).reshape(3 * count)
        span = lax.dynamic_slice_in_dim(lengths, blk, 3, 0).reshape(3 * count)
        sign = lax.dynamic_slice_in_dim(signs, blk, 3, 0).reshape(3 * count)
        column = blk * B + jnp.arange(B, dtype=jnp.int32)
        cover = (first[:, None] <= column[None, :]) & (column[None, :] < first[:, None] + span[:, None])
        loads = sign[:, None] * (0.5 + 0.5 * jax.random.normal(jax.random.fold_in(keys[5], blk), (3 * count, B), jnp.float32))
        loads = jnp.where(cover, loads, 0.0)
        scale = lax.rsqrt(jnp.sum(loads * loads, axis=0) + 0.25)
        return jnp.dot(near, loads) * scale[None, :]
    latent = lax.map(one_block, jnp.arange(NBLK, dtype=jnp.int32))
    latent = jnp.transpose(latent, (1, 0, 2)).reshape(SAMPLES, NSNP)
    latent = latent + 0.6 * jax.random.normal(keys[6], (SAMPLES, NSNP), jnp.float32)
    ramp = jnp.arange(SAMPLES, dtype=jnp.float32) / SAMPLES - 0.5
    tilt = jax.random.uniform(keys[7], (NSNP,), jnp.float32, -1.5, 1.5)
    slope = jax.random.uniform(keys[8], (NSNP,), jnp.float32, 0.6, 1.6)
    offset = 0.7 * jax.random.normal(keys[9], (NSNP,), jnp.float32)
    latent = latent + ramp[:, None] * tilt[None, :]
    return (2.0 * jax.nn.sigmoid(slope * latent + offset)).astype(jnp.bfloat16)


def plant(values, own_key, smallest, top_value):
    shape = values.shape
    index_at = [jax.random.randint(jax.random.fold_in(own_key, axis), (), 0, shape[axis]) for axis in range(len(shape))]
    values = values.at[tuple(index_at)].set(smallest)
    longest = shape.index(max(shape))
    index_at[longest] = (index_at[longest] + 1) % shape[longest]
    return values.at[tuple(index_at)].set(top_value)


def setup_inputs(seed: int = 0) -> dict:
    key_of = jax.random.split(jax.random.key(seed), 4)
    dosage = draw_dosage(jax.random.fold_in(key_of[3], 71), 0)
    observed = plant((jax.random.randint(key_of[1], (SAMPLES, NSNP), 0, 10) < 9).astype(jnp.int32), jax.random.fold_in(key_of[1], 1), 0, 1)
    band = plant(jax.random.randint(key_of[2], (NBLK,), 1, 3), jax.random.fold_in(key_of[2], 1), 1, 2).astype(jnp.int32)
    return {"dosage": dosage, "observed": observed, "band": band}


eps = 1e-05

def reference(dosage, observed, band):
    weight = observed.astype(jnp.float32)
    values = dosage.astype(jnp.float32)
    cnt = lax.optimization_barrier(jnp.sum(weight, axis=0))
    first = lax.optimization_barrier(jnp.sum(weight * values, axis=0))
    second = lax.optimization_barrier(jnp.sum(weight * values * values, axis=0))
    mean = first / cnt
    spread = second - first * mean
    zed = (weight * (values - mean) * lax.rsqrt(spread + eps * cnt)).astype(jnp.bfloat16)
    padded = jnp.pad(zed, ((0, 0), (2 * B, 2 * B)))
    offsets = jnp.arange(5, dtype=jnp.int32) - 2

    def one_block(blk):
        own = lax.dynamic_slice_in_dim(zed, blk * B, B, 1)
        near = lax.dynamic_slice_in_dim(padded, blk * B, 5 * B, 1)
        gram = jnp.dot(own.T, near, preferred_element_type=jnp.float32)
        other = blk + offsets
        inside = (other >= 0) & (other < NBLK)
        other_band = band[jnp.clip(other, 0, NBLK - 1)]
        keep = inside & (jnp.abs(offsets) <= jnp.minimum(band[blk], other_band))
        keep = jnp.where(keep, 1.0, 0.0).astype(jnp.float32)
        return (gram.reshape(B, 5, B) * keep[None, :, None]).reshape(B, 5 * B)
    result = lax.map(one_block, jnp.arange(NBLK, dtype=jnp.int32))
    return result.reshape(NSNP, 5 * B)
```

```python
import functools

import jax
import jax.numpy as jnp
from jax import lax
from jax.experimental import pallas as pl
from jax.experimental.pallas import tpu as pltpu
from jax.sharding import Mesh
from jax.sharding import PartitionSpec as P

eps = 1e-05

AXES = ("z", "yh", "yl", "x", "core")
SIZES = (8, 2, 2, 4, 2)
SNP = ("z", "yh")
SAMP = ("yl", "x", "core")
NSNP = 16
PIECES = 8
SWAP = [(0, 1), (1, 0)]
HOP_U = [(i, i ^ 1) for i in range(4)]
HOP_W = [(i, 3 - i) for i in range(4)]
HOPS = ((("yl"), SWAP), (("x"), HOP_W), (("x"), HOP_U))
ORDERS = ((2, 1, 0), (1, 0, 2), (0, 2, 1))
TO_OTHER = [(i, i ^ 1) for i in range(NSNP)]
EVEN_DOWN = [(i + 2, i) for i in range(0, NSNP - 2, 2)]
ODD_UP = [(i, i + 2) for i in range(1, NSNP - 2, 2)]
EVEN_UP = [(i, i + 2) for i in range(0, NSNP - 2, 2)]
ODD_DOWN = [(i + 2, i) for i in range(1, NSNP - 2, 2)]


def sum_over_samples(x):
    parts = [
        lax.ppermute(x, ("yl", "core"), [(i, i ^ k) for i in range(4)]) for k in (1, 2, 3)
    ]
    x = x + parts[0] + parts[1] + parts[2]
    parts = [
        lax.ppermute(x, "x", [(i, (i + k) % 4) for i in range(4)]) for k in (1, 2, 3)
    ]
    return x + parts[0] + parts[1] + parts[2]


def pair_kept(band, mine, offset):
    total = band.shape[0]
    other = mine + offset
    inside = (other >= 0) & (other < total)
    other_band = band[jnp.clip(other, 0, total - 1)]
    keep = inside & (abs(offset) <= jnp.minimum(band[mine], other_band))
    return jnp.where(keep, 1.0, 0.0).astype(jnp.float32)


def product_kernel(meta, left_ref, first_ref, second_ref, keep_ref, send_ref):
    lower = meta[PIECES] == 0

    def store(right):
        for g in range(4):
            acc = jnp.dot(
                left_ref[256 * g : 256 * (g + 1), :], right, preferred_element_type=jnp.float32
            )
            for h in range(2):
                at = meta[2 * g + h]
                low = acc[128 * h : 128 * h + 64]
                high = acc[128 * h + 64 : 128 * h + 128]
                keep_ref[at] = jnp.where(lower, low, high)
                send_ref[at] = jnp.where(lower, high, low)

    @pl.when(meta[PIECES + 1] == 0)
    def _():
        store(first_ref[...])

    @pl.when(meta[PIECES + 1] != 0)
    def _():
        store(second_ref[...])


def product(meta, left, first, second, name):
    rows, depth = left.shape
    columns = first.shape[1]
    width = min(512, columns)
    pieces = jax.ShapeDtypeStruct((PIECES, rows // 16, columns), jnp.float32)
    right = pl.BlockSpec((depth, width), lambda j, m: (0, j))
    out = pl.BlockSpec((PIECES, rows // 16, width), lambda j, m: (0, 0, j))
    return pl.pallas_call(
        product_kernel,
        name=name,
        out_shape=(pieces, pieces),
        grid_spec=pltpu.PrefetchScalarGridSpec(
            num_scalar_prefetch=1,
            grid=(columns // width,),
            in_specs=[pl.BlockSpec((rows, depth), lambda j, m: (0, 0)), right, right],
            out_specs=(out, out),
        ),
        compiler_params=pltpu.CompilerParams(vmem_limit_bytes=48 << 20),
        cost_estimate=pl.CostEstimate(
            flops=2 * rows * depth * columns,
            bytes_accessed=2 * rows * depth + 4 * depth * columns + 4 * rows * columns,
            transcendentals=0,
        ),
    )(meta, left, first, second)


def scatter_sum(pair, cuts):
    keep, send = pair
    x = keep + lax.ppermute(send, "core", SWAP)
    _, rows, columns = x.shape
    x = x.reshape(2, 2, 2, rows, columns)
    done = []
    begin = 0
    for order, width in zip(ORDERS, cuts):
        part = x[..., begin : begin + width]
        begin += width
        axes = [0, 1, 2]
        for hop in order:
            axis, pairs = HOPS[hop]
            at = axes.index(hop)
            axes.remove(hop)
            out = lax.index_in_dim(part, 1, at, keepdims=False)
            part = lax.index_in_dim(part, 0, at, keepdims=False) + lax.ppermute(out, axis, pairs)
        done.append(part)
    return jnp.concatenate(done, axis=-1)


def transposed(rows_a, rows_b):
    size, columns = rows_a.shape
    both = jnp.stack([rows_a.reshape(size, 16, size), rows_b.reshape(size, 16, size)], axis=2)
    both = both.transpose(1, 0, 2, 3).reshape(16, size, 2 * size)
    both = lax.all_to_all(both, SAMP, 0, 0)
    both = both.reshape(columns, 2 * size).T
    return both[:size], both[size:]


def on_device(dosage, observed, band):
    width = dosage.shape[1]
    mine = lax.axis_index(SNP)
    odd = lax.axis_index("yh")
    at_x = lax.axis_index("x")
    at_y = lax.axis_index("yl")
    code = lambda x: 2 * (x >> 1) + ((x >> 1) ^ (x & 1))
    piece = jnp.arange(PIECES, dtype=jnp.int32)
    relative = (4 * (piece >> 2) + code(piece & 3)) ^ (4 * at_y + code(at_x))
    core = lax.axis_index("core").reshape(1)
    zero = jnp.zeros((1,), jnp.int32)
    meta = jnp.concatenate([relative, core, zero]).astype(jnp.int32)
    meta_odd = jnp.concatenate([relative, core, odd.reshape(1)]).astype(jnp.int32)

    weight = observed.astype(jnp.float32)
    values = dosage.astype(jnp.float32)
    sums = jnp.stack(
        [
            jnp.sum(weight, axis=0),
            jnp.sum(weight * values, axis=0),
            jnp.sum(weight * values * values, axis=0),
        ]
    )
    cnt, first, second = sum_over_samples(sums)
    mean = first / cnt
    spread = second - first * mean
    zed = (weight * (values - mean) * lax.rsqrt(spread + eps * cnt)).astype(jnp.bfloat16)
    flipped = zed.T
    along = lax.ppermute(zed, SNP, EVEN_DOWN + ODD_UP)
    across = lax.ppermute(flipped, SNP, TO_OTHER)

    rows0 = scatter_sum(product(meta, flipped, zed, zed, "own"), (384, 384, 256))
    keep2, send2 = product(meta, flipped, along, along, "along")
    keep1, send1 = product(meta_odd, across, along, zed, "across")
    rows2 = scatter_sum((keep2, send2), (384, 384, 256))
    rows1 = scatter_sum((keep1, send1), (256, 384, 384))

    beside = lax.ppermute(rows1, SNP, TO_OTHER)
    turned2, turned1 = transposed(rows2, rows1)
    far = lax.ppermute(turned2, SNP, EVEN_UP + ODD_DOWN)
    near = lax.ppermute(turned1, SNP, EVEN_UP)

    keeps = [pair_kept(band, mine, offset) for offset in (-2, -1, 0, 1, 2)]
    even = odd == 0
    return jnp.concatenate(
        [
            jnp.where(even, far, rows2) * keeps[0],
            jnp.where(even, near, turned1) * keeps[1],
            rows0 * keeps[2],
            beside * keeps[3],
            jnp.where(even, rows2, far) * keeps[4],
        ],
        axis=1,
    )


def solution(mesh):
    whole = Mesh(mesh.devices.reshape(SIZES), AXES)
    return jax.shard_map(
        on_device,
        mesh=whole,
        in_specs=(P(SAMP, SNP), P(SAMP, SNP), P()),
        out_specs=P(AXES, None),
        check_vma=False,
    )
```

```python
import jax
import jax.numpy as jnp
from jax import lax
from jax.experimental import pallas as pl
from jax.experimental.pallas import tpu as pltpu
from jax.sharding import Mesh
from jax.sharding import PartitionSpec as P

eps = 1e-05

AXES = ("z", "yh", "yl", "x", "core")
SIZES = (8, 2, 2, 4, 2)
SNP = ("z", "yh")
SAMP = ("yl", "x", "core")
CHIP = ("yl", "x")
NSNP = 16
B = 1024
DEPTH = 1280
HALF = B // 2
STEP = 256
PIECES = 8
ROWS = 64
TURN = 32
SWAP = [(0, 1), (1, 0)]
TO_OTHER = [(i, i ^ 1) for i in range(NSNP)]
EVEN_DOWN = [(i + 2, i) for i in range(0, NSNP - 2, 2)]
ODD_UP = [(i, i + 2) for i in range(1, NSNP - 2, 2)]
EVEN_UP = [(i, i + 2) for i in range(0, NSNP - 2, 2)]
ODD_DOWN = [(i + 2, i) for i in range(1, NSNP - 2, 2)]


def sum_over_samples(x):
    parts = [
        lax.ppermute(x, ("yl", "core"), [(i, i ^ k) for i in range(4)]) for k in (1, 2, 3)
    ]
    x = x + parts[0] + parts[1] + parts[2]
    parts = [
        lax.ppermute(x, "x", [(i, (i + k) % 4) for i in range(4)]) for k in (1, 2, 3)
    ]
    return x + parts[0] + parts[1] + parts[2]


def params():
    return pltpu.CompilerParams(vmem_limit_bytes=56 << 20)


def cost(flops, moved):
    return pl.CostEstimate(flops=1024, bytes_accessed=1024, transcendentals=0)


def whole(shape):
    return pl.BlockSpec(shape, lambda j, m: (0,) * len(shape))


def f32(*shape):
    return jax.ShapeDtypeStruct(shape, jnp.float32)


def bf16(*shape):
    return jax.ShapeDtypeStruct(shape, jnp.bfloat16)


def matmul(left, right):
    return jnp.dot(left, right, preferred_element_type=jnp.float32)


def standard_kernel(meta, dosage, observed, stats, zed, zed0, zed1, kept0, kept1, sent0, sent1):
    weight = observed[...].astype(jnp.float32)
    values = dosage[...].astype(jnp.float32)
    z = (weight * (values - stats[0:1, :]) * stats[1:2, :]).astype(jnp.bfloat16)
    zed[...] = z
    zed0[...] = z[:, :HALF]
    zed1[...] = z[:, HALF:]
    turned = z.T

    def store(*outs):
        for c in range(PIECES):
            for k, out in enumerate(outs):
                at = 2 * ROWS * c + TURN * k
                out[c] = turned[at : at + TURN]

    pl.when(meta[0] == 0)(lambda: store(kept0, kept1, sent0, sent1))
    pl.when(meta[0] != 0)(lambda: store(sent0, sent1, kept0, kept1))


def standardize(meta, dosage, observed, stats):
    rows = 256
    block = lambda width: pl.BlockSpec((rows, width), lambda i, m: (i, 0))
    turned = pl.BlockSpec((PIECES, TURN, rows), lambda i, m: (0, 0, i))
    return pl.pallas_call(
        standard_kernel,
        name="standardize",
        out_shape=(bf16(DEPTH, B), bf16(DEPTH, HALF), bf16(DEPTH, HALF))
        + (bf16(PIECES, TURN, DEPTH),) * 4,
        grid_spec=pltpu.PrefetchScalarGridSpec(
            num_scalar_prefetch=1,
            grid=(DEPTH // rows,),
            in_specs=[block(B), block(B), whole((2, B))],
            out_specs=(block(B), block(HALF), block(HALF)) + (turned,) * 4,
        ),
        compiler_params=params(),
        cost_estimate=cost(4 * DEPTH * B, 12 * DEPTH * B),
    )(meta, dosage, observed, stats)


LEFT = (PIECES * TURN, DEPTH)


def flat(*turned):
    return [t.reshape(LEFT) for t in turned]


def own_kernel(meta, kept0, kept1, sent0, sent1, right, out):
    core = meta[0]
    r = right[...]
    for left, half, at in (
        (kept0, core, 0),
        (kept1, core, TURN),
        (sent0, 1 - core, 0),
        (sent1, 1 - core, TURN),
    ):
        acc = matmul(left[...], r)
        for c in range(PIECES):
            out[c, half, at : at + TURN] = acc[TURN * c : TURN * (c + 1)]


def own_product(meta, turned, zed):
    out = pl.pallas_call(
        own_kernel,
        name="own",
        out_shape=f32(PIECES, 2, ROWS, B),
        grid_spec=pltpu.PrefetchScalarGridSpec(
            num_scalar_prefetch=1,
            grid=(B // STEP,),
            in_specs=[whole(LEFT)] * 4 + [pl.BlockSpec((DEPTH, STEP), lambda j, m: (0, j))],
            out_specs=pl.BlockSpec((PIECES, 2, ROWS, STEP), lambda j, m: (0, 0, 0, j)),
        ),
        compiler_params=params(),
        cost_estimate=cost(2 * DEPTH * B * B, 4 * DEPTH * B + 4 * B * B),
    )(meta, *flat(*turned), zed)
    return out.reshape(B, B)


def turn_kernel(meta, zed, out0, out1):
    turned = zed[...].T

    def store(at):
        out0[0] = turned[at : at + TURN]
        out1[0] = turned[at + TURN : at + ROWS]

    pl.when(meta[0] == 0)(lambda: store(0))
    pl.when(meta[0] != 0)(lambda: store(ROWS))


def turn(meta, zed):
    out = pl.BlockSpec((1, TURN, DEPTH), lambda c, m: (c, 0, 0))
    return pl.pallas_call(
        turn_kernel,
        name="turn",
        out_shape=(bf16(PIECES, TURN, DEPTH),) * 2,
        grid_spec=pltpu.PrefetchScalarGridSpec(
            num_scalar_prefetch=1,
            grid=(PIECES,),
            in_specs=[pl.BlockSpec((DEPTH, 2 * ROWS), lambda c, m: (0, c))],
            out_specs=(out, out),
        ),
        compiler_params=params(),
        cost_estimate=cost(DEPTH * B, 3 * DEPTH * B),
    )(meta, zed)


def store_pieces(out, at, left_a, left_b, right_a, right_b):
    acc = matmul(left_a[...], right_a[...]) + matmul(left_b[...], right_b[...])
    out[:, at : at + TURN] = acc.reshape(PIECES, TURN, STEP)


def early_kernel(
    meta, own0_a, own1_a, own0_b, own1_b, other_a, other_b, near_a, near_b, zed_a, zed_b, out
):
    store_pieces(out, 0, own0_a, own0_b, near_a, near_b)
    store_pieces(out, TURN, own1_a, own1_b, near_a, near_b)
    even = meta[1] == 0
    pl.when(even)(lambda: store_pieces(out, ROWS, other_a, other_b, near_a, near_b))
    pl.when(~even)(lambda: store_pieces(out, ROWS, other_a, other_b, zed_a, zed_b))


def early_product(meta, own_a, own_b, other, near, zed):
    right = pl.BlockSpec((DEPTH, STEP), lambda j, m: (0, j))
    rows = ROWS + TURN
    return pl.pallas_call(
        early_kernel,
        name="early",
        out_shape=f32(PIECES, rows, HALF),
        grid_spec=pltpu.PrefetchScalarGridSpec(
            num_scalar_prefetch=1,
            grid=(HALF // STEP,),
            in_specs=[whole(LEFT)] * 6 + [right] * 4,
            out_specs=pl.BlockSpec((PIECES, rows, STEP), lambda j, m: (0, 0, j)),
        ),
        compiler_params=params(),
        cost_estimate=cost(32 * DEPTH * rows * HALF, 10 * DEPTH * B + 32 * rows * HALF),
    )(meta, *flat(*own_a, *own_b, *other), *near, *zed)


def late_kernel(
    meta,
    own0_a,
    own1_a,
    own0_b,
    own1_b,
    other0_a,
    other0_b,
    other1_a,
    other1_b,
    near0_a,
    near0_b,
    near1_a,
    near1_b,
    zed0_a,
    zed0_b,
    zed1_a,
    zed1_b,
    out,
):
    def across(first_a, first_b, second_a, second_b):
        store_pieces(out, ROWS, other0_a, other0_b, second_a, second_b)
        store_pieces(out, ROWS + TURN, other1_a, other1_b, second_a, second_b)
        store_pieces(out, 2 * ROWS, other1_a, other1_b, first_a, first_b)

    store_pieces(out, 0, own0_a, own0_b, near1_a, near1_b)
    store_pieces(out, TURN, own1_a, own1_b, near1_a, near1_b)
    even = meta[1] == 0
    pl.when(even)(lambda: across(near0_a, near0_b, near1_a, near1_b))
    pl.when(~even)(lambda: across(zed0_a, zed0_b, zed1_a, zed1_b))


def late_product(meta, own_a, own_b, other0, other1, near0, near1, zed):
    right = pl.BlockSpec((DEPTH, STEP), lambda j, m: (0, j))
    second = pl.BlockSpec((DEPTH, STEP), lambda j, m: (0, j + HALF // STEP))
    rows = 2 * ROWS + TURN
    return pl.pallas_call(
        late_kernel,
        name="late",
        out_shape=f32(PIECES, rows, HALF),
        grid_spec=pltpu.PrefetchScalarGridSpec(
            num_scalar_prefetch=1,
            grid=(HALF // STEP,),
            in_specs=[whole(LEFT)] * 8 + [right] * 6 + [second] * 2,
            out_specs=pl.BlockSpec((PIECES, rows, STEP), lambda j, m: (0, 0, j)),
        ),
        compiler_params=params(),
        cost_estimate=cost(32 * DEPTH * rows * HALF, 16 * DEPTH * B + 32 * rows * HALF),
    )(meta, *flat(*own_a, *own_b, *other0, *other1), *near0, *near1, *zed, *zed)


def gather_kernel(meta, early, late, rows2, rows1, both):
    a = early[0]
    b = late[0]
    for r in range(1, PIECES):
        a = a + early[r]
        b = b + late[r]
    rows2[:, :HALF] = a[:ROWS]
    rows2[:, HALF:] = b[:ROWS]
    rows1[:TURN, :HALF] = a[ROWS:]
    rows1[:TURN, HALF:] = b[ROWS : ROWS + TURN]
    rows1[TURN:, HALF:] = b[ROWS + TURN : 2 * ROWS]
    rows1[TURN:, :HALF] = b[2 * ROWS :]
    for s in range(2 * PIECES):
        both[s, :, :ROWS] = rows2[:, ROWS * s : ROWS * (s + 1)]
        both[s, :, ROWS:] = rows1[:, ROWS * s : ROWS * (s + 1)]


def gather_pieces(meta, early, late):
    return pl.pallas_call(
        gather_kernel,
        name="gather",
        out_shape=(f32(ROWS, B), f32(ROWS, B), f32(2 * PIECES, ROWS, 2 * ROWS)),
        grid_spec=pltpu.PrefetchScalarGridSpec(
            num_scalar_prefetch=1,
            grid=(1,),
            in_specs=[whole(early.shape), whole(late.shape)],
            out_specs=(
                whole((ROWS, B)),
                whole((ROWS, B)),
                whole((2 * PIECES, ROWS, 2 * ROWS)),
            ),
        ),
        compiler_params=params(),
        cost_estimate=cost(PIECES * ROWS * 2 * B, 4 * PIECES * ROWS * 2 * B),
    )(meta, early, late)


def assemble_kernel(flags, far, here, rows2, beside, rows0, out):
    even = flags[5] == 0
    far_turned = far[...].T
    near = jnp.where(even, far_turned[ROWS:], here[...].T[ROWS:])
    far2 = far_turned[:ROWS]
    mine2 = rows2[...]
    blocks = (
        jnp.where(even, far2, mine2),
        near,
        rows0[...],
        beside[...],
        jnp.where(even, mine2, far2),
    )
    for d, block in enumerate(blocks):
        out[:, B * d : B * (d + 1)] = jnp.where(flags[d] > 0, block, 0.0)


def assemble(flags, far, here, rows2, beside, rows0):
    return pl.pallas_call(
        assemble_kernel,
        name="assemble",
        out_shape=f32(ROWS, 5 * B),
        grid_spec=pltpu.PrefetchScalarGridSpec(
            num_scalar_prefetch=1,
            grid=(1,),
            in_specs=[whole((B, 2 * ROWS))] * 2 + [whole((ROWS, B))] * 3,
            out_specs=whole((ROWS, 5 * B)),
        ),
        compiler_params=params(),
        cost_estimate=cost(ROWS * 5 * B, 40 * ROWS * B),
    )(flags, far, here, rows2, beside, rows0)


def kept_flags(band, mine):
    total = band.shape[0]
    offsets = jnp.arange(5, dtype=jnp.int32) - 2
    other = mine + offsets
    inside = (other >= 0) & (other < total)
    reach = jnp.minimum(band[mine], band[jnp.clip(other, 0, total - 1)])
    return (inside & (jnp.abs(offsets) <= reach)).astype(jnp.int32)


def on_device(dosage, observed, band):
    mine = lax.axis_index(SNP)
    odd = lax.axis_index("yh").reshape(1)
    core = lax.axis_index("core").reshape(1)
    meta = jnp.concatenate([core, odd]).astype(jnp.int32)

    weight = observed.astype(jnp.float32)
    values = dosage.astype(jnp.float32)
    sums = jnp.stack(
        [
            jnp.sum(weight, axis=0),
            jnp.sum(weight * values, axis=0),
            jnp.sum(weight * values * values, axis=0),
        ]
    )
    cnt, first, second = sum_over_samples(sums)
    mean = first / cnt
    spread = second - first * mean
    stats = jnp.stack([mean, lax.rsqrt(spread + eps * cnt)])

    zed, zed0, zed1, kept0, kept1, sent0, sent1 = standardize(meta, dosage, observed, stats)
    along = lambda t: lax.ppermute(t, SNP, EVEN_DOWN + ODD_UP)
    across = lambda t: lax.ppermute(t, SNP, TO_OTHER)
    athwart = lambda t: lax.ppermute(t, ("yh", "core"), [(i, 3 - i) for i in range(4)])
    swap = lambda t: lax.ppermute(t, "core", SWAP)
    zed_b = swap(zed)
    near0 = along(zed0)
    other0 = (across(kept0), athwart(sent0))
    near1 = along(zed1)
    other1 = (across(kept1), athwart(sent1))

    own = own_product(meta, (kept0, kept1, sent0, sent1), zed)
    rows0 = lax.psum_scatter(own, SAMP, scatter_dimension=0, tiled=True)
    near0, zed_b, other0 = lax.optimization_barrier((near0, zed_b, other0))
    own_a = (kept0, kept1)
    own_b = turn(meta, zed_b)
    near0 = (near0, swap(near0))
    early = early_product(meta, own_a, own_b, other0, near0, (zed, zed_b))
    early = lax.all_to_all(early, CHIP, 0, 0)
    near1, other1 = lax.optimization_barrier((near1, other1))
    near1 = (near1, swap(near1))
    late = late_product(meta, own_a, own_b, other0, other1, near0, near1, (zed, zed_b))
    late = lax.all_to_all(late, CHIP, 0, 0)
    rows2, rows1, both = gather_pieces(meta, early, late)
    beside = lax.ppermute(rows1, SNP, TO_OTHER)
    here = lax.all_to_all(both, SAMP, 0, 0).reshape(B, 2 * ROWS)
    far = lax.ppermute(here, SNP, EVEN_UP + ODD_DOWN)
    flags = jnp.concatenate([kept_flags(band, mine), odd]).astype(jnp.int32)
    return assemble(flags, far, here, rows2, beside, rows0)


def solution(mesh):
    whole_mesh = Mesh(mesh.devices.reshape(SIZES), AXES)
    return jax.shard_map(
        on_device,
        mesh=whole_mesh,
        in_specs=(P(SAMP, SNP), P(SAMP, SNP), P()),
        out_specs=P(AXES, None),
        check_vma=False,
    )
```

```python
import jax
import jax.numpy as jnp
from jax import lax
from jax.experimental import pallas as pl
from jax.experimental.pallas import tpu as pltpu
from jax.sharding import Mesh
from jax.sharding import PartitionSpec as P

eps = 1e-05

AXES = ("z", "yh", "yl", "x", "core")
SIZES = (8, 2, 2, 4, 2)
SNP = ("z", "yh")
SAMP = ("yl", "x", "core")
NSNP = 16
B = 1024
DEPTH = 1280
HALF = B // 2
STEP = 256
PIECES = 8
ROWS = 64
TURN = 32
SWAP = [(0, 1), (1, 0)]
TO_OTHER = [(i, i ^ 1) for i in range(NSNP)]
EVEN_DOWN = [(i + 2, i) for i in range(0, NSNP - 2, 2)]
ODD_UP = [(i, i + 2) for i in range(1, NSNP - 2, 2)]
EVEN_UP = [(i, i + 2) for i in range(0, NSNP - 2, 2)]
ODD_DOWN = [(i + 2, i) for i in range(1, NSNP - 2, 2)]


def sum_over_samples(x):
    parts = [
        lax.ppermute(x, ("yl", "core"), [(i, i ^ k) for i in range(4)]) for k in (1, 2, 3)
    ]
    x = x + parts[0] + parts[1] + parts[2]
    parts = [
        lax.ppermute(x, "x", [(i, (i + k) % 4) for i in range(4)]) for k in (1, 2, 3)
    ]
    return x + parts[0] + parts[1] + parts[2]


def chip_of(piece):
    return piece // 2 + 4 * (piece % 2)


def params():
    return pltpu.CompilerParams(vmem_limit_bytes=56 << 20)


def cost(flops, moved):
    return pl.CostEstimate(flops=1024, bytes_accessed=1024, transcendentals=0)


def whole(shape):
    return pl.BlockSpec(shape, lambda j, m: (0,) * len(shape))


def f32(*shape):
    return jax.ShapeDtypeStruct(shape, jnp.float32)


def bf16(*shape):
    return jax.ShapeDtypeStruct(shape, jnp.bfloat16)


def matmul(left, right):
    return jnp.dot(left, right, preferred_element_type=jnp.float32)


def standard_kernel(meta, dosage, observed, stats, zed, zed0, zed1, kept0, kept1, sent0, sent1):
    weight = observed[...].astype(jnp.float32)
    values = dosage[...].astype(jnp.float32)
    z = (weight * (values - stats[0:1, :]) * stats[1:2, :]).astype(jnp.bfloat16)
    zed[...] = z
    zed0[...] = z[:, :HALF]
    zed1[...] = z[:, HALF:]
    turned = z.T

    def store(*outs):
        for p in range(PIECES):
            for k, out in enumerate(outs):
                at = 2 * ROWS * chip_of(p) + TURN * k
                out[p] = turned[at : at + TURN]

    pl.when(meta[0] == 0)(lambda: store(kept0, kept1, sent0, sent1))
    pl.when(meta[0] != 0)(lambda: store(sent0, sent1, kept0, kept1))


def standardize(meta, dosage, observed, stats):
    rows = 256
    block = lambda width: pl.BlockSpec((rows, width), lambda i, m: (i, 0))
    turned = pl.BlockSpec((PIECES, TURN, rows), lambda i, m: (0, 0, i))
    return pl.pallas_call(
        standard_kernel,
        name="standardize",
        out_shape=(bf16(DEPTH, B), bf16(DEPTH, HALF), bf16(DEPTH, HALF))
        + (bf16(PIECES, TURN, DEPTH),) * 4,
        grid_spec=pltpu.PrefetchScalarGridSpec(
            num_scalar_prefetch=1,
            grid=(DEPTH // rows,),
            in_specs=[block(B), block(B), whole((2, B))],
            out_specs=(block(B), block(HALF), block(HALF)) + (turned,) * 4,
        ),
        compiler_params=params(),
        cost_estimate=cost(4 * DEPTH * B, 12 * DEPTH * B),
    )(meta, dosage, observed, stats)


LEFT = (PIECES * TURN, DEPTH)


def flat(*turned):
    return [t.reshape(LEFT) for t in turned]


def turn_kernel(meta, zed, out0, out1):
    turned = zed[...].T

    def store(at):
        out0[0] = turned[at : at + TURN]
        out1[0] = turned[at + TURN : at + ROWS]

    pl.when(meta[0] == 0)(lambda: store(0))
    pl.when(meta[0] != 0)(lambda: store(ROWS))


def turn(meta, zed):
    out = pl.BlockSpec((1, TURN, DEPTH), lambda c, m: (c, 0, 0))
    return pl.pallas_call(
        turn_kernel,
        name="turn",
        out_shape=(bf16(PIECES, TURN, DEPTH),) * 2,
        grid_spec=pltpu.PrefetchScalarGridSpec(
            num_scalar_prefetch=1,
            grid=(PIECES,),
            in_specs=[pl.BlockSpec((DEPTH, 2 * ROWS), lambda p, m: (0, p // 2 + 4 * (p % 2)))],
            out_specs=(out, out),
        ),
        compiler_params=params(),
        cost_estimate=cost(DEPTH * B, 3 * DEPTH * B),
    )(meta, zed)


def store_pieces(out, at, left_a, left_b, right_a, right_b):
    acc = matmul(left_a[...], right_a[...]) + matmul(left_b[...], right_b[...])
    out[:, at : at + TURN] = acc.reshape(PIECES, TURN, STEP)


def own_kernel(meta, own0_a, own1_a, own0_b, own1_b, zed_a, zed_b, out):
    store_pieces(out, 0, own0_a, own0_b, zed_a, zed_b)
    store_pieces(out, TURN, own1_a, own1_b, zed_a, zed_b)


def own_product(meta, own_a, own_b, zed):
    right = pl.BlockSpec((DEPTH, STEP), lambda j, m: (0, j))
    return pl.pallas_call(
        own_kernel,
        name="own",
        out_shape=f32(PIECES, ROWS, B),
        grid_spec=pltpu.PrefetchScalarGridSpec(
            num_scalar_prefetch=1,
            grid=(B // STEP,),
            in_specs=[whole(LEFT)] * 4 + [right] * 2,
            out_specs=pl.BlockSpec((PIECES, ROWS, STEP), lambda j, m: (0, 0, j)),
        ),
        compiler_params=params(),
        cost_estimate=cost(2 * DEPTH * B * B, 4 * DEPTH * B + 4 * B * B),
    )(meta, *flat(*own_a, *own_b), *zed)


def fold_kernel(meta, parts, keep, send):
    mine = meta[2]
    for out, half in ((keep, mine), (send, 1 - mine)):
        out[...] = parts[0, half] + parts[1, half] + parts[2, half] + parts[3, half]


def after(value, *others):
    return lax.optimization_barrier((value, *others))[0]


def fold(meta, parts, *others):
    _, rows, columns = parts.shape
    parts = after(lax.all_to_all(parts.reshape(4, 2, rows, columns), "x", 0, 0), *others)
    out = pl.BlockSpec((rows, STEP), lambda j, m: (0, j))
    keep, send = pl.pallas_call(
        fold_kernel,
        name="fold",
        out_shape=(f32(rows, columns),) * 2,
        grid_spec=pltpu.PrefetchScalarGridSpec(
            num_scalar_prefetch=1,
            grid=(columns // STEP,),
            in_specs=[pl.BlockSpec((4, 2, rows, STEP), lambda j, m: (0, 0, 0, j))],
            out_specs=(out, out),
        ),
        compiler_params=params(),
        cost_estimate=cost(6 * rows * columns, 40 * rows * columns),
    )(meta, parts)
    return keep, lax.ppermute(send, "yl", SWAP)


def early_kernel(
    meta, own0_a, own1_a, own0_b, own1_b, other_a, other_b, near_a, near_b, zed_a, zed_b, out
):
    store_pieces(out, 0, own0_a, own0_b, near_a, near_b)
    store_pieces(out, TURN, own1_a, own1_b, near_a, near_b)
    even = meta[1] == 0
    pl.when(even)(lambda: store_pieces(out, ROWS, other_a, other_b, near_a, near_b))
    pl.when(~even)(lambda: store_pieces(out, ROWS, other_a, other_b, zed_a, zed_b))


def early_product(meta, own_a, own_b, other, near, zed):
    right = pl.BlockSpec((DEPTH, STEP), lambda j, m: (0, j))
    rows = ROWS + TURN
    return pl.pallas_call(
        early_kernel,
        name="early",
        out_shape=f32(PIECES, rows, HALF),
        grid_spec=pltpu.PrefetchScalarGridSpec(
            num_scalar_prefetch=1,
            grid=(HALF // STEP,),
            in_specs=[whole(LEFT)] * 6 + [right] * 4,
            out_specs=pl.BlockSpec((PIECES, rows, STEP), lambda j, m: (0, 0, j)),
        ),
        compiler_params=params(),
        cost_estimate=cost(32 * DEPTH * rows * HALF, 10 * DEPTH * B + 32 * rows * HALF),
    )(meta, *flat(*own_a, *own_b, *other), *near, *zed)


def late_kernel(
    meta,
    own0_a,
    own1_a,
    own0_b,
    own1_b,
    other0_a,
    other0_b,
    other1_a,
    other1_b,
    near0_a,
    near0_b,
    near1_a,
    near1_b,
    zed0_a,
    zed0_b,
    zed1_a,
    zed1_b,
    out,
):
    def across(first_a, first_b, second_a, second_b):
        store_pieces(out, ROWS, other0_a, other0_b, second_a, second_b)
        store_pieces(out, ROWS + TURN, other1_a, other1_b, second_a, second_b)
        store_pieces(out, 2 * ROWS, other1_a, other1_b, first_a, first_b)

    store_pieces(out, 0, own0_a, own0_b, near1_a, near1_b)
    store_pieces(out, TURN, own1_a, own1_b, near1_a, near1_b)
    even = meta[1] == 0
    pl.when(even)(lambda: across(near0_a, near0_b, near1_a, near1_b))
    pl.when(~even)(lambda: across(zed0_a, zed0_b, zed1_a, zed1_b))


def late_product(meta, own_a, own_b, other0, other1, near0, near1, zed):
    right = pl.BlockSpec((DEPTH, STEP), lambda j, m: (0, j))
    second = pl.BlockSpec((DEPTH, STEP), lambda j, m: (0, j + HALF // STEP))
    rows = 2 * ROWS + TURN
    return pl.pallas_call(
        late_kernel,
        name="late",
        out_shape=f32(PIECES, rows, HALF),
        grid_spec=pltpu.PrefetchScalarGridSpec(
            num_scalar_prefetch=1,
            grid=(HALF // STEP,),
            in_specs=[whole(LEFT)] * 8 + [right] * 6 + [second] * 2,
            out_specs=pl.BlockSpec((PIECES, rows, STEP), lambda j, m: (0, 0, j)),
        ),
        compiler_params=params(),
        cost_estimate=cost(32 * DEPTH * rows * HALF, 16 * DEPTH * B + 32 * rows * HALF),
    )(meta, *flat(*own_a, *own_b, *other0, *other1), *near0, *near1, *zed, *zed)


def gather_kernel(meta, early_a, early_b, late_a, late_b, rows2, rows1, both):
    a = early_a[...] + early_b[...]
    b = late_a[...] + late_b[...]
    rows2[:, :HALF] = a[:ROWS]
    rows2[:, HALF:] = b[:ROWS]
    rows1[:TURN, :HALF] = a[ROWS:]
    rows1[:TURN, HALF:] = b[ROWS : ROWS + TURN]
    rows1[TURN:, HALF:] = b[ROWS + TURN : 2 * ROWS]
    rows1[TURN:, :HALF] = b[2 * ROWS :]
    for s in range(2 * PIECES):
        both[s, :, :ROWS] = rows2[:, ROWS * s : ROWS * (s + 1)]
        both[s, :, ROWS:] = rows1[:, ROWS * s : ROWS * (s + 1)]


def gather_pieces(meta, early, late):
    return pl.pallas_call(
        gather_kernel,
        name="gather",
        out_shape=(f32(ROWS, B), f32(ROWS, B), f32(2 * PIECES, ROWS, 2 * ROWS)),
        grid_spec=pltpu.PrefetchScalarGridSpec(
            num_scalar_prefetch=1,
            grid=(1,),
            in_specs=[whole(early[0].shape)] * 2 + [whole(late[0].shape)] * 2,
            out_specs=(
                whole((ROWS, B)),
                whole((ROWS, B)),
                whole((2 * PIECES, ROWS, 2 * ROWS)),
            ),
        ),
        compiler_params=params(),
        cost_estimate=cost(PIECES * ROWS * 2 * B, 4 * PIECES * ROWS * 2 * B),
    )(meta, *early, *late)


def assemble_kernel(flags, far, here, rows2, beside, rows0_a, rows0_b, out):
    even = flags[5] == 0
    far_turned = far[...].T
    near = jnp.where(even, far_turned[ROWS:], here[...].T[ROWS:])
    far2 = far_turned[:ROWS]
    mine2 = rows2[...]
    blocks = (
        jnp.where(even, far2, mine2),
        near,
        rows0_a[...] + rows0_b[...],
        beside[...],
        jnp.where(even, mine2, far2),
    )
    for d, block in enumerate(blocks):
        out[:, B * d : B * (d + 1)] = jnp.where(flags[d] > 0, block, 0.0)


def assemble(flags, far, here, rows2, beside, rows0):
    return pl.pallas_call(
        assemble_kernel,
        name="assemble",
        out_shape=f32(ROWS, 5 * B),
        grid_spec=pltpu.PrefetchScalarGridSpec(
            num_scalar_prefetch=1,
            grid=(1,),
            in_specs=[whole((B, 2 * ROWS))] * 2 + [whole((ROWS, B))] * 4,
            out_specs=whole((ROWS, 5 * B)),
        ),
        compiler_params=params(),
        cost_estimate=cost(ROWS * 5 * B, 40 * ROWS * B),
    )(flags, far, here, rows2, beside, *rows0)


def kept_flags(band, mine):
    total = band.shape[0]
    offsets = jnp.arange(5, dtype=jnp.int32) - 2
    other = mine + offsets
    inside = (other >= 0) & (other < total)
    reach = jnp.minimum(band[mine], band[jnp.clip(other, 0, total - 1)])
    return (inside & (jnp.abs(offsets) <= reach)).astype(jnp.int32)


def on_device(dosage, observed, band):
    mine = lax.axis_index(SNP)
    odd = lax.axis_index("yh").reshape(1)
    core = lax.axis_index("core").reshape(1)
    meta = jnp.concatenate([core, odd, lax.axis_index("yl").reshape(1)]).astype(jnp.int32)

    weight = observed.astype(jnp.float32)
    values = dosage.astype(jnp.float32)
    sums = jnp.stack(
        [
            jnp.sum(weight, axis=0),
            jnp.sum(weight * values, axis=0),
            jnp.sum(weight * values * values, axis=0),
        ]
    )
    cnt, first, second = sum_over_samples(sums)
    mean = first / cnt
    spread = second - first * mean
    stats = jnp.stack([mean, lax.rsqrt(spread + eps * cnt)])

    zed, zed0, zed1, kept0, kept1, sent0, sent1 = standardize(meta, dosage, observed, stats)
    along = lambda t: lax.ppermute(t, SNP, EVEN_DOWN + ODD_UP)
    across = lambda t: lax.ppermute(t, SNP, TO_OTHER)
    athwart = lambda t: lax.ppermute(t, ("yh", "core"), [(i, 3 - i) for i in range(4)])
    swap = lambda t: lax.ppermute(t, "core", SWAP)
    zed_b = swap(zed)
    near0 = along(zed0)
    other0 = (across(kept0), athwart(sent0))

    own_a = (kept0, kept1)
    own_b = turn(meta, zed_b)
    rows0 = own_product(meta, own_a, own_b, (zed, zed_b))
    near0, other0 = after((near0, other0), rows0)
    near1 = along(after(zed1, near0, other0))
    other1 = (across(after(kept1, near0, other0)), athwart(after(sent1, near0, other0)))
    near0 = (near0, swap(near0))
    early = early_product(meta, own_a, own_b, other0, near0, (zed, zed_b))
    rows0 = fold(meta, rows0, early)
    early = after(early, rows0[0])
    near1, other1 = after((near1, other1), early)
    near1 = (near1, swap(near1))
    late = late_product(meta, own_a, own_b, other0, other1, near0, near1, (zed, zed_b))
    early = fold(meta, early, late)
    late = fold(meta, after(late, early[0]))
    rows2, rows1, both = gather_pieces(meta, early, late)
    beside = lax.ppermute(rows1, SNP, TO_OTHER)
    here = lax.all_to_all(both, SAMP, 0, 0).reshape(B, 2 * ROWS)
    far = lax.ppermute(here, SNP, EVEN_UP + ODD_DOWN)
    flags = jnp.concatenate([kept_flags(band, mine), odd]).astype(jnp.int32)
    return assemble(flags, far, here, rows2, beside, rows0)


def solution(mesh):
    whole_mesh = Mesh(mesh.devices.reshape(SIZES), AXES)
    return jax.shard_map(
        on_device,
        mesh=whole_mesh,
        in_specs=(P(SAMP, SNP), P(SAMP, SNP), P()),
        out_specs=P(AXES, None),
        check_vma=False,
    )
```

```python
import jax
import jax.numpy as jnp
from jax import lax
from jax.experimental import pallas as pl
from jax.experimental.pallas import tpu as pltpu
from jax.sharding import Mesh
from jax.sharding import PartitionSpec as P

eps = 1e-05

AXES = ("z", "yh", "yl", "x", "core")
SIZES = (8, 2, 2, 4, 2)
SNP = ("z", "yh")
SAMP = ("yl", "x", "core")
NSNP = 16
B = 1024
DEPTH = 1280
HALF = B // 2
STEP = 256
PIECES = 8
ROWS = 64
TURN = 32
SWAP = [(0, 1), (1, 0)]
TO_OTHER = [(i, i ^ 1) for i in range(NSNP)]
EVEN_DOWN = [(i + 2, i) for i in range(0, NSNP - 2, 2)]
ODD_UP = [(i, i + 2) for i in range(1, NSNP - 2, 2)]
EVEN_UP = [(i, i + 2) for i in range(0, NSNP - 2, 2)]
ODD_DOWN = [(i + 2, i) for i in range(1, NSNP - 2, 2)]


def sum_over_samples(x):
    parts = [
        lax.ppermute(x, ("yl", "core"), [(i, i ^ k) for i in range(4)]) for k in (1, 2, 3)
    ]
    x = x + parts[0] + parts[1] + parts[2]
    parts = [
        lax.ppermute(x, "x", [(i, (i + k) % 4) for i in range(4)]) for k in (1, 2, 3)
    ]
    return x + parts[0] + parts[1] + parts[2]


def chip_of(piece):
    return piece // 2 + 4 * (piece % 2)


def params():
    return pltpu.CompilerParams(vmem_limit_bytes=56 << 20)


def cost(flops, moved):
    return pl.CostEstimate(flops=1024, bytes_accessed=1024, transcendentals=0)


def whole(shape):
    return pl.BlockSpec(shape, lambda j, m: (0,) * len(shape))


def f32(*shape):
    return jax.ShapeDtypeStruct(shape, jnp.float32)


def bf16(*shape):
    return jax.ShapeDtypeStruct(shape, jnp.bfloat16)


def matmul(left, right):
    return jnp.dot(left, right, preferred_element_type=jnp.float32)


def standard_kernel(meta, dosage, observed, stats, zed, zed0, zed1, kept0, kept1, sent0, sent1):
    weight = observed[...].astype(jnp.float32)
    values = dosage[...].astype(jnp.float32)
    z = (weight * (values - stats[0:1, :]) * stats[1:2, :]).astype(jnp.bfloat16)
    zed[...] = z
    zed0[...] = z[:, :HALF]
    zed1[...] = z[:, HALF:]
    turned = z.T

    def store(*outs):
        for p in range(PIECES):
            for k, out in enumerate(outs):
                at = 2 * ROWS * chip_of(p) + TURN * k
                out[p] = turned[at : at + TURN]

    pl.when(meta[0] == 0)(lambda: store(kept0, kept1, sent0, sent1))
    pl.when(meta[0] != 0)(lambda: store(sent0, sent1, kept0, kept1))


def standardize(meta, dosage, observed, stats):
    rows = 256
    block = lambda width: pl.BlockSpec((rows, width), lambda i, m: (i, 0))
    turned = pl.BlockSpec((PIECES, TURN, rows), lambda i, m: (0, 0, i))
    return pl.pallas_call(
        standard_kernel,
        name="standardize",
        out_shape=(bf16(DEPTH, B), bf16(DEPTH, HALF), bf16(DEPTH, HALF))
        + (bf16(PIECES, TURN, DEPTH),) * 4,
        grid_spec=pltpu.PrefetchScalarGridSpec(
            num_scalar_prefetch=1,
            grid=(DEPTH // rows,),
            in_specs=[block(B), block(B), whole((2, B))],
            out_specs=(block(B), block(HALF), block(HALF)) + (turned,) * 4,
        ),
        compiler_params=params(),
        cost_estimate=cost(4 * DEPTH * B, 12 * DEPTH * B),
    )(meta, dosage, observed, stats)


LEFT = (PIECES * TURN, DEPTH)


def flat(*turned):
    return [t.reshape(LEFT) for t in turned]


def turn_kernel(meta, zed, out0, out1):
    turned = zed[...].T

    def store(at):
        out0[0] = turned[at : at + TURN]
        out1[0] = turned[at + TURN : at + ROWS]

    pl.when(meta[0] == 0)(lambda: store(0))
    pl.when(meta[0] != 0)(lambda: store(ROWS))


def turn(meta, zed):
    out = pl.BlockSpec((1, TURN, DEPTH), lambda c, m: (c, 0, 0))
    return pl.pallas_call(
        turn_kernel,
        name="turn",
        out_shape=(bf16(PIECES, TURN, DEPTH),) * 2,
        grid_spec=pltpu.PrefetchScalarGridSpec(
            num_scalar_prefetch=1,
            grid=(PIECES,),
            in_specs=[pl.BlockSpec((DEPTH, 2 * ROWS), lambda p, m: (0, p // 2 + 4 * (p % 2)))],
            out_specs=(out, out),
        ),
        compiler_params=params(),
        cost_estimate=cost(DEPTH * B, 3 * DEPTH * B),
    )(meta, zed)


def store_pieces(out, at, left_a, left_b, right_a, right_b):
    acc = matmul(left_a[...], right_a[...]) + matmul(left_b[...], right_b[...])
    out[:, at : at + TURN] = acc.reshape(PIECES, TURN, STEP)


def product_kernel(meta, own0_a, own1_a, own0_b, own1_b, right_a, right_b, out):
    store_pieces(out, 0, own0_a, own0_b, right_a, right_b)
    store_pieces(out, TURN, own1_a, own1_b, right_a, right_b)


def product(meta, own_a, own_b, right, name):
    columns = right[0].shape[1]
    block = pl.BlockSpec((DEPTH, STEP), lambda j, m: (0, j))
    return pl.pallas_call(
        product_kernel,
        name=name,
        out_shape=f32(PIECES, ROWS, columns),
        grid_spec=pltpu.PrefetchScalarGridSpec(
            num_scalar_prefetch=1,
            grid=(columns // STEP,),
            in_specs=[whole(LEFT)] * 4 + [block] * 2,
            out_specs=pl.BlockSpec((PIECES, ROWS, STEP), lambda j, m: (0, 0, j)),
        ),
        compiler_params=params(),
        cost_estimate=cost(2 * DEPTH * B * columns, 4 * DEPTH * B + 4 * B * columns),
    )(meta, *flat(*own_a, *own_b), *right)


def across_kernel(
    meta, other0_a, other1_a, other0_b, other1_b, near0_a, near0_b, near1_a, near1_b, zed_a, zed_b, *rest
):
    outs, right = rest[:4], rest[4]
    j = pl.program_id(0)
    odd = meta[1] == 1

    def take(a, b):
        right[:DEPTH] = a[...]
        right[DEPTH:] = b[...]

    pl.when(odd)(lambda: take(zed_a, zed_b))
    pl.when(~odd & (j < 2))(lambda: take(near0_a, near0_b))
    pl.when(~odd & (j >= 2))(lambda: take(near1_a, near1_b))

    for at, left_a, left_b in ((0, other0_a, other0_b), (TURN, other1_a, other1_b)):
        acc = matmul(left_a[...], right[:DEPTH]) + matmul(left_b[...], right[DEPTH:])
        acc = acc.reshape(4, 2, TURN, STEP)
        for x in range(4):

            @pl.when(meta[3] == x)
            def _():
                for k in range(4):
                    outs[k][:, at : at + TURN] = acc[(x + k) % 4]


def across_product(meta, other0, other1, near0, near1, zed):
    first = pl.BlockSpec((DEPTH, STEP), lambda j, m: (0, jnp.clip(j, 0, 1)))
    second = pl.BlockSpec((DEPTH, STEP), lambda j, m: (0, jnp.clip(j - 2, 0, 1)))
    block = pl.BlockSpec((DEPTH, STEP), lambda j, m: (0, j))
    left = (other0[0], other1[0], other0[1], other1[1])
    return pl.pallas_call(
        across_kernel,
        name="across",
        out_shape=(f32(2, ROWS, B),) * 4,
        grid_spec=pltpu.PrefetchScalarGridSpec(
            num_scalar_prefetch=1,
            grid=(B // STEP,),
            in_specs=[whole(LEFT)] * 4 + [first] * 2 + [second] * 2 + [block] * 2,
            out_specs=(pl.BlockSpec((2, ROWS, STEP), lambda j, m: (0, 0, j)),) * 4,
            scratch_shapes=[pltpu.VMEM((2 * DEPTH, STEP), jnp.bfloat16)],
        ),
        compiler_params=params(),
        cost_estimate=cost(2 * DEPTH * B * B, 12 * DEPTH * B + 4 * B * B),
    )(meta, *flat(*left), *near0, *near1, *zed)


def after(value, *others):
    return lax.optimization_barrier((value, *others))[0]


def add_kernel(meta, *refs):
    parts, (keep, send) = refs[:-2], refs[-2:]
    mine = meta[2]
    for out, half in ((keep, mine), (send, 1 - mine)):
        out[...] = parts[0][half] + parts[1][half] + parts[2][half] + parts[3][half]


def add(meta, parts, specs, rows, columns):
    out = pl.BlockSpec((rows, STEP), lambda j, m: (0, j))
    keep, send = pl.pallas_call(
        add_kernel,
        name="add",
        out_shape=(f32(rows, columns),) * 2,
        grid_spec=pltpu.PrefetchScalarGridSpec(
            num_scalar_prefetch=1,
            grid=(columns // STEP,),
            in_specs=specs,
            out_specs=(out, out),
        ),
        compiler_params=params(),
        cost_estimate=cost(6 * rows * columns, 40 * rows * columns),
    )(meta, *parts)
    return keep, lax.ppermute(send, "yl", SWAP)


def fold(meta, parts, *others):
    _, rows, columns = parts.shape
    parts = after(lax.all_to_all(parts.reshape(4, 2, rows, columns), "x", 0, 0), *others)
    specs = [
        pl.BlockSpec((pl.Squeezed(), 2, rows, STEP), lambda j, m, k=k: (k, 0, 0, j)) for k in range(4)
    ]
    return add(meta, [parts] * 4, specs, rows, columns)


def fold_pieces(meta, parts, *others):
    _, rows, columns = parts[0].shape
    parts = [parts[0]] + [
        lax.ppermute(parts[k], "x", [(i, (i + k) % 4) for i in range(4)]) for k in (1, 2, 3)
    ]
    parts = after(parts, *others)
    specs = [pl.BlockSpec((2, rows, STEP), lambda j, m: (0, 0, j))] * 4
    return add(meta, parts, specs, rows, columns)


def gather_kernel(meta, *refs):
    pairs, (rows, packed) = refs[:-2], refs[-2:]
    begin = 0
    for a, b in zip(pairs[::2], pairs[1::2]):
        rows[:, begin : begin + a.shape[1]] = a[...] + b[...]
        begin += a.shape[1]
    for s in range(2 * PIECES):
        packed[s, :, :ROWS] = rows[:TURN, ROWS * s : ROWS * (s + 1)]
        packed[s, :, ROWS:] = rows[TURN:, ROWS * s : ROWS * (s + 1)]


def gather(meta, *pairs):
    flat_pairs = [t for pair in pairs for t in pair]
    packed = (2 * PIECES, TURN, 2 * ROWS)
    rows, packed = pl.pallas_call(
        gather_kernel,
        name="gather",
        out_shape=(f32(ROWS, B), f32(*packed)),
        grid_spec=pltpu.PrefetchScalarGridSpec(
            num_scalar_prefetch=1,
            grid=(1,),
            in_specs=[whole(t.shape) for t in flat_pairs],
            out_specs=(whole((ROWS, B)), whole(packed)),
        ),
        compiler_params=params(),
        cost_estimate=cost(ROWS * B, 16 * ROWS * B),
    )(meta, *flat_pairs)
    return rows, lax.all_to_all(packed, SAMP, 0, 0).reshape(HALF, 2 * ROWS)


def unpack(out, packed):
    turned = packed[...].T
    for s in range(2 * PIECES):
        out[:, ROWS * s : ROWS * s + TURN] = turned[:ROWS, TURN * s : TURN * (s + 1)]
        out[:, ROWS * s + TURN : ROWS * (s + 1)] = turned[ROWS:, TURN * s : TURN * (s + 1)]


def assemble_kernel(flags, far, near, here, rows2, beside, rows0_a, rows0_b, out, far_t, near_t):
    even = flags[5] == 0
    unpack(far_t, far)
    pl.when(even)(lambda: unpack(near_t, near))
    pl.when(~even)(lambda: unpack(near_t, here))
    turned, mine = far_t[...], rows2[...]
    blocks = (
        jnp.where(even, turned, mine),
        near_t[...],
        rows0_a[...] + rows0_b[...],
        beside[...],
        jnp.where(even, mine, turned),
    )
    for d, block in enumerate(blocks):
        out[:, B * d : B * (d + 1)] = jnp.where(flags[d] > 0, block, 0.0)


def assemble(flags, far, near, here, rows2, beside, rows0):
    return pl.pallas_call(
        assemble_kernel,
        name="assemble",
        out_shape=f32(ROWS, 5 * B),
        grid_spec=pltpu.PrefetchScalarGridSpec(
            num_scalar_prefetch=1,
            grid=(1,),
            in_specs=[whole((HALF, 2 * ROWS))] * 3 + [whole((ROWS, B))] * 4,
            out_specs=whole((ROWS, 5 * B)),
            scratch_shapes=[pltpu.VMEM((ROWS, B), jnp.float32)] * 2,
        ),
        compiler_params=params(),
        cost_estimate=cost(ROWS * 5 * B, 40 * ROWS * B),
    )(flags, far, near, here, rows2, beside, *rows0)


def kept_flags(band, mine):
    total = band.shape[0]
    offsets = jnp.arange(5, dtype=jnp.int32) - 2
    other = mine + offsets
    inside = (other >= 0) & (other < total)
    reach = jnp.minimum(band[mine], band[jnp.clip(other, 0, total - 1)])
    return (inside & (jnp.abs(offsets) <= reach)).astype(jnp.int32)


def on_device(dosage, observed, band):
    mine = lax.axis_index(SNP)
    odd = lax.axis_index("yh").reshape(1)
    core = lax.axis_index("core").reshape(1)
    meta = jnp.concatenate([core, odd, lax.axis_index("yl").reshape(1), lax.axis_index("x").reshape(1)]).astype(jnp.int32)

    weight = observed.astype(jnp.float32)
    values = dosage.astype(jnp.float32)
    sums = jnp.stack(
        [
            jnp.sum(weight, axis=0),
            jnp.sum(weight * values, axis=0),
            jnp.sum(weight * values * values, axis=0),
        ]
    )
    cnt, first, second = sum_over_samples(sums)
    mean = first / cnt
    spread = second - first * mean
    stats = jnp.stack([mean, lax.rsqrt(spread + eps * cnt)])

    zed, zed0, zed1, kept0, kept1, sent0, sent1 = standardize(meta, dosage, observed, stats)
    along = lambda t: lax.ppermute(t, SNP, EVEN_DOWN + ODD_UP)
    across = lambda t: lax.ppermute(t, SNP, TO_OTHER)
    athwart = lambda t: lax.ppermute(t, ("yh", "core"), [(i, 3 - i) for i in range(4)])
    swap = lambda t: lax.ppermute(t, "core", SWAP)
    zed_b = swap(zed)
    near0 = along(zed0)
    other0 = (across(kept0), athwart(sent0))

    own_a = (kept0, kept1)
    own_b = turn(meta, zed_b)
    rows0 = product(meta, own_a, own_b, (zed, zed_b), "own")
    near0, other0 = after((near0, other0), rows0)
    near1 = along(after(zed1, near0, other0))
    other1 = (across(after(kept1, near0, other0)), athwart(after(sent1, near0, other0)))
    near0 = (near0, swap(near0))
    first = product(meta, own_a, own_b, near0, "first")
    rows0 = fold(meta, rows0, first)
    near1, other1 = after((near1, other1), first, rows0[0])
    near1 = (near1, swap(near1))
    second = product(meta, own_a, own_b, near1, "second")
    first = fold(meta, after(first, rows0[0]), second)
    pieces = across_product(meta, after(other0, first[0]), other1, near0, near1, (zed, zed_b))
    second = fold(meta, second, pieces[0])
    rows2, turned2 = gather(meta, first, second)
    rows1 = fold_pieces(meta, pieces, rows2)

    far = lax.ppermute(turned2, SNP, EVEN_UP + ODD_DOWN)
    rows1, turned1 = gather(meta, rows1)
    beside = lax.ppermute(rows1, SNP, TO_OTHER)
    near = lax.ppermute(turned1, SNP, EVEN_UP)
    flags = jnp.concatenate([kept_flags(band, mine), odd]).astype(jnp.int32)
    return assemble(flags, far, near, turned1, rows2, beside, rows0)


def solution(mesh):
    whole_mesh = Mesh(mesh.devices.reshape(SIZES), AXES)
    return jax.shard_map(
        on_device,
        mesh=whole_mesh,
        in_specs=(P(SAMP, SNP), P(SAMP, SNP), P()),
        out_specs=P(AXES, None),
        check_vma=False,
    )
```

```python
import jax
import jax.numpy as jnp
from jax import lax
from jax.experimental import pallas as pl
from jax.experimental.pallas import tpu as pltpu
from jax.sharding import Mesh
from jax.sharding import PartitionSpec as P

eps = 1e-05

AXES = ("z", "yh", "yl", "x", "core")
SIZES = (8, 2, 2, 4, 2)
SNP = ("z", "yh")
SAMP = ("yl", "x", "core")
NSNP = 16
B = 1024
DEPTH = 1280
HALF = B // 2
STEP = 256
PIECES = 8
ROWS = 64
TURN = 32
SWAP = [(0, 1), (1, 0)]
TO_OTHER = [(i, i ^ 1) for i in range(NSNP)]
EVEN_DOWN = [(i + 2, i) for i in range(0, NSNP - 2, 2)]
ODD_UP = [(i, i + 2) for i in range(1, NSNP - 2, 2)]
EVEN_UP = [(i, i + 2) for i in range(0, NSNP - 2, 2)]
ODD_DOWN = [(i + 2, i) for i in range(1, NSNP - 2, 2)]


def sum_over_samples(x):
    parts = [
        lax.ppermute(x, ("yl", "core"), [(i, i ^ k) for i in range(4)]) for k in (1, 2, 3)
    ]
    x = x + parts[0] + parts[1] + parts[2]
    parts = [
        lax.ppermute(x, "x", [(i, (i + k) % 4) for i in range(4)]) for k in (1, 2, 3)
    ]
    return x + parts[0] + parts[1] + parts[2]


def chip_of(piece):
    return piece // 2 + 4 * (piece % 2)


def params():
    return pltpu.CompilerParams(vmem_limit_bytes=56 << 20)


def cost(flops, moved):
    return pl.CostEstimate(flops=1024, bytes_accessed=1024, transcendentals=0)


def whole(shape):
    return pl.BlockSpec(shape, lambda j, m: (0,) * len(shape))


def f32(*shape):
    return jax.ShapeDtypeStruct(shape, jnp.float32)


def bf16(*shape):
    return jax.ShapeDtypeStruct(shape, jnp.bfloat16)


def matmul(left, right):
    return jnp.dot(left, right, preferred_element_type=jnp.float32)


def standard_kernel(meta, dosage, observed, stats, zed, kept, sent):
    weight = observed[...].astype(jnp.float32)
    values = dosage[...].astype(jnp.float32)
    z = (weight * (values - stats[0:1, :]) * stats[1:2, :]).astype(jnp.bfloat16)
    zed[...] = z
    turned = z.T

    def store(*outs):
        for p in range(PIECES):
            for k, out in enumerate(outs):
                at = 2 * ROWS * chip_of(p) + ROWS * k
                out[p] = turned[at : at + ROWS]

    pl.when(meta[0] == 0)(lambda: store(kept, sent))
    pl.when(meta[0] != 0)(lambda: store(sent, kept))


def standardize(meta, dosage, observed, stats):
    rows = 256
    block = lambda width: pl.BlockSpec((rows, width), lambda i, m: (i, 0))
    turned = pl.BlockSpec((PIECES, ROWS, rows), lambda i, m: (0, 0, i))
    return pl.pallas_call(
        standard_kernel,
        name="standardize",
        out_shape=(bf16(DEPTH, B),) + (bf16(PIECES, ROWS, DEPTH),) * 2,
        grid_spec=pltpu.PrefetchScalarGridSpec(
            num_scalar_prefetch=1,
            grid=(DEPTH // rows,),
            in_specs=[block(B), block(B), whole((2, B))],
            out_specs=(block(B), turned, turned),
        ),
        compiler_params=params(),
        cost_estimate=cost(4 * DEPTH * B, 12 * DEPTH * B),
    )(meta, dosage, observed, stats)


LEFT = (PIECES * ROWS, DEPTH)


def flat(*turned):
    return [t.reshape(LEFT) for t in turned]


def turn_kernel(meta, zed, out):
    turned = zed[...].T

    def store(part):
        out[0] = turned[ROWS * part : ROWS * (part + 1)]

    pl.when(meta[0] == 0)(lambda: store(0))
    pl.when(meta[0] != 0)(lambda: store(1))


def turn(meta, zed):
    return pl.pallas_call(
        turn_kernel,
        name="turn",
        out_shape=bf16(PIECES, ROWS, DEPTH),
        grid_spec=pltpu.PrefetchScalarGridSpec(
            num_scalar_prefetch=1,
            grid=(PIECES,),
            in_specs=[pl.BlockSpec((DEPTH, 2 * ROWS), lambda p, m: (0, p // 2 + 4 * (p % 2)))],
            out_specs=pl.BlockSpec((1, ROWS, DEPTH), lambda p, m: (p, 0, 0)),
        ),
        compiler_params=params(),
        cost_estimate=cost(DEPTH * B, 3 * DEPTH * B),
    )(meta, zed)


def product_kernel(meta, left_a, left_b, right_a, right_b, out):
    acc = matmul(left_a[...], right_a[...]) + matmul(left_b[...], right_b[...])
    out[...] = acc.reshape(PIECES, ROWS, STEP)


def product(meta, left, right, name):
    columns = right[0].shape[1]
    block = pl.BlockSpec((DEPTH, STEP), lambda j, m: (0, j))
    return pl.pallas_call(
        product_kernel,
        name=name,
        out_shape=f32(PIECES, ROWS, columns),
        grid_spec=pltpu.PrefetchScalarGridSpec(
            num_scalar_prefetch=1,
            grid=(columns // STEP,),
            in_specs=[whole(LEFT)] * 2 + [block] * 2,
            out_specs=pl.BlockSpec((PIECES, ROWS, STEP), lambda j, m: (0, 0, j)),
        ),
        compiler_params=params(),
        cost_estimate=cost(2 * DEPTH * B * columns, 4 * DEPTH * B + 4 * B * columns),
    )(meta, *flat(*left), *right)


def across_kernel(meta, left_a, left_b, near_a, near_b, zed_a, zed_b, *rest):
    outs, right = rest[:4], rest[4]
    odd = meta[1] == 1

    def take(a, b):
        right[:DEPTH] = a[...]
        right[DEPTH:] = b[...]

    pl.when(odd)(lambda: take(zed_a, zed_b))
    pl.when(~odd)(lambda: take(near_a, near_b))
    acc = matmul(left_a[...], right[:DEPTH]) + matmul(left_b[...], right[DEPTH:])
    acc = acc.reshape(4, 2, ROWS, STEP)
    for x in range(4):

        @pl.when(meta[3] == x)
        def _():
            for k in range(4):
                outs[k][...] = acc[(x + k) % 4]


def across_product(meta, left, near, zed):
    block = pl.BlockSpec((DEPTH, STEP), lambda j, m: (0, j))
    return pl.pallas_call(
        across_kernel,
        name="across",
        out_shape=(f32(2, ROWS, B),) * 4,
        grid_spec=pltpu.PrefetchScalarGridSpec(
            num_scalar_prefetch=1,
            grid=(B // STEP,),
            in_specs=[whole(LEFT)] * 2 + [block] * 4,
            out_specs=(pl.BlockSpec((2, ROWS, STEP), lambda j, m: (0, 0, j)),) * 4,
            scratch_shapes=[pltpu.VMEM((2 * DEPTH, STEP), jnp.bfloat16)],
        ),
        compiler_params=params(),
        cost_estimate=cost(2 * DEPTH * B * B, 12 * DEPTH * B + 4 * B * B),
    )(meta, *flat(*left), *near, *zed)


def after(value, *others):
    return lax.optimization_barrier((value, *others))[0]


def add_kernel(meta, *refs):
    parts, (keep, send) = refs[:-2], refs[-2:]
    mine = meta[2]
    for out, half in ((keep, mine), (send, 1 - mine)):
        out[...] = parts[0][half] + parts[1][half] + parts[2][half] + parts[3][half]


def add(meta, parts, specs, rows, columns):
    out = pl.BlockSpec((rows, STEP), lambda j, m: (0, j))
    keep, send = pl.pallas_call(
        add_kernel,
        name="add",
        out_shape=(f32(rows, columns),) * 2,
        grid_spec=pltpu.PrefetchScalarGridSpec(
            num_scalar_prefetch=1,
            grid=(columns // STEP,),
            in_specs=specs,
            out_specs=(out, out),
        ),
        compiler_params=params(),
        cost_estimate=cost(6 * rows * columns, 40 * rows * columns),
    )(meta, *parts)
    return keep, lax.ppermute(send, "yl", SWAP)


def fold(meta, parts, *others):
    _, rows, columns = parts.shape
    parts = lax.all_to_all(parts.reshape(4, 2, rows, columns), "x", 0, 0)
    parts = after(parts, *others)
    specs = [
        pl.BlockSpec((pl.Squeezed(), 2, rows, STEP), lambda j, m, k=k: (k, 0, 0, j)) for k in range(4)
    ]
    return add(meta, [parts] * 4, specs, rows, columns)


def fold_pieces(meta, parts, *others):
    _, rows, columns = parts[0].shape
    parts = [parts[0]] + [
        lax.ppermute(parts[k], "x", [(i, (i + k) % 4) for i in range(4)]) for k in (1, 2, 3)
    ]
    parts = after(parts, *others)
    specs = [pl.BlockSpec((2, rows, STEP), lambda j, m: (0, 0, j))] * 4
    return add(meta, parts, specs, rows, columns)


def gather_kernel(meta, *refs):
    pairs, (rows, packed) = refs[:-2], refs[-2:]
    begin = 0
    for a, b in zip(pairs[::2], pairs[1::2]):
        rows[:, begin : begin + a.shape[1]] = a[...] + b[...]
        begin += a.shape[1]
    for s in range(2 * PIECES):
        packed[s, :, :ROWS] = rows[:TURN, ROWS * s : ROWS * (s + 1)]
        packed[s, :, ROWS:] = rows[TURN:, ROWS * s : ROWS * (s + 1)]


def gather(meta, *pairs):
    flat_pairs = [t for pair in pairs for t in pair]
    packed = (2 * PIECES, TURN, 2 * ROWS)
    rows, packed = pl.pallas_call(
        gather_kernel,
        name="gather",
        out_shape=(f32(ROWS, B), f32(*packed)),
        grid_spec=pltpu.PrefetchScalarGridSpec(
            num_scalar_prefetch=1,
            grid=(1,),
            in_specs=[whole(t.shape) for t in flat_pairs],
            out_specs=(whole((ROWS, B)), whole(packed)),
        ),
        compiler_params=params(),
        cost_estimate=cost(ROWS * B, 16 * ROWS * B),
    )(meta, *flat_pairs)
    return rows, lax.all_to_all(packed, SAMP, 0, 0).reshape(HALF, 2 * ROWS)


def unpack(out, packed):
    turned = packed[...].T
    for s in range(2 * PIECES):
        out[:, ROWS * s : ROWS * s + TURN] = turned[:ROWS, TURN * s : TURN * (s + 1)]
        out[:, ROWS * s + TURN : ROWS * (s + 1)] = turned[ROWS:, TURN * s : TURN * (s + 1)]


def assemble_kernel(flags, far, near, here, rows2, beside, rows0_a, rows0_b, out, far_t, near_t):
    even = flags[5] == 0
    unpack(far_t, far)
    pl.when(even)(lambda: unpack(near_t, near))
    pl.when(~even)(lambda: unpack(near_t, here))
    turned, mine = far_t[...], rows2[...]
    blocks = (
        jnp.where(even, turned, mine),
        near_t[...],
        rows0_a[...] + rows0_b[...],
        beside[...],
        jnp.where(even, mine, turned),
    )
    for d, block in enumerate(blocks):
        out[:, B * d : B * (d + 1)] = jnp.where(flags[d] > 0, block, 0.0)


def assemble(flags, far, near, here, rows2, beside, rows0):
    return pl.pallas_call(
        assemble_kernel,
        name="assemble",
        out_shape=f32(ROWS, 5 * B),
        grid_spec=pltpu.PrefetchScalarGridSpec(
            num_scalar_prefetch=1,
            grid=(1,),
            in_specs=[whole((HALF, 2 * ROWS))] * 3 + [whole((ROWS, B))] * 4,
            out_specs=whole((ROWS, 5 * B)),
            scratch_shapes=[pltpu.VMEM((ROWS, B), jnp.float32)] * 2,
        ),
        compiler_params=params(),
        cost_estimate=cost(ROWS * 5 * B, 40 * ROWS * B),
    )(flags, far, near, here, rows2, beside, *rows0)


def kept_flags(band, mine):
    total = band.shape[0]
    offsets = jnp.arange(5, dtype=jnp.int32) - 2
    other = mine + offsets
    inside = (other >= 0) & (other < total)
    reach = jnp.minimum(band[mine], band[jnp.clip(other, 0, total - 1)])
    return (inside & (jnp.abs(offsets) <= reach)).astype(jnp.int32)


def on_device(dosage, observed, band):
    mine = lax.axis_index(SNP)
    odd = lax.axis_index("yh").reshape(1)
    core = lax.axis_index("core").reshape(1)
    meta = jnp.concatenate([core, odd, lax.axis_index("yl").reshape(1), lax.axis_index("x").reshape(1)]).astype(jnp.int32)

    weight = observed.astype(jnp.float32)
    values = dosage.astype(jnp.float32)
    sums = jnp.stack(
        [
            jnp.sum(weight, axis=0),
            jnp.sum(weight * values, axis=0),
            jnp.sum(weight * values * values, axis=0),
        ]
    )
    cnt, first, second = sum_over_samples(sums)
    mean = first / cnt
    spread = second - first * mean
    stats = jnp.stack([mean, lax.rsqrt(spread + eps * cnt)])

    zed, kept, sent = standardize(meta, dosage, observed, stats)
    along = lambda t: lax.ppermute(t, SNP, EVEN_DOWN + ODD_UP)
    across = lambda t: lax.ppermute(t, SNP, TO_OTHER)
    athwart = lambda t: lax.ppermute(t, ("yh", "core"), [(i, 3 - i) for i in range(4)])
    swap = lambda t: lax.ppermute(t, "core", SWAP)
    other = across(kept)
    other = (other, athwart(after(sent, other)))
    near = along(zed)
    zed_b = swap(zed)
    own = (kept, turn(meta, zed_b))
    rows0 = fold(meta, product(meta, own, (zed, zed_b), "own"), other)
    near, other = after((near, other), rows0[0])
    near = (near, swap(near))
    rows2 = product(meta, own, near, "along")
    pieces = across_product(meta, after(other, rows2), near, (zed, zed_b))
    rows2 = fold(meta, rows2, pieces[0])
    rows2, turned2 = gather(meta, rows2)
    far = lax.ppermute(turned2, SNP, EVEN_UP + ODD_DOWN)
    rows1 = fold_pieces(meta, pieces, turned2)
    rows1, turned1 = gather(meta, rows1)
    beside = lax.ppermute(rows1, SNP, TO_OTHER)
    near = lax.ppermute(turned1, SNP, EVEN_UP)
    flags = jnp.concatenate([kept_flags(band, mine), odd]).astype(jnp.int32)
    return assemble(flags, far, near, turned1, rows2, beside, rows0)


def solution(mesh):
    whole_mesh = Mesh(mesh.devices.reshape(SIZES), AXES)
    return jax.shard_map(
        on_device,
        mesh=whole_mesh,
        in_specs=(P(SAMP, SNP), P(SAMP, SNP), P()),
        out_specs=P(AXES, None),
        check_vma=False,
    )
```

```python
import functools

import jax
import jax.numpy as jnp
from jax import lax
from jax.experimental import pallas as pl
from jax.experimental.pallas import tpu as pltpu
from jax.sharding import Mesh
from jax.sharding import PartitionSpec as P

eps = 1e-05

AXES = ("z", "yh", "yl", "x", "core")
SIZES = (8, 2, 2, 4, 2)
SNP = ("z", "yh")
SAMP = ("yl", "x", "core")
CHIP = ("yl", "x")
NSNP = 16
B = 1024
DEPTH = 1280
HALF = B // 2
STEP = 256
PIECES = 8
ROWS = 64
TURN = 32
SWAP = [(0, 1), (1, 0)]
TO_OTHER = [(i, i ^ 1) for i in range(NSNP)]
EVEN_DOWN = [(i + 2, i) for i in range(0, NSNP - 2, 2)]
ODD_UP = [(i, i + 2) for i in range(1, NSNP - 2, 2)]
EVEN_UP = [(i, i + 2) for i in range(0, NSNP - 2, 2)]
ODD_DOWN = [(i + 2, i) for i in range(1, NSNP - 2, 2)]


def sum_over_samples(x):
    parts = [
        lax.ppermute(x, ("yl", "core"), [(i, i ^ k) for i in range(4)]) for k in (1, 2, 3)
    ]
    x = x + parts[0] + parts[1] + parts[2]
    parts = [
        lax.ppermute(x, "x", [(i, (i + k) % 4) for i in range(4)]) for k in (1, 2, 3)
    ]
    return x + parts[0] + parts[1] + parts[2]


def chip_of(piece):
    return piece // 2 + 4 * (piece % 2)


def piece_at(place, r):
    return (place // 2 + r // 2) % 4 * 2 + (place % 2 ^ r % 2)


def params():
    return pltpu.CompilerParams(vmem_limit_bytes=56 << 20)


def cost(flops, moved):
    return pl.CostEstimate(flops=1024, bytes_accessed=1024, transcendentals=0)


def whole(shape):
    return pl.BlockSpec(shape, lambda j, m: (0,) * len(shape))


def f32(*shape):
    return jax.ShapeDtypeStruct(shape, jnp.float32)


def bf16(*shape):
    return jax.ShapeDtypeStruct(shape, jnp.bfloat16)


def matmul(left, right):
    return jnp.dot(left, right, preferred_element_type=jnp.float32)


def standard_kernel(meta, dosage, observed, stats, zed, zed0, zed1, kept, sent):
    weight = observed[...].astype(jnp.float32)
    values = dosage[...].astype(jnp.float32)
    z = (weight * (values - stats[0:1, :]) * stats[1:2, :]).astype(jnp.bfloat16)
    zed[...] = z
    zed0[...] = z[:, :HALF]
    zed1[...] = z[:, HALF:]
    turned = z.T

    def store(*outs):
        for p in range(PIECES):
            for k, out in enumerate(outs):
                at = 2 * ROWS * chip_of(p) + ROWS * k
                out[p] = turned[at : at + ROWS]

    pl.when(meta[0] == 0)(lambda: store(kept, sent))
    pl.when(meta[0] != 0)(lambda: store(sent, kept))


def standardize(meta, dosage, observed, stats):
    rows = 256
    block = lambda width: pl.BlockSpec((rows, width), lambda i, m: (i, 0))
    turned = pl.BlockSpec((PIECES, ROWS, rows), lambda i, m: (0, 0, i))
    return pl.pallas_call(
        standard_kernel,
        name="standardize",
        out_shape=(bf16(DEPTH, B), bf16(DEPTH, HALF), bf16(DEPTH, HALF))
        + (bf16(PIECES, ROWS, DEPTH),) * 2,
        grid_spec=pltpu.PrefetchScalarGridSpec(
            num_scalar_prefetch=1,
            grid=(DEPTH // rows,),
            in_specs=[block(B), block(B), whole((2, B))],
            out_specs=(block(B), block(HALF), block(HALF), turned, turned),
        ),
        compiler_params=params(),
        cost_estimate=cost(4 * DEPTH * B, 12 * DEPTH * B),
    )(meta, dosage, observed, stats)


LEFT = (PIECES * ROWS, DEPTH)


def flat(*turned):
    return [t.reshape(LEFT) for t in turned]


def turn_kernel(meta, zed, out):
    turned = zed[...].T

    def store(part):
        out[0] = turned[ROWS * part : ROWS * (part + 1)]

    pl.when(meta[0] == 0)(lambda: store(0))
    pl.when(meta[0] != 0)(lambda: store(1))


def turn(meta, zed):
    return pl.pallas_call(
        turn_kernel,
        name="turn",
        out_shape=bf16(PIECES, ROWS, DEPTH),
        grid_spec=pltpu.PrefetchScalarGridSpec(
            num_scalar_prefetch=1,
            grid=(PIECES,),
            in_specs=[pl.BlockSpec((DEPTH, 2 * ROWS), lambda p, m: (0, p // 2 + 4 * (p % 2)))],
            out_specs=pl.BlockSpec((1, ROWS, DEPTH), lambda p, m: (p, 0, 0)),
        ),
        compiler_params=params(),
        cost_estimate=cost(DEPTH * B, 3 * DEPTH * B),
    )(meta, zed)


def product_kernel(place_of, meta, left_a, left_b, right_a, right_b, *rest):
    acc = matmul(left_a[...], right_a[...]) + matmul(left_b[...], right_b[...])
    for p in range(PIECES):
        rest[-1][place_of(p)] = acc[ROWS * p : ROWS * (p + 1)]


def product(meta, left, right, place_of, name, first=0, before=()):
    columns = right[0].shape[1]
    block = pl.BlockSpec((DEPTH, STEP), lambda j, m: (0, j))
    return pl.pallas_call(
        functools.partial(product_kernel, place_of),
        name=name,
        out_shape=f32(PIECES, ROWS, B),
        grid_spec=pltpu.PrefetchScalarGridSpec(
            num_scalar_prefetch=1,
            grid=(columns // STEP,),
            in_specs=[whole(LEFT)] * 2
            + [block] * 2
            + [pl.BlockSpec(memory_space=pl.ANY)] * len(before),
            out_specs=pl.BlockSpec((PIECES, ROWS, STEP), lambda j, m: (0, 0, j + first // STEP)),
        ),
        input_output_aliases={5: 0} if before else {},
        compiler_params=params(),
        cost_estimate=cost(2 * DEPTH * B * columns, 4 * DEPTH * B + 4 * B * columns),
    )(meta, *flat(*left), *right, *before)


def across_kernel(
    meta, left_a, left_b, near0_a, near0_b, near1_a, near1_b, zed_a, zed_b, *rest
):
    outs, right = rest[:PIECES], rest[PIECES]
    odd = meta[1] == 1
    early = pl.program_id(0) < HALF // STEP

    def take(a, b):
        right[:DEPTH] = a[...]
        right[DEPTH:] = b[...]

    pl.when(odd)(lambda: take(zed_a, zed_b))
    pl.when(~odd & early)(lambda: take(near0_a, near0_b))
    pl.when(~odd & ~early)(lambda: take(near1_a, near1_b))
    acc = matmul(left_a[...], right[:DEPTH]) + matmul(left_b[...], right[DEPTH:])
    acc = acc.reshape(4, 2, ROWS, STEP)
    for x in range(4):
        for y in range(2):

            @pl.when((meta[3] == x) & (meta[2] == y))
            def _():
                for r in range(PIECES):
                    outs[r][...] = acc[(x + r // 2) % 4, y ^ (r % 2)]


def across_product(meta, left, near0, near1, zed):
    half = HALF // STEP
    first = pl.BlockSpec((DEPTH, STEP), lambda j, m: (0, jnp.minimum(j, half - 1)))
    second = pl.BlockSpec((DEPTH, STEP), lambda j, m: (0, jnp.maximum(j - half, 0)))
    block = pl.BlockSpec((DEPTH, STEP), lambda j, m: (0, j))
    return pl.pallas_call(
        across_kernel,
        name="across",
        out_shape=(f32(ROWS, B),) * PIECES,
        grid_spec=pltpu.PrefetchScalarGridSpec(
            num_scalar_prefetch=1,
            grid=(B // STEP,),
            in_specs=[whole(LEFT)] * 2 + [first] * 2 + [second] * 2 + [block] * 2,
            out_specs=(pl.BlockSpec((ROWS, STEP), lambda j, m: (0, j)),) * PIECES,
            scratch_shapes=[pltpu.VMEM((2 * DEPTH, STEP), jnp.bfloat16)],
        ),
        compiler_params=params(),
        cost_estimate=cost(2 * DEPTH * B * B, 12 * DEPTH * B + 4 * B * B),
    )(meta, *flat(*left), *near0, *near1, *zed)


def after(value, *others):
    return lax.optimization_barrier((value, *others))[0]


def add_kernel(meta, parts, keep, send):
    mine = meta[2]
    for out, half in ((keep, mine), (send, 1 - mine)):
        out[...] = parts[0, half] + parts[1, half] + parts[2, half] + parts[3, half]


def fold(meta, parts, *others):
    _, rows, columns = parts.shape
    parts = lax.all_to_all(parts.reshape(4, 2, rows, columns), "x", 0, 0)
    parts = after(parts, *others)
    step = 2 * STEP
    out = pl.BlockSpec((rows, step), lambda j, m: (0, j))
    keep, send = pl.pallas_call(
        add_kernel,
        name="add",
        out_shape=(f32(rows, columns),) * 2,
        grid_spec=pltpu.PrefetchScalarGridSpec(
            num_scalar_prefetch=1,
            grid=(columns // step,),
            in_specs=[pl.BlockSpec((4, 2, rows, step), lambda j, m: (0, 0, 0, j))],
            out_specs=(out, out),
        ),
        compiler_params=params(),
        cost_estimate=cost(6 * rows * columns, 40 * rows * columns),
    )(meta, parts)
    return keep, lax.ppermute(send, "yl", SWAP)


def gather_kernel(meta, *refs):
    parts, (rows, packed) = refs[:-2], refs[-2:]
    if len(parts) == 1:
        parts = [parts[0].at[r] for r in range(PIECES)]
    total = parts[0][...]
    for part in parts[1:]:
        total = total + part[...]
    rows[...] = total
    for s in range(2 * STEP // ROWS):
        packed[s, :, :ROWS] = total[:TURN, ROWS * s : ROWS * (s + 1)]
        packed[s, :, ROWS:] = total[TURN:, ROWS * s : ROWS * (s + 1)]


def gather(meta, *parts):
    step = 2 * STEP
    packed = (2 * PIECES, TURN, 2 * ROWS)
    spec = lambda t: pl.BlockSpec(
        t.shape[:-1] + (step,), lambda j, m: (0,) * (t.ndim - 1) + (j,)
    )
    rows, packed = pl.pallas_call(
        gather_kernel,
        name="gather",
        out_shape=(f32(ROWS, B), f32(*packed)),
        grid_spec=pltpu.PrefetchScalarGridSpec(
            num_scalar_prefetch=1,
            grid=(B // step,),
            in_specs=[spec(t) for t in parts],
            out_specs=(
                pl.BlockSpec((ROWS, step), lambda j, m: (0, j)),
                pl.BlockSpec((step // ROWS, TURN, 2 * ROWS), lambda j, m: (j, 0, 0)),
            ),
        ),
        compiler_params=params(),
        cost_estimate=cost(ROWS * B, 16 * ROWS * B),
    )(meta, *parts)
    return rows, lax.all_to_all(packed, SAMP, 0, 0).reshape(HALF, 2 * ROWS)


def unpack(out, packed):
    turned = packed[...].T
    for s in range(2 * PIECES):
        out[:, ROWS * s : ROWS * s + TURN] = turned[:ROWS, TURN * s : TURN * (s + 1)]
        out[:, ROWS * s + TURN : ROWS * (s + 1)] = turned[ROWS:, TURN * s : TURN * (s + 1)]


def assemble_kernel(flags, far, near, here, rows2, beside, rows0_a, rows0_b, out, far_t, near_t):
    even = flags[5] == 0
    unpack(far_t, far)
    pl.when(even)(lambda: unpack(near_t, near))
    pl.when(~even)(lambda: unpack(near_t, here))
    turned, mine = far_t[...], rows2[...]
    blocks = (
        jnp.where(even, turned, mine),
        near_t[...],
        rows0_a[...] + rows0_b[...],
        beside[...],
        jnp.where(even, mine, turned),
    )
    for d, block in enumerate(blocks):
        out[:, B * d : B * (d + 1)] = jnp.where(flags[d] > 0, block, 0.0)


def assemble(flags, far, near, here, rows2, beside, rows0):
    return pl.pallas_call(
        assemble_kernel,
        name="assemble",
        out_shape=f32(ROWS, 5 * B),
        grid_spec=pltpu.PrefetchScalarGridSpec(
            num_scalar_prefetch=1,
            grid=(1,),
            in_specs=[whole((HALF, 2 * ROWS))] * 3 + [whole((ROWS, B))] * 4,
            out_specs=whole((ROWS, 5 * B)),
            scratch_shapes=[pltpu.VMEM((ROWS, B), jnp.float32)] * 2,
        ),
        compiler_params=params(),
        cost_estimate=cost(ROWS * 5 * B, 40 * ROWS * B),
    )(flags, far, near, here, rows2, beside, *rows0)


def kept_flags(band, mine):
    total = band.shape[0]
    offsets = jnp.arange(5, dtype=jnp.int32) - 2
    other = mine + offsets
    inside = (other >= 0) & (other < total)
    reach = jnp.minimum(band[mine], band[jnp.clip(other, 0, total - 1)])
    return (inside & (jnp.abs(offsets) <= reach)).astype(jnp.int32)


def on_device(dosage, observed, band):
    mine = lax.axis_index(SNP)
    odd = lax.axis_index("yh").reshape(1)
    core = lax.axis_index("core").reshape(1)
    meta = jnp.concatenate([core, odd, lax.axis_index("yl").reshape(1), lax.axis_index("x").reshape(1)]).astype(jnp.int32)

    weight = observed.astype(jnp.float32)
    values = dosage.astype(jnp.float32)
    sums = jnp.stack(
        [
            jnp.sum(weight, axis=0),
            jnp.sum(weight * values, axis=0),
            jnp.sum(weight * values * values, axis=0),
        ]
    )
    cnt, first, second = sum_over_samples(sums)
    mean = first / cnt
    spread = second - first * mean
    stats = jnp.stack([mean, lax.rsqrt(spread + eps * cnt)])

    zed, zed0, zed1, kept, sent = standardize(meta, dosage, observed, stats)
    along = lambda t: lax.ppermute(t, SNP, EVEN_DOWN + ODD_UP)
    across = lambda t: lax.ppermute(t, SNP, TO_OTHER)
    athwart = lambda t: lax.ppermute(t, ("yh", "core"), [(i, 3 - i) for i in range(4)])
    swap = lambda t: lax.ppermute(t, "core", SWAP)
    other0 = across(kept)
    near0 = along(zed0)
    zed_b = swap(zed)
    own = (kept, turn(meta, zed_b))
    rows0 = product(meta, own, (zed, zed_b), lambda p: p, "own")
    near0, other0 = after((near0, other0), rows0)
    other1 = athwart(after(sent, near0, other0))
    near1 = along(after(zed1, near0, other0))
    near0 = (near0, swap(near0))
    rows2 = product(meta, own, near0, chip_of, "first")
    rows0 = fold(meta, rows0, rows2)
    near1, other1 = after((near1, other1), rows2, rows0[0])
    near1 = (near1, swap(near1))
    rows2 = product(meta, own, near1, chip_of, "second", HALF, (rows2,))
    pieces = across_product(meta, (other0, other1), near0, near1, (zed, zed_b))
    rows2 = lax.all_to_all(after(rows2, rows0[0]), CHIP, 0, 0)
    rows2, turned2 = gather(meta, after(rows2, pieces[0]))
    pieces = [pieces[0]] + [
        lax.ppermute(
            pieces[r], CHIP, [(chip_of(i), chip_of(piece_at(i, r))) for i in range(PIECES)]
        )
        for r in range(1, PIECES)
    ]
    rows1, turned1 = gather(meta, *after(pieces, turned2, rows0[1]))
    far = lax.ppermute(turned2, SNP, EVEN_UP + ODD_DOWN)
    beside = lax.ppermute(rows1, SNP, TO_OTHER)
    near = lax.ppermute(after(turned1, far, beside), SNP, EVEN_UP)
    flags = jnp.concatenate([kept_flags(band, mine), odd]).astype(jnp.int32)
    return assemble(flags, far, near, turned1, rows2, beside, rows0)


def solution(mesh):
    whole_mesh = Mesh(mesh.devices.reshape(SIZES), AXES)
    return jax.shard_map(
        on_device,
        mesh=whole_mesh,
        in_specs=(P(SAMP, SNP), P(SAMP, SNP), P()),
        out_specs=P(AXES, None),
        check_vma=False,
    )
```

```python
import jax
import jax.numpy as jnp
from jax import lax
from jax.experimental import pallas as pl
from jax.experimental.pallas import tpu as pltpu
from jax.sharding import Mesh
from jax.sharding import PartitionSpec as P

eps = 1e-05

AXES = ("z", "yh", "yl", "x", "core")
SIZES = (8, 2, 2, 4, 2)
SNP = ("z", "yh")
SAMP = ("yl", "x", "core")
CHIP = ("yl", "x")
NSNP = 16
B = 1024
DEPTH = 1280
HALF = B // 2
FIRST = 768
REST = B - FIRST
STEP = 256
PIECES = 8
ROWS = 64
TURN = 32
SWAP = [(0, 1), (1, 0)]
TO_OTHER = [(i, i ^ 1) for i in range(NSNP)]
EVEN_DOWN = [(i + 2, i) for i in range(0, NSNP - 2, 2)]
ODD_UP = [(i, i + 2) for i in range(1, NSNP - 2, 2)]
EVEN_UP = [(i, i + 2) for i in range(0, NSNP - 2, 2)]
ODD_DOWN = [(i + 2, i) for i in range(1, NSNP - 2, 2)]


def sum_over_samples(x):
    parts = [
        lax.ppermute(x, ("yl", "core"), [(i, i ^ k) for i in range(4)]) for k in (1, 2, 3)
    ]
    x = x + parts[0] + parts[1] + parts[2]
    parts = [
        lax.ppermute(x, "x", [(i, (i + k) % 4) for i in range(4)]) for k in (1, 2, 3)
    ]
    return x + parts[0] + parts[1] + parts[2]


def chip_of(piece):
    return piece // 2 + 4 * (piece % 2)


def piece_at(place, r):
    return (place // 2 + r // 2) % 4 * 2 + (place % 2 ^ r % 2)


def params():
    return pltpu.CompilerParams(vmem_limit_bytes=56 << 20)


def cost(flops, moved):
    return pl.CostEstimate(flops=1024, bytes_accessed=1024, transcendentals=0)


def whole(shape):
    return pl.BlockSpec(shape, lambda j, m: (0,) * len(shape))


def f32(*shape):
    return jax.ShapeDtypeStruct(shape, jnp.float32)


def bf16(*shape):
    return jax.ShapeDtypeStruct(shape, jnp.bfloat16)


def matmul(left, right):
    return jnp.dot(left, right, preferred_element_type=jnp.float32)


def standard_kernel(meta, dosage, observed, stats, zed, zed0, zed1, turned):
    weight = observed[...].astype(jnp.float32)
    values = dosage[...].astype(jnp.float32)
    z = (weight * (values - stats[0:1, :]) * stats[1:2, :]).astype(jnp.bfloat16)
    zed[...] = z
    zed0[...] = z[:, :FIRST]
    zed1[...] = z[:, FIRST:]
    columns = z.T
    for p in range(PIECES):
        for k in range(2):
            at = 2 * ROWS * chip_of(p) + ROWS * k
            turned[meta[0] ^ k, p] = columns[at : at + ROWS]


def standardize(meta, dosage, observed, stats):
    rows = 256
    block = lambda width: pl.BlockSpec((rows, width), lambda i, m: (i, 0))
    turned = pl.BlockSpec((2, PIECES, ROWS, rows), lambda i, m: (0, 0, 0, i))
    return pl.pallas_call(
        standard_kernel,
        name="standardize",
        out_shape=(bf16(DEPTH, B), bf16(DEPTH, FIRST), bf16(DEPTH, REST))
        + (bf16(2, PIECES, ROWS, DEPTH),),
        grid_spec=pltpu.PrefetchScalarGridSpec(
            num_scalar_prefetch=1,
            grid=(DEPTH // rows,),
            in_specs=[block(B), block(B), whole((2, B))],
            out_specs=(block(B), block(FIRST), block(REST), turned),
        ),
        compiler_params=params(),
        cost_estimate=cost(4 * DEPTH * B, 12 * DEPTH * B),
    )(meta, dosage, observed, stats)


LEFT = (PIECES * ROWS, DEPTH)


def flat(*turned):
    return [t.reshape(-1, DEPTH) for t in turned]


def turn_kernel(meta, zed, out):
    turned = zed[...].T

    def store(part):
        out[0] = turned[ROWS * part : ROWS * (part + 1)]

    pl.when(meta[0] == 0)(lambda: store(0))
    pl.when(meta[0] != 0)(lambda: store(1))


def turn(meta, zed):
    return pl.pallas_call(
        turn_kernel,
        name="turn",
        out_shape=bf16(PIECES, ROWS, DEPTH),
        grid_spec=pltpu.PrefetchScalarGridSpec(
            num_scalar_prefetch=1,
            grid=(PIECES,),
            in_specs=[pl.BlockSpec((DEPTH, 2 * ROWS), lambda p, m: (0, p // 2 + 4 * (p % 2)))],
            out_specs=pl.BlockSpec((1, ROWS, DEPTH), lambda p, m: (p, 0, 0)),
        ),
        compiler_params=params(),
        cost_estimate=cost(DEPTH * B, 3 * DEPTH * B),
    )(meta, zed)


def own_kernel(meta, left_a, left_b, right_a, right_b, out):
    acc = matmul(left_a[...], right_a[...]) + matmul(left_b[...], right_b[...])
    out[...] = acc.reshape(PIECES, ROWS, STEP)


def own_product(meta, left, right):
    block = pl.BlockSpec((DEPTH, STEP), lambda j, m: (0, j))
    return pl.pallas_call(
        own_kernel,
        name="own",
        out_shape=f32(PIECES, ROWS, B),
        grid_spec=pltpu.PrefetchScalarGridSpec(
            num_scalar_prefetch=1,
            grid=(B // STEP,),
            in_specs=[whole(LEFT)] * 2 + [block] * 2,
            out_specs=pl.BlockSpec((PIECES, ROWS, STEP), lambda j, m: (0, 0, j)),
        ),
        compiler_params=params(),
        cost_estimate=cost(2 * DEPTH * B * B, 8 * DEPTH * B + 4 * B * B),
    )(meta, *flat(*left), *right)


def store_relative(meta, outs, acc):
    acc = acc.reshape(4, 2, ROWS, STEP)
    for x in range(4):
        for y in range(2):

            @pl.when((meta[3] == x) & (meta[2] == y))
            def _():
                for r in range(PIECES):
                    outs[r][...] = acc[(x + r // 2) % 4, y ^ (r % 2)]


def along_kernel(meta, left_a, left_b, right_a, right_b, *rest):
    acc = matmul(left_a[...], right_a[...]) + matmul(left_b[...], right_b[...])
    store_relative(meta, rest[-PIECES:], acc)


def along_product(meta, left, right, first=0, before=()):
    columns = right[0].shape[1]
    block = pl.BlockSpec((DEPTH, STEP), lambda j, m: (0, j))
    out = pl.BlockSpec((ROWS, STEP), lambda j, m: (0, j + first // STEP))
    return pl.pallas_call(
        along_kernel,
        name="along",
        out_shape=(f32(ROWS, B),) * PIECES,
        grid_spec=pltpu.PrefetchScalarGridSpec(
            num_scalar_prefetch=1,
            grid=(columns // STEP,),
            in_specs=[whole(LEFT)] * 2
            + [block] * 2
            + [pl.BlockSpec(memory_space=pl.ANY)] * len(before),
            out_specs=(out,) * PIECES,
        ),
        input_output_aliases={5 + r: r for r in range(len(before))},
        compiler_params=params(),
        cost_estimate=cost(2 * DEPTH * B * columns, 4 * DEPTH * B + 4 * B * columns),
    )(meta, *flat(*left), *right, *before)


def across_kernel(
    meta, left_a, left_b, near0_a, near0_b, near1_a, near1_b, zed_a, zed_b, *rest
):
    outs, right = rest[:PIECES], rest[PIECES]
    odd = meta[1] == 1
    early = pl.program_id(0) < FIRST // STEP

    def take(a, b):
        right[:DEPTH] = a[...]
        right[DEPTH:] = b[...]

    pl.when(odd)(lambda: take(zed_a, zed_b))
    pl.when(~odd & early)(lambda: take(near0_a, near0_b))
    pl.when(~odd & ~early)(lambda: take(near1_a, near1_b))
    acc = matmul(left_a[...], right[:DEPTH]) + matmul(left_b[...], right[DEPTH:])
    store_relative(meta, outs, acc)


def across_product(meta, left, near0, near1, zed):
    half = FIRST // STEP
    first = pl.BlockSpec((DEPTH, STEP), lambda j, m: (0, jnp.minimum(j, half - 1)))
    second = pl.BlockSpec((DEPTH, STEP), lambda j, m: (0, jnp.maximum(j - half, 0)))
    block = pl.BlockSpec((DEPTH, STEP), lambda j, m: (0, j))
    return pl.pallas_call(
        across_kernel,
        name="across",
        out_shape=(f32(ROWS, B),) * PIECES,
        grid_spec=pltpu.PrefetchScalarGridSpec(
            num_scalar_prefetch=1,
            grid=(B // STEP,),
            in_specs=[whole(LEFT)] * 2 + [first] * 2 + [second] * 2 + [block] * 2,
            out_specs=(pl.BlockSpec((ROWS, STEP), lambda j, m: (0, j)),) * PIECES,
            scratch_shapes=[pltpu.VMEM((2 * DEPTH, STEP), jnp.bfloat16)],
        ),
        compiler_params=params(),
        cost_estimate=cost(2 * DEPTH * B * B, 12 * DEPTH * B + 4 * B * B),
    )(meta, *flat(*left), *near0, *near1, *zed)


def after(value, *others):
    return lax.optimization_barrier((value, *others))[0]


def add_kernel(meta, parts, keep, send):
    mine = meta[2]
    for out, half in ((keep, mine), (send, 1 - mine)):
        out[...] = parts[0, half] + parts[1, half] + parts[2, half] + parts[3, half]


def fold(meta, parts, *others):
    _, rows, columns = parts.shape
    parts = lax.all_to_all(parts.reshape(4, 2, rows, columns), "x", 0, 0)
    parts = after(parts, *others)
    step = 2 * STEP
    out = pl.BlockSpec((rows, step), lambda j, m: (0, j))
    keep, send = pl.pallas_call(
        add_kernel,
        name="add",
        out_shape=(f32(rows, columns),) * 2,
        grid_spec=pltpu.PrefetchScalarGridSpec(
            num_scalar_prefetch=1,
            grid=(columns // step,),
            in_specs=[pl.BlockSpec((4, 2, rows, step), lambda j, m: (0, 0, 0, j))],
            out_specs=(out, out),
        ),
        compiler_params=params(),
        cost_estimate=cost(6 * rows * columns, 40 * rows * columns),
    )(meta, parts)
    return keep, lax.ppermute(send, "yl", SWAP)


def gather_kernel(meta, *refs):
    parts, (rows, packed) = refs[:-2], refs[-2:]
    if len(parts) == 1:
        parts = [parts[0].at[r] for r in range(PIECES)]
    total = parts[0][...]
    for part in parts[1:]:
        total = total + part[...]
    rows[...] = total
    for s in range(2 * STEP // ROWS):
        packed[s, :, :ROWS] = total[:TURN, ROWS * s : ROWS * (s + 1)]
        packed[s, :, ROWS:] = total[TURN:, ROWS * s : ROWS * (s + 1)]


def gather(meta, *parts):
    step = 2 * STEP
    packed = (2 * PIECES, TURN, 2 * ROWS)
    spec = lambda t: pl.BlockSpec(
        t.shape[:-1] + (step,), lambda j, m: (0,) * (t.ndim - 1) + (j,)
    )
    rows, packed = pl.pallas_call(
        gather_kernel,
        name="gather",
        out_shape=(f32(ROWS, B), f32(*packed)),
        grid_spec=pltpu.PrefetchScalarGridSpec(
            num_scalar_prefetch=1,
            grid=(B // step,),
            in_specs=[spec(t) for t in parts],
            out_specs=(
                pl.BlockSpec((ROWS, step), lambda j, m: (0, j)),
                pl.BlockSpec((step // ROWS, TURN, 2 * ROWS), lambda j, m: (j, 0, 0)),
            ),
        ),
        compiler_params=params(),
        cost_estimate=cost(ROWS * B, 16 * ROWS * B),
    )(meta, *parts)
    return rows, lax.all_to_all(packed, SAMP, 0, 0).reshape(HALF, 2 * ROWS)


def send_pieces(pieces):
    pairs = lambda r: [(chip_of(i), chip_of(piece_at(i, r))) for i in range(PIECES)]
    return [pieces[0]] + [lax.ppermute(pieces[r], CHIP, pairs(r)) for r in range(1, PIECES)]


def unpack(out, packed):
    turned = packed[...].T
    for s in range(2 * PIECES):
        out[:, ROWS * s : ROWS * s + TURN] = turned[:ROWS, TURN * s : TURN * (s + 1)]
        out[:, ROWS * s + TURN : ROWS * (s + 1)] = turned[ROWS:, TURN * s : TURN * (s + 1)]


def assemble_kernel(flags, far, near, here, rows2, beside, rows0_a, rows0_b, out, far_t, near_t):
    even = flags[5] == 0
    unpack(far_t, far)
    pl.when(even)(lambda: unpack(near_t, near))
    pl.when(~even)(lambda: unpack(near_t, here))
    turned, mine = far_t[...], rows2[...]
    blocks = (
        jnp.where(even, turned, mine),
        near_t[...],
        rows0_a[...] + rows0_b[...],
        beside[...],
        jnp.where(even, mine, turned),
    )
    for d, block in enumerate(blocks):
        out[:, B * d : B * (d + 1)] = jnp.where(flags[d] > 0, block, 0.0)


def assemble(flags, far, near, here, rows2, beside, rows0):
    return pl.pallas_call(
        assemble_kernel,
        name="assemble",
        out_shape=f32(ROWS, 5 * B),
        grid_spec=pltpu.PrefetchScalarGridSpec(
            num_scalar_prefetch=1,
            grid=(1,),
            in_specs=[whole((HALF, 2 * ROWS))] * 3 + [whole((ROWS, B))] * 4,
            out_specs=whole((ROWS, 5 * B)),
            scratch_shapes=[pltpu.VMEM((ROWS, B), jnp.float32)] * 2,
        ),
        compiler_params=params(),
        cost_estimate=cost(ROWS * 5 * B, 40 * ROWS * B),
    )(flags, far, near, here, rows2, beside, *rows0)


def kept_flags(band, mine):
    total = band.shape[0]
    offsets = jnp.arange(5, dtype=jnp.int32) - 2
    other = mine + offsets
    inside = (other >= 0) & (other < total)
    reach = jnp.minimum(band[mine], band[jnp.clip(other, 0, total - 1)])
    return (inside & (jnp.abs(offsets) <= reach)).astype(jnp.int32)


def on_device(dosage, observed, band):
    mine = lax.axis_index(SNP)
    odd = lax.axis_index("yh").reshape(1)
    core = lax.axis_index("core").reshape(1)
    meta = jnp.concatenate([core, odd, lax.axis_index("yl").reshape(1), lax.axis_index("x").reshape(1)]).astype(jnp.int32)

    weight = observed.astype(jnp.float32)
    values = dosage.astype(jnp.float32)
    sums = jnp.stack(
        [
            jnp.sum(weight, axis=0),
            jnp.sum(weight * values, axis=0),
            jnp.sum(weight * values * values, axis=0),
        ]
    )
    cnt, first, second = sum_over_samples(sums)
    mean = first / cnt
    spread = second - first * mean
    stats = jnp.stack([mean, lax.rsqrt(spread + eps * cnt)])

    zed, zed0, zed1, turned = standardize(meta, dosage, observed, stats)
    along = lambda t: lax.ppermute(t, SNP, EVEN_DOWN + ODD_UP)
    swap = lambda t: lax.ppermute(t, "core", SWAP)
    other = lax.ppermute(turned, SNP, TO_OTHER)
    near0 = along(zed0)
    zed_b = swap(zed)
    own = (turned, turn(meta, zed_b))
    rows0 = own_product(meta, own, (zed, zed_b))
    near0 = after(near0, rows0)
    near1 = along(after(zed1, near0))
    near0 = (near0, swap(near0))
    rows2 = along_product(meta, own, near0)
    rows0 = fold(meta, rows0, rows2[0])
    near1, other = after((near1, other), rows2[0], rows0[0])
    near1 = (near1, swap(near1))
    other = (other, swap(other[1]))
    pieces = across_product(meta, other, near0, near1, (zed, zed_b))
    near1 = after(near1, pieces[0])
    rows2 = along_product(meta, own, near1, FIRST, rows2)
    rows1, turned1 = gather(meta, *after(send_pieces(pieces), rows2[0]))
    beside = lax.ppermute(rows1, SNP, TO_OTHER)
    near = lax.ppermute(turned1, SNP, EVEN_UP)
    rows2, turned2 = gather(meta, *after(send_pieces(rows2), rows1))
    far = lax.ppermute(after(turned2, near, beside, rows0[1]), SNP, EVEN_UP + ODD_DOWN)
    flags = jnp.concatenate([kept_flags(band, mine), odd]).astype(jnp.int32)
    return assemble(flags, far, near, turned1, rows2, beside, rows0)


def solution(mesh):
    whole_mesh = Mesh(mesh.devices.reshape(SIZES), AXES)
    return jax.shard_map(
        on_device,
        mesh=whole_mesh,
        in_specs=(P(SAMP, SNP), P(SAMP, SNP), P()),
        out_specs=P(AXES, None),
        check_vma=False,
    )
```

```python
import jax
import jax.numpy as jnp
from jax import lax
from jax.experimental import pallas as pl
from jax.experimental.pallas import tpu as pltpu
from jax.sharding import Mesh
from jax.sharding import PartitionSpec as P

eps = 1e-05

AXES = ("z", "yh", "yl", "x", "core")
SIZES = (8, 2, 2, 4, 2)
SNP = ("z", "yh")
SAMP = ("yl", "x", "core")
NSNP = 16
B = 1024
DEPTH = 1280
HALF = B // 2
STEP = 256
PIECES = 8
ROWS = 64
TURN = 32
SWAP = [(0, 1), (1, 0)]
TO_OTHER = [(i, i ^ 1) for i in range(NSNP)]
EVEN_DOWN = [(i + 2, i) for i in range(0, NSNP - 2, 2)]
ODD_UP = [(i, i + 2) for i in range(1, NSNP - 2, 2)]
EVEN_UP = [(i, i + 2) for i in range(0, NSNP - 2, 2)]
ODD_DOWN = [(i + 2, i) for i in range(1, NSNP - 2, 2)]


def sum_over_samples(x):
    parts = [
        lax.ppermute(x, ("yl", "core"), [(i, i ^ k) for i in range(4)]) for k in (1, 2, 3)
    ]
    x = x + parts[0] + parts[1] + parts[2]
    parts = [
        lax.ppermute(x, "x", [(i, (i + k) % 4) for i in range(4)]) for k in (1, 2, 3)
    ]
    return x + parts[0] + parts[1] + parts[2]


def chip_of(piece):
    return piece // 2 + 4 * (piece % 2)


def params():
    return pltpu.CompilerParams(vmem_limit_bytes=56 << 20)


def cost(flops, moved):
    return pl.CostEstimate(flops=1024, bytes_accessed=1024, transcendentals=0)


def whole(shape):
    return pl.BlockSpec(shape, lambda j, m: (0,) * len(shape))


def f32(*shape):
    return jax.ShapeDtypeStruct(shape, jnp.float32)


def bf16(*shape):
    return jax.ShapeDtypeStruct(shape, jnp.bfloat16)


def matmul(left, right):
    return jnp.dot(left, right, preferred_element_type=jnp.float32)


def standard_kernel(meta, dosage, observed, stats, zed, zed0, zed1, turned):
    weight = observed[...].astype(jnp.float32)
    values = dosage[...].astype(jnp.float32)
    z = (weight * (values - stats[0:1, :]) * stats[1:2, :]).astype(jnp.bfloat16)
    zed[...] = z
    zed0[...] = z[:, :HALF]
    zed1[...] = z[:, HALF:]
    columns = z.T
    for p in range(PIECES):
        for k in range(2):
            at = 2 * ROWS * chip_of(p) + ROWS * k
            turned[meta[0] ^ k, p] = columns[at : at + ROWS]


def standardize(meta, dosage, observed, stats):
    rows = 256
    block = lambda width: pl.BlockSpec((rows, width), lambda i, m: (i, 0))
    turned = pl.BlockSpec((2, PIECES, ROWS, rows), lambda i, m: (0, 0, 0, i))
    return pl.pallas_call(
        standard_kernel,
        name="standardize",
        out_shape=(bf16(DEPTH, B), bf16(DEPTH, HALF), bf16(DEPTH, HALF))
        + (bf16(2, PIECES, ROWS, DEPTH),),
        grid_spec=pltpu.PrefetchScalarGridSpec(
            num_scalar_prefetch=1,
            grid=(DEPTH // rows,),
            in_specs=[block(B), block(B), whole((2, B))],
            out_specs=(block(B), block(HALF), block(HALF), turned),
        ),
        compiler_params=params(),
        cost_estimate=cost(4 * DEPTH * B, 12 * DEPTH * B),
    )(meta, dosage, observed, stats)


LEFT = (PIECES * ROWS, DEPTH)


def flat(*turned):
    return [t.reshape(-1, DEPTH) for t in turned]


def turn_kernel(meta, zed, out):
    turned = zed[...].T

    def store(part):
        out[0] = turned[ROWS * part : ROWS * (part + 1)]

    pl.when(meta[0] == 0)(lambda: store(0))
    pl.when(meta[0] != 0)(lambda: store(1))


def turn(meta, zed):
    return pl.pallas_call(
        turn_kernel,
        name="turn",
        out_shape=bf16(PIECES, ROWS, DEPTH),
        grid_spec=pltpu.PrefetchScalarGridSpec(
            num_scalar_prefetch=1,
            grid=(PIECES,),
            in_specs=[pl.BlockSpec((DEPTH, 2 * ROWS), lambda p, m: (0, p // 2 + 4 * (p % 2)))],
            out_specs=pl.BlockSpec((1, ROWS, DEPTH), lambda p, m: (p, 0, 0)),
        ),
        compiler_params=params(),
        cost_estimate=cost(DEPTH * B, 3 * DEPTH * B),
    )(meta, zed)


def product_kernel(meta, left_a, left_b, right_a, right_b, *rest):
    acc = matmul(left_a[...], right_a[...]) + matmul(left_b[...], right_b[...])
    rest[-1][...] = acc.reshape(PIECES, ROWS, STEP)


def product(meta, left, right, name, first=0, before=()):
    columns = right[0].shape[1]
    block = pl.BlockSpec((DEPTH, STEP), lambda j, m: (0, j))
    return pl.pallas_call(
        product_kernel,
        name=name,
        out_shape=f32(PIECES, ROWS, B),
        grid_spec=pltpu.PrefetchScalarGridSpec(
            num_scalar_prefetch=1,
            grid=(columns // STEP,),
            in_specs=[whole(LEFT)] * 2
            + [block] * 2
            + [pl.BlockSpec(memory_space=pl.ANY)] * len(before),
            out_specs=pl.BlockSpec((PIECES, ROWS, STEP), lambda j, m: (0, 0, j + first // STEP)),
        ),
        input_output_aliases={5: 0} if before else {},
        compiler_params=params(),
        cost_estimate=cost(2 * DEPTH * B * columns, 4 * DEPTH * B + 4 * B * columns),
    )(meta, *flat(*left), *right, *before)


def across_kernel(
    meta, left_a, left_b, near0_a, near0_b, near1_a, near1_b, zed_a, zed_b, *rest
):
    outs, right = rest[:4], rest[4]
    odd = meta[1] == 1
    early = pl.program_id(0) < HALF // STEP

    def take(a, b):
        right[:DEPTH] = a[...]
        right[DEPTH:] = b[...]

    pl.when(odd)(lambda: take(zed_a, zed_b))
    pl.when(~odd & early)(lambda: take(near0_a, near0_b))
    pl.when(~odd & ~early)(lambda: take(near1_a, near1_b))
    acc = matmul(left_a[...], right[:DEPTH]) + matmul(left_b[...], right[DEPTH:])
    acc = acc.reshape(4, 2, ROWS, STEP)
    for x in range(4):

        @pl.when(meta[3] == x)
        def _():
            for k in range(4):
                outs[k][...] = acc[(x + k) % 4]


def across_product(meta, left, near0, near1, zed):
    half = HALF // STEP
    first = pl.BlockSpec((DEPTH, STEP), lambda j, m: (0, jnp.minimum(j, half - 1)))
    second = pl.BlockSpec((DEPTH, STEP), lambda j, m: (0, jnp.maximum(j - half, 0)))
    block = pl.BlockSpec((DEPTH, STEP), lambda j, m: (0, j))
    return pl.pallas_call(
        across_kernel,
        name="across",
        out_shape=(f32(2, ROWS, B),) * 4,
        grid_spec=pltpu.PrefetchScalarGridSpec(
            num_scalar_prefetch=1,
            grid=(B // STEP,),
            in_specs=[whole(LEFT)] * 2 + [first] * 2 + [second] * 2 + [block] * 2,
            out_specs=(pl.BlockSpec((2, ROWS, STEP), lambda j, m: (0, 0, j)),) * 4,
            scratch_shapes=[pltpu.VMEM((2 * DEPTH, STEP), jnp.bfloat16)],
        ),
        compiler_params=params(),
        cost_estimate=cost(2 * DEPTH * B * B, 12 * DEPTH * B + 4 * B * B),
    )(meta, *flat(*left), *near0, *near1, *zed)


def after(value, *others):
    return lax.optimization_barrier((value, *others))[0]


def add_kernel(meta, *refs):
    parts, (keep, send) = refs[:-2], refs[-2:]
    if len(parts) == 1:
        parts = [parts[0].at[k] for k in range(4)]
    mine = meta[2]
    for out, half in ((keep, mine), (send, 1 - mine)):
        out[...] = parts[0][half] + parts[1][half] + parts[2][half] + parts[3][half]


def add(meta, *parts):
    rows, columns = parts[0].shape[-2:]
    step = 2 * STEP
    out = pl.BlockSpec((rows, step), lambda j, m: (0, j))
    spec = lambda t: pl.BlockSpec(t.shape[:-1] + (step,), lambda j, m: (0,) * (t.ndim - 1) + (j,))
    keep, send = pl.pallas_call(
        add_kernel,
        name="add",
        out_shape=(f32(rows, columns),) * 2,
        grid_spec=pltpu.PrefetchScalarGridSpec(
            num_scalar_prefetch=1,
            grid=(columns // step,),
            in_specs=[spec(t) for t in parts],
            out_specs=(out, out),
        ),
        compiler_params=params(),
        cost_estimate=cost(6 * rows * columns, 40 * rows * columns),
    )(meta, *parts)
    return keep, lax.ppermute(send, "yl", SWAP)


def fold(meta, parts, *others):
    _, rows, columns = parts.shape
    parts = lax.all_to_all(parts.reshape(4, 2, rows, columns), "x", 0, 0)
    return add(meta, after(parts, *others))


def fold_pieces(meta, pieces, *others):
    moved = [
        lax.ppermute(pieces[k], "x", [(i, (i + k) % 4) for i in range(4)]) for k in (1, 2, 3)
    ]
    return add(meta, *after((pieces[0], *moved), *others))


def gather_kernel(meta, *refs):
    parts, (rows, packed) = refs[:-2], refs[-2:]
    if len(parts) == 1:
        parts = [parts[0].at[r] for r in range(PIECES)]
    total = parts[0][...]
    for part in parts[1:]:
        total = total + part[...]
    rows[...] = total
    for s in range(2 * STEP // ROWS):
        packed[s, :, :ROWS] = total[:TURN, ROWS * s : ROWS * (s + 1)]
        packed[s, :, ROWS:] = total[TURN:, ROWS * s : ROWS * (s + 1)]


def gather(meta, *parts):
    step = 2 * STEP
    packed = (2 * PIECES, TURN, 2 * ROWS)
    spec = lambda t: pl.BlockSpec(
        t.shape[:-1] + (step,), lambda j, m: (0,) * (t.ndim - 1) + (j,)
    )
    rows, packed = pl.pallas_call(
        gather_kernel,
        name="gather",
        out_shape=(f32(ROWS, B), f32(*packed)),
        grid_spec=pltpu.PrefetchScalarGridSpec(
            num_scalar_prefetch=1,
            grid=(B // step,),
            in_specs=[spec(t) for t in parts],
            out_specs=(
                pl.BlockSpec((ROWS, step), lambda j, m: (0, j)),
                pl.BlockSpec((step // ROWS, TURN, 2 * ROWS), lambda j, m: (j, 0, 0)),
            ),
        ),
        compiler_params=params(),
        cost_estimate=cost(ROWS * B, 16 * ROWS * B),
    )(meta, *parts)
    return rows, lax.all_to_all(packed, SAMP, 0, 0).reshape(HALF, 2 * ROWS)


def unpack(out, packed):
    turned = packed[...].T
    for s in range(2 * PIECES):
        out[:, ROWS * s : ROWS * s + TURN] = turned[:ROWS, TURN * s : TURN * (s + 1)]
        out[:, ROWS * s + TURN : ROWS * (s + 1)] = turned[ROWS:, TURN * s : TURN * (s + 1)]


def assemble_kernel(flags, far, near, here, rows2, beside, rows0_a, rows0_b, out, far_t, near_t):
    even = flags[5] == 0
    unpack(far_t, far)
    pl.when(even)(lambda: unpack(near_t, near))
    pl.when(~even)(lambda: unpack(near_t, here))
    turned, mine = far_t[...], rows2[...]
    blocks = (
        jnp.where(even, turned, mine),
        near_t[...],
        rows0_a[...] + rows0_b[...],
        beside[...],
        jnp.where(even, mine, turned),
    )
    for d, block in enumerate(blocks):
        out[:, B * d : B * (d + 1)] = jnp.where(flags[d] > 0, block, 0.0)


def assemble(flags, far, near, here, rows2, beside, rows0):
    return pl.pallas_call(
        assemble_kernel,
        name="assemble",
        out_shape=f32(ROWS, 5 * B),
        grid_spec=pltpu.PrefetchScalarGridSpec(
            num_scalar_prefetch=1,
            grid=(1,),
            in_specs=[whole((HALF, 2 * ROWS))] * 3 + [whole((ROWS, B))] * 4,
            out_specs=whole((ROWS, 5 * B)),
            scratch_shapes=[pltpu.VMEM((ROWS, B), jnp.float32)] * 2,
        ),
        compiler_params=params(),
        cost_estimate=cost(ROWS * 5 * B, 40 * ROWS * B),
    )(flags, far, near, here, rows2, beside, *rows0)


def kept_flags(band, mine):
    total = band.shape[0]
    offsets = jnp.arange(5, dtype=jnp.int32) - 2
    other = mine + offsets
    inside = (other >= 0) & (other < total)
    reach = jnp.minimum(band[mine], band[jnp.clip(other, 0, total - 1)])
    return (inside & (jnp.abs(offsets) <= reach)).astype(jnp.int32)


def on_device(dosage, observed, band):
    mine = lax.axis_index(SNP)
    odd = lax.axis_index("yh").reshape(1)
    core = lax.axis_index("core").reshape(1)
    meta = jnp.concatenate([core, odd, lax.axis_index("yl").reshape(1), lax.axis_index("x").reshape(1)]).astype(jnp.int32)

    weight = observed.astype(jnp.float32)
    values = dosage.astype(jnp.float32)
    sums = jnp.stack(
        [
            jnp.sum(weight, axis=0),
            jnp.sum(weight * values, axis=0),
            jnp.sum(weight * values * values, axis=0),
        ]
    )
    cnt, first, second = sum_over_samples(sums)
    mean = first / cnt
    spread = second - first * mean
    stats = jnp.stack([mean, lax.rsqrt(spread + eps * cnt)])

    zed, zed0, zed1, turned = standardize(meta, dosage, observed, stats)
    along = lambda t: lax.ppermute(t, SNP, EVEN_DOWN + ODD_UP)
    swap = lambda t: lax.ppermute(t, "core", SWAP)
    other = lax.ppermute(turned, SNP, TO_OTHER)
    near0 = along(zed0)
    zed_b = swap(zed)
    own = (turned, turn(meta, zed_b))
    rows0 = product(meta, own, (zed, zed_b), "own")
    near0 = after(near0, rows0)
    near1 = along(after(zed1, near0))
    rows0 = fold(meta, rows0)
    near0 = after((near0, swap(near0)), rows0[0])
    rows2 = product(meta, own, near0, "first")
    near1, other = after((near1, other), rows2)
    near1 = (near1, swap(near1))
    other = (other, swap(other[1]))
    near1 = after(near1, other[1])
    rows2 = product(meta, own, near1, "second", HALF, (rows2,))
    other = after(other, rows2)
    pieces = across_product(meta, other, near0, near1, (zed, zed_b))
    rows2 = fold(meta, rows2, pieces[0])
    rows2, turned2 = gather(meta, *rows2)
    far = lax.ppermute(turned2, SNP, EVEN_UP + ODD_DOWN)
    rows1 = fold_pieces(meta, pieces, turned2, rows0[1])
    rows1, turned1 = gather(meta, *rows1)
    beside = lax.ppermute(rows1, SNP, TO_OTHER)
    near = lax.ppermute(after(turned1, far, beside), SNP, EVEN_UP)
    flags = jnp.concatenate([kept_flags(band, mine), odd]).astype(jnp.int32)
    return assemble(flags, far, near, turned1, rows2, beside, rows0)


def solution(mesh):
    whole_mesh = Mesh(mesh.devices.reshape(SIZES), AXES)
    return jax.shard_map(
        on_device,
        mesh=whole_mesh,
        in_specs=(P(SAMP, SNP), P(SAMP, SNP), P()),
        out_specs=P(AXES, None),
        check_vma=False,
    )
```

```python
import jax
import jax.numpy as jnp
from jax import lax
from jax.experimental import pallas as pl
from jax.experimental.pallas import tpu as pltpu
from jax.sharding import Mesh
from jax.sharding import PartitionSpec as P

eps = 1e-05

AXES = ("z", "yh", "yl", "x", "core")
SIZES = (8, 2, 2, 4, 2)
SNP = ("z", "yh")
SAMP = ("yl", "x", "core")
NSNP = 16
B = 1024
DEPTH = 1280
HALF = B // 2
STEP = 256
PIECES = 8
ROWS = 64
TURN = 32
SWAP = [(0, 1), (1, 0)]
TO_OTHER = [(i, i ^ 1) for i in range(NSNP)]
EVEN_DOWN = [(i + 2, i) for i in range(0, NSNP - 2, 2)]
ODD_UP = [(i, i + 2) for i in range(1, NSNP - 2, 2)]
EVEN_UP = [(i, i + 2) for i in range(0, NSNP - 2, 2)]
ODD_DOWN = [(i + 2, i) for i in range(1, NSNP - 2, 2)]


def sum_over_samples(x):
    parts = [
        lax.ppermute(x, ("yl", "core"), [(i, i ^ k) for i in range(4)]) for k in (1, 2, 3)
    ]
    x = x + parts[0] + parts[1] + parts[2]
    parts = [
        lax.ppermute(x, "x", [(i, (i + k) % 4) for i in range(4)]) for k in (1, 2, 3)
    ]
    return x + parts[0] + parts[1] + parts[2]


def chip_of(piece):
    return piece // 2 + 4 * (piece % 2)


def params():
    return pltpu.CompilerParams(vmem_limit_bytes=56 << 20)


def cost(flops, moved):
    return pl.CostEstimate(flops=1024, bytes_accessed=1024, transcendentals=0)


def whole(shape):
    return pl.BlockSpec(shape, lambda j, m: (0,) * len(shape))


def f32(*shape):
    return jax.ShapeDtypeStruct(shape, jnp.float32)


def bf16(*shape):
    return jax.ShapeDtypeStruct(shape, jnp.bfloat16)


def matmul(left, right):
    return jnp.dot(left, right, preferred_element_type=jnp.float32)


def standard_kernel(meta, dosage, observed, stats, zed, turned):
    weight = observed[...].astype(jnp.float32)
    values = dosage[...].astype(jnp.float32)
    z = (weight * (values - stats[0:1, :]) * stats[1:2, :]).astype(jnp.bfloat16)
    zed[...] = z
    columns = z.T
    for p in range(PIECES):
        for k in range(2):
            at = 2 * ROWS * chip_of(p) + ROWS * k
            turned[meta[0] ^ k, p] = columns[at : at + ROWS]


def standardize(meta, dosage, observed, stats):
    rows = 256
    block = lambda width: pl.BlockSpec((rows, width), lambda i, m: (i, 0))
    turned = pl.BlockSpec((2, PIECES, ROWS, rows), lambda i, m: (0, 0, 0, i))
    return pl.pallas_call(
        standard_kernel,
        name="standardize",
        out_shape=(bf16(DEPTH, B),)
        + (bf16(2, PIECES, ROWS, DEPTH),),
        grid_spec=pltpu.PrefetchScalarGridSpec(
            num_scalar_prefetch=1,
            grid=(DEPTH // rows,),
            in_specs=[block(B), block(B), whole((2, B))],
            out_specs=(block(B), turned),
        ),
        compiler_params=params(),
        cost_estimate=cost(4 * DEPTH * B, 12 * DEPTH * B),
    )(meta, dosage, observed, stats)


LEFT = (PIECES * ROWS, DEPTH)


def flat(*turned):
    return [t.reshape(-1, DEPTH) for t in turned]


def turn_kernel(meta, zed, out):
    turned = zed[...].T

    def store(part):
        out[0] = turned[ROWS * part : ROWS * (part + 1)]

    pl.when(meta[0] == 0)(lambda: store(0))
    pl.when(meta[0] != 0)(lambda: store(1))


def turn(meta, zed):
    return pl.pallas_call(
        turn_kernel,
        name="turn",
        out_shape=bf16(PIECES, ROWS, DEPTH),
        grid_spec=pltpu.PrefetchScalarGridSpec(
            num_scalar_prefetch=1,
            grid=(PIECES,),
            in_specs=[pl.BlockSpec((DEPTH, 2 * ROWS), lambda p, m: (0, p // 2 + 4 * (p % 2)))],
            out_specs=pl.BlockSpec((1, ROWS, DEPTH), lambda p, m: (p, 0, 0)),
        ),
        compiler_params=params(),
        cost_estimate=cost(DEPTH * B, 3 * DEPTH * B),
    )(meta, zed)


def product_kernel(meta, left_a, left_b, right_a, right_b, out):
    acc = matmul(left_a[...], right_a[...]) + matmul(left_b[...], right_b[...])
    out[...] = acc.reshape(PIECES, ROWS, STEP)


def product(meta, left, right, name):
    block = pl.BlockSpec((DEPTH, STEP), lambda j, m: (0, j))
    return pl.pallas_call(
        product_kernel,
        name=name,
        out_shape=f32(PIECES, ROWS, B),
        grid_spec=pltpu.PrefetchScalarGridSpec(
            num_scalar_prefetch=1,
            grid=(B // STEP,),
            in_specs=[whole(LEFT)] * 2 + [block] * 2,
            out_specs=pl.BlockSpec((PIECES, ROWS, STEP), lambda j, m: (0, 0, j)),
        ),
        compiler_params=params(),
        cost_estimate=cost(2 * DEPTH * B * B, 8 * DEPTH * B + 4 * B * B),
    )(meta, *flat(*left), *right)


def across_kernel(meta, left_a, left_b, near_a, near_b, zed_a, zed_b, *rest):
    outs, right = rest[:4], rest[4]
    odd = meta[1] == 1

    def take(a, b):
        right[:DEPTH] = a[...]
        right[DEPTH:] = b[...]

    pl.when(odd)(lambda: take(zed_a, zed_b))
    pl.when(~odd)(lambda: take(near_a, near_b))
    acc = matmul(left_a[...], right[:DEPTH]) + matmul(left_b[...], right[DEPTH:])
    acc = acc.reshape(4, 2, ROWS, STEP)
    for x in range(4):

        @pl.when(meta[3] == x)
        def _():
            for k in range(4):
                outs[k][...] = acc[(x + k) % 4]


def across_product(meta, left, near, zed):
    block = pl.BlockSpec((DEPTH, STEP), lambda j, m: (0, j))
    return pl.pallas_call(
        across_kernel,
        name="across",
        out_shape=(f32(2, ROWS, B),) * 4,
        grid_spec=pltpu.PrefetchScalarGridSpec(
            num_scalar_prefetch=1,
            grid=(B // STEP,),
            in_specs=[whole(LEFT)] * 2 + [block] * 4,
            out_specs=(pl.BlockSpec((2, ROWS, STEP), lambda j, m: (0, 0, j)),) * 4,
            scratch_shapes=[pltpu.VMEM((2 * DEPTH, STEP), jnp.bfloat16)],
        ),
        compiler_params=params(),
        cost_estimate=cost(2 * DEPTH * B * B, 12 * DEPTH * B + 4 * B * B),
    )(meta, *flat(*left), *near, *zed)


def after(value, *others):
    return lax.optimization_barrier((value, *others))[0]


def add_kernel(meta, *refs):
    parts, (keep, send) = refs[:-2], refs[-2:]
    if len(parts) == 1:
        parts = [parts[0].at[k] for k in range(4)]
    mine = meta[2]
    for out, half in ((keep, mine), (send, 1 - mine)):
        out[...] = parts[0][half] + parts[1][half] + parts[2][half] + parts[3][half]


def add(meta, *parts):
    rows, columns = parts[0].shape[-2:]
    step = 2 * STEP
    out = pl.BlockSpec((rows, step), lambda j, m: (0, j))
    spec = lambda t: pl.BlockSpec(t.shape[:-1] + (step,), lambda j, m: (0,) * (t.ndim - 1) + (j,))
    keep, send = pl.pallas_call(
        add_kernel,
        name="add",
        out_shape=(f32(rows, columns),) * 2,
        grid_spec=pltpu.PrefetchScalarGridSpec(
            num_scalar_prefetch=1,
            grid=(columns // step,),
            in_specs=[spec(t) for t in parts],
            out_specs=(out, out),
        ),
        compiler_params=params(),
        cost_estimate=cost(6 * rows * columns, 40 * rows * columns),
    )(meta, *parts)
    return keep, lax.ppermute(send, "yl", SWAP)


def fold(meta, parts, *others):
    _, rows, columns = parts.shape
    parts = lax.all_to_all(parts.reshape(4, 2, rows, columns), "x", 0, 0)
    return add(meta, after(parts, *others))


def fold_pieces(meta, pieces, *others):
    moved = [
        lax.ppermute(pieces[k], "x", [(i, (i + k) % 4) for i in range(4)]) for k in (1, 2, 3)
    ]
    return add(meta, *after((pieces[0], *moved), *others))


def gather_kernel(meta, *refs):
    parts, (rows, packed) = refs[:-2], refs[-2:]
    if len(parts) == 1:
        parts = [parts[0].at[r] for r in range(PIECES)]
    total = parts[0][...]
    for part in parts[1:]:
        total = total + part[...]
    rows[...] = total
    for s in range(2 * STEP // ROWS):
        packed[s, :, :ROWS] = total[:TURN, ROWS * s : ROWS * (s + 1)]
        packed[s, :, ROWS:] = total[TURN:, ROWS * s : ROWS * (s + 1)]


def gather(meta, *parts):
    step = 2 * STEP
    packed = (2 * PIECES, TURN, 2 * ROWS)
    spec = lambda t: pl.BlockSpec(
        t.shape[:-1] + (step,), lambda j, m: (0,) * (t.ndim - 1) + (j,)
    )
    rows, packed = pl.pallas_call(
        gather_kernel,
        name="gather",
        out_shape=(f32(ROWS, B), f32(*packed)),
        grid_spec=pltpu.PrefetchScalarGridSpec(
            num_scalar_prefetch=1,
            grid=(B // step,),
            in_specs=[spec(t) for t in parts],
            out_specs=(
                pl.BlockSpec((ROWS, step), lambda j, m: (0, j)),
                pl.BlockSpec((step // ROWS, TURN, 2 * ROWS), lambda j, m: (j, 0, 0)),
            ),
        ),
        compiler_params=params(),
        cost_estimate=cost(ROWS * B, 16 * ROWS * B),
    )(meta, *parts)
    return rows, lax.all_to_all(packed, SAMP, 0, 0).reshape(HALF, 2 * ROWS)


def unpack(out, packed):
    turned = packed[...].T
    for s in range(2 * PIECES):
        out[:, ROWS * s : ROWS * s + TURN] = turned[:ROWS, TURN * s : TURN * (s + 1)]
        out[:, ROWS * s + TURN : ROWS * (s + 1)] = turned[ROWS:, TURN * s : TURN * (s + 1)]


def assemble_kernel(flags, far, near, here, rows2, beside, rows0_a, rows0_b, out, far_t, near_t):
    even = flags[5] == 0
    unpack(far_t, far)
    pl.when(even)(lambda: unpack(near_t, near))
    pl.when(~even)(lambda: unpack(near_t, here))
    turned, mine = far_t[...], rows2[...]
    blocks = (
        jnp.where(even, turned, mine),
        near_t[...],
        rows0_a[...] + rows0_b[...],
        beside[...],
        jnp.where(even, mine, turned),
    )
    for d, block in enumerate(blocks):
        out[:, B * d : B * (d + 1)] = jnp.where(flags[d] > 0, block, 0.0)


def assemble(flags, far, near, here, rows2, beside, rows0):
    return pl.pallas_call(
        assemble_kernel,
        name="assemble",
        out_shape=f32(ROWS, 5 * B),
        grid_spec=pltpu.PrefetchScalarGridSpec(
            num_scalar_prefetch=1,
            grid=(1,),
            in_specs=[whole((HALF, 2 * ROWS))] * 3 + [whole((ROWS, B))] * 4,
            out_specs=whole((ROWS, 5 * B)),
            scratch_shapes=[pltpu.VMEM((ROWS, B), jnp.float32)] * 2,
        ),
        compiler_params=params(),
        cost_estimate=cost(ROWS * 5 * B, 40 * ROWS * B),
    )(flags, far, near, here, rows2, beside, *rows0)


def kept_flags(band, mine):
    total = band.shape[0]
    offsets = jnp.arange(5, dtype=jnp.int32) - 2
    other = mine + offsets
    inside = (other >= 0) & (other < total)
    reach = jnp.minimum(band[mine], band[jnp.clip(other, 0, total - 1)])
    return (inside & (jnp.abs(offsets) <= reach)).astype(jnp.int32)


def on_device(dosage, observed, band):
    mine = lax.axis_index(SNP)
    odd = lax.axis_index("yh").reshape(1)
    core = lax.axis_index("core").reshape(1)
    meta = jnp.concatenate([core, odd, lax.axis_index("yl").reshape(1), lax.axis_index("x").reshape(1)]).astype(jnp.int32)

    weight = observed.astype(jnp.float32)
    values = dosage.astype(jnp.float32)
    sums = jnp.stack(
        [
            jnp.sum(weight, axis=0),
            jnp.sum(weight * values, axis=0),
            jnp.sum(weight * values * values, axis=0),
        ]
    )
    cnt, first, second = sum_over_samples(sums)
    mean = first / cnt
    spread = second - first * mean
    stats = jnp.stack([mean, lax.rsqrt(spread + eps * cnt)])

    zed, turned = standardize(meta, dosage, observed, stats)
    swap = lambda t: lax.ppermute(t, "core", SWAP)
    other = lax.ppermute(turned, SNP, TO_OTHER)
    near = lax.ppermute(zed, SNP, EVEN_DOWN + ODD_UP)
    zed_b = swap(zed)
    own = (turned, turn(meta, zed_b))
    rows0 = fold(meta, product(meta, own, (zed, zed_b), "own"))
    near, other = after((near, other), rows0[0])
    near = (near, swap(near))
    other = (other, swap(other[1]))
    rows2 = product(meta, own, after(near, other[1]), "along")
    pieces = across_product(meta, after(other, rows2), near, (zed, zed_b))
    rows2 = fold(meta, rows2, pieces[0])
    rows2, turned2 = gather(meta, *rows2)
    far = lax.ppermute(turned2, SNP, EVEN_UP + ODD_DOWN)
    rows1 = fold_pieces(meta, pieces, rows2, rows0[1])
    rows1, turned1 = gather(meta, *after(rows1, turned2))
    beside = lax.ppermute(rows1, SNP, TO_OTHER)
    near = lax.ppermute(after(turned1, far, beside), SNP, EVEN_UP)
    flags = jnp.concatenate([kept_flags(band, mine), odd]).astype(jnp.int32)
    return assemble(flags, far, near, turned1, rows2, beside, rows0)


def solution(mesh):
    whole_mesh = Mesh(mesh.devices.reshape(SIZES), AXES)
    return jax.shard_map(
        on_device,
        mesh=whole_mesh,
        in_specs=(P(SAMP, SNP), P(SAMP, SNP), P()),
        out_specs=P(AXES, None),
        check_vma=False,
    )
```

```python
import jax
import jax.numpy as jnp
from jax import lax
from jax.experimental import pallas as pl
from jax.experimental.pallas import tpu as pltpu
from jax.sharding import Mesh
from jax.sharding import PartitionSpec as P

eps = 1e-05

AXES = ("z", "yh", "yl", "x", "core")
SIZES = (8, 2, 2, 4, 2)
SNP = ("z", "yh")
SAMP = ("yl", "x", "core")
NSNP = 16
B = 1024
DEPTH = 1280
HALF = B // 2
STEP = 256
PIECES = 8
ROWS = 64
TURN = 32
SWAP = [(0, 1), (1, 0)]
TO_OTHER = [(i, i ^ 1) for i in range(NSNP)]
EVEN_DOWN = [(i + 2, i) for i in range(0, NSNP - 2, 2)]
ODD_UP = [(i, i + 2) for i in range(1, NSNP - 2, 2)]
EVEN_UP = [(i, i + 2) for i in range(0, NSNP - 2, 2)]
ODD_DOWN = [(i + 2, i) for i in range(1, NSNP - 2, 2)]


def sum_over_samples(x):
    parts = [
        lax.ppermute(x, ("yl", "core"), [(i, i ^ k) for i in range(4)]) for k in (1, 2, 3)
    ]
    x = x + parts[0] + parts[1] + parts[2]
    parts = [
        lax.ppermute(x, "x", [(i, (i + k) % 4) for i in range(4)]) for k in (1, 2, 3)
    ]
    return x + parts[0] + parts[1] + parts[2]


def chip_of(piece):
    return piece // 2 + 4 * (piece % 2)


def params():
    return pltpu.CompilerParams(vmem_limit_bytes=56 << 20)


def cost(flops, moved):
    return pl.CostEstimate(flops=1024, bytes_accessed=1024, transcendentals=0)


def whole(shape):
    return pl.BlockSpec(shape, lambda j, m: (0,) * len(shape))


def f32(*shape):
    return jax.ShapeDtypeStruct(shape, jnp.float32)


def bf16(*shape):
    return jax.ShapeDtypeStruct(shape, jnp.bfloat16)


def matmul(left, right):
    return jnp.dot(left, right, preferred_element_type=jnp.float32)


def standard_kernel(meta, dosage, observed, stats, zed, turned):
    weight = observed[...].astype(jnp.float32)
    values = dosage[...].astype(jnp.float32)
    z = (weight * (values - stats[0:1, :]) * stats[1:2, :]).astype(jnp.bfloat16)
    zed[...] = z
    columns = z.T
    for p in range(PIECES):
        for k in range(2):
            at = 2 * ROWS * chip_of(p) + ROWS * k
            turned[meta[0] ^ k, p] = columns[at : at + ROWS]


def standardize(meta, dosage, observed, stats):
    rows = 256
    block = lambda width: pl.BlockSpec((rows, width), lambda i, m: (i, 0))
    turned = pl.BlockSpec((2, PIECES, ROWS, rows), lambda i, m: (0, 0, 0, i))
    return pl.pallas_call(
        standard_kernel,
        name="standardize",
        out_shape=(bf16(DEPTH, B),)
        + (bf16(2, PIECES, ROWS, DEPTH),),
        grid_spec=pltpu.PrefetchScalarGridSpec(
            num_scalar_prefetch=1,
            grid=(DEPTH // rows,),
            in_specs=[block(B), block(B), whole((2, B))],
            out_specs=(block(B), turned),
        ),
        compiler_params=params(),
        cost_estimate=cost(4 * DEPTH * B, 12 * DEPTH * B),
    )(meta, dosage, observed, stats)


LEFT = (PIECES * ROWS, DEPTH)


def flat(*turned):
    return [t.reshape(-1, DEPTH) for t in turned]


def turn_kernel(meta, zed, out):
    turned = zed[...].T

    def store(part):
        out[0] = turned[ROWS * part : ROWS * (part + 1)]

    pl.when(meta[0] == 0)(lambda: store(0))
    pl.when(meta[0] != 0)(lambda: store(1))


def turn(meta, zed):
    return pl.pallas_call(
        turn_kernel,
        name="turn",
        out_shape=bf16(PIECES, ROWS, DEPTH),
        grid_spec=pltpu.PrefetchScalarGridSpec(
            num_scalar_prefetch=1,
            grid=(PIECES,),
            in_specs=[pl.BlockSpec((DEPTH, 2 * ROWS), lambda p, m: (0, p // 2 + 4 * (p % 2)))],
            out_specs=pl.BlockSpec((1, ROWS, DEPTH), lambda p, m: (p, 0, 0)),
        ),
        compiler_params=params(),
        cost_estimate=cost(DEPTH * B, 3 * DEPTH * B),
    )(meta, zed)


def product_kernel(meta, left_a, left_b, right_a, right_b, out):
    acc = matmul(left_a[...], right_a[...]) + matmul(left_b[...], right_b[...])
    out[...] = acc.reshape(PIECES, ROWS, STEP)


def product(meta, left, right, name):
    block = pl.BlockSpec((DEPTH, STEP), lambda j, m: (0, j))
    return pl.pallas_call(
        product_kernel,
        name=name,
        out_shape=f32(PIECES, ROWS, B),
        grid_spec=pltpu.PrefetchScalarGridSpec(
            num_scalar_prefetch=1,
            grid=(B // STEP,),
            in_specs=[whole(LEFT)] * 2 + [block] * 2,
            out_specs=pl.BlockSpec((PIECES, ROWS, STEP), lambda j, m: (0, 0, j)),
        ),
        compiler_params=params(),
        cost_estimate=cost(2 * DEPTH * B * B, 8 * DEPTH * B + 4 * B * B),
    )(meta, *flat(*left), *right)


def store_relative(meta, outs, acc):
    acc = acc.reshape(4, 2, ROWS, STEP)
    for x in range(4):

        @pl.when(meta[3] == x)
        def _():
            for k in range(4):
                outs[k][...] = acc[(x + k) % 4]


def along_kernel(meta, left_a, left_b, right_a, right_b, *outs):
    acc = matmul(left_a[...], right_a[...]) + matmul(left_b[...], right_b[...])
    store_relative(meta, outs, acc)


def along_product(meta, left, right):
    block = pl.BlockSpec((DEPTH, STEP), lambda j, m: (0, j))
    return pl.pallas_call(
        along_kernel,
        name="along",
        out_shape=(f32(2, ROWS, B),) * 4,
        grid_spec=pltpu.PrefetchScalarGridSpec(
            num_scalar_prefetch=1,
            grid=(B // STEP,),
            in_specs=[whole(LEFT)] * 2 + [block] * 2,
            out_specs=(pl.BlockSpec((2, ROWS, STEP), lambda j, m: (0, 0, j)),) * 4,
        ),
        compiler_params=params(),
        cost_estimate=cost(2 * DEPTH * B * B, 8 * DEPTH * B + 4 * B * B),
    )(meta, *flat(*left), *right)


def across_kernel(meta, left_a, left_b, near_a, near_b, zed_a, zed_b, *rest):
    outs, right = rest[:4], rest[4]
    odd = meta[1] == 1

    def take(a, b):
        right[:DEPTH] = a[...]
        right[DEPTH:] = b[...]

    pl.when(odd)(lambda: take(zed_a, zed_b))
    pl.when(~odd)(lambda: take(near_a, near_b))
    acc = matmul(left_a[...], right[:DEPTH]) + matmul(left_b[...], right[DEPTH:])
    store_relative(meta, outs, acc)


def across_product(meta, left, near, zed):
    block = pl.BlockSpec((DEPTH, STEP), lambda j, m: (0, j))
    return pl.pallas_call(
        across_kernel,
        name="across",
        out_shape=(f32(2, ROWS, B),) * 4,
        grid_spec=pltpu.PrefetchScalarGridSpec(
            num_scalar_prefetch=1,
            grid=(B // STEP,),
            in_specs=[whole(LEFT)] * 2 + [block] * 4,
            out_specs=(pl.BlockSpec((2, ROWS, STEP), lambda j, m: (0, 0, j)),) * 4,
            scratch_shapes=[pltpu.VMEM((2 * DEPTH, STEP), jnp.bfloat16)],
        ),
        compiler_params=params(),
        cost_estimate=cost(2 * DEPTH * B * B, 12 * DEPTH * B + 4 * B * B),
    )(meta, *flat(*left), *near, *zed)


def after(value, *others):
    return lax.optimization_barrier((value, *others))[0]


def add_kernel(meta, *refs):
    parts, (keep, send) = refs[:-2], refs[-2:]
    if len(parts) == 1:
        parts = [parts[0].at[k] for k in range(4)]
    mine = meta[2]
    for out, half in ((keep, mine), (send, 1 - mine)):
        out[...] = parts[0][half] + parts[1][half] + parts[2][half] + parts[3][half]


def add(meta, *parts):
    rows, columns = parts[0].shape[-2:]
    step = 2 * STEP
    out = pl.BlockSpec((rows, step), lambda j, m: (0, j))
    spec = lambda t: pl.BlockSpec(t.shape[:-1] + (step,), lambda j, m: (0,) * (t.ndim - 1) + (j,))
    keep, send = pl.pallas_call(
        add_kernel,
        name="add",
        out_shape=(f32(rows, columns),) * 2,
        grid_spec=pltpu.PrefetchScalarGridSpec(
            num_scalar_prefetch=1,
            grid=(columns // step,),
            in_specs=[spec(t) for t in parts],
            out_specs=(out, out),
        ),
        compiler_params=params(),
        cost_estimate=cost(6 * rows * columns, 40 * rows * columns),
    )(meta, *parts)
    return keep, lax.ppermute(send, "yl", SWAP)


def fold(meta, parts, *others):
    _, rows, columns = parts.shape
    parts = lax.all_to_all(parts.reshape(4, 2, rows, columns), "x", 0, 0)
    return add(meta, after(parts, *others))


def fold_pieces(meta, pieces, *others):
    moved = [
        lax.ppermute(pieces[k], "x", [(i, (i + k) % 4) for i in range(4)]) for k in (1, 2, 3)
    ]
    return add(meta, *after((pieces[0], *moved), *others))


def gather_kernel(meta, *refs):
    parts, (rows, packed) = refs[:-2], refs[-2:]
    if len(parts) == 1:
        parts = [parts[0].at[r] for r in range(PIECES)]
    total = parts[0][...]
    for part in parts[1:]:
        total = total + part[...]
    rows[...] = total
    for s in range(2 * STEP // ROWS):
        packed[s, :, :ROWS] = total[:TURN, ROWS * s : ROWS * (s + 1)]
        packed[s, :, ROWS:] = total[TURN:, ROWS * s : ROWS * (s + 1)]


def gather(meta, *parts):
    step = 2 * STEP
    packed = (2 * PIECES, TURN, 2 * ROWS)
    spec = lambda t: pl.BlockSpec(
        t.shape[:-1] + (step,), lambda j, m: (0,) * (t.ndim - 1) + (j,)
    )
    rows, packed = pl.pallas_call(
        gather_kernel,
        name="gather",
        out_shape=(f32(ROWS, B), f32(*packed)),
        grid_spec=pltpu.PrefetchScalarGridSpec(
            num_scalar_prefetch=1,
            grid=(B // step,),
            in_specs=[spec(t) for t in parts],
            out_specs=(
                pl.BlockSpec((ROWS, step), lambda j, m: (0, j)),
                pl.BlockSpec((step // ROWS, TURN, 2 * ROWS), lambda j, m: (j, 0, 0)),
            ),
        ),
        compiler_params=params(),
        cost_estimate=cost(ROWS * B, 16 * ROWS * B),
    )(meta, *parts)
    return rows, lax.all_to_all(packed, SAMP, 0, 0).reshape(HALF, 2 * ROWS)


def unpack(out, packed):
    turned = packed[...].T
    for s in range(2 * PIECES):
        out[:, ROWS * s : ROWS * s + TURN] = turned[:ROWS, TURN * s : TURN * (s + 1)]
        out[:, ROWS * s + TURN : ROWS * (s + 1)] = turned[ROWS:, TURN * s : TURN * (s + 1)]


def assemble_kernel(flags, far, near, here, rows2, beside, rows0_a, rows0_b, out, far_t, near_t):
    even = flags[5] == 0
    unpack(far_t, far)
    pl.when(even)(lambda: unpack(near_t, near))
    pl.when(~even)(lambda: unpack(near_t, here))
    turned, mine = far_t[...], rows2[...]
    blocks = (
        jnp.where(even, turned, mine),
        near_t[...],
        rows0_a[...] + rows0_b[...],
        beside[...],
        jnp.where(even, mine, turned),
    )
    for d, block in enumerate(blocks):
        out[:, B * d : B * (d + 1)] = jnp.where(flags[d] > 0, block, 0.0)


def assemble(flags, far, near, here, rows2, beside, rows0):
    return pl.pallas_call(
        assemble_kernel,
        name="assemble",
        out_shape=f32(ROWS, 5 * B),
        grid_spec=pltpu.PrefetchScalarGridSpec(
            num_scalar_prefetch=1,
            grid=(1,),
            in_specs=[whole((HALF, 2 * ROWS))] * 3 + [whole((ROWS, B))] * 4,
            out_specs=whole((ROWS, 5 * B)),
            scratch_shapes=[pltpu.VMEM((ROWS, B), jnp.float32)] * 2,
        ),
        compiler_params=params(),
        cost_estimate=cost(ROWS * 5 * B, 40 * ROWS * B),
    )(flags, far, near, here, rows2, beside, *rows0)


def kept_flags(band, mine):
    total = band.shape[0]
    offsets = jnp.arange(5, dtype=jnp.int32) - 2
    other = mine + offsets
    inside = (other >= 0) & (other < total)
    reach = jnp.minimum(band[mine], band[jnp.clip(other, 0, total - 1)])
    return (inside & (jnp.abs(offsets) <= reach)).astype(jnp.int32)


def on_device(dosage, observed, band):
    mine = lax.axis_index(SNP)
    odd = lax.axis_index("yh").reshape(1)
    core = lax.axis_index("core").reshape(1)
    meta = jnp.concatenate([core, odd, lax.axis_index("yl").reshape(1), lax.axis_index("x").reshape(1)]).astype(jnp.int32)

    weight = observed.astype(jnp.float32)
    values = dosage.astype(jnp.float32)
    sums = jnp.stack(
        [
            jnp.sum(weight, axis=0),
            jnp.sum(weight * values, axis=0),
            jnp.sum(weight * values * values, axis=0),
        ]
    )
    cnt, first, second = sum_over_samples(sums)
    mean = first / cnt
    spread = second - first * mean
    stats = jnp.stack([mean, lax.rsqrt(spread + eps * cnt)])

    zed, turned = standardize(meta, dosage, observed, stats)
    swap = lambda t: lax.ppermute(t, "core", SWAP)
    other = lax.ppermute(turned, SNP, TO_OTHER)
    near = lax.ppermute(zed, SNP, EVEN_DOWN + ODD_UP)
    zed_b = swap(zed)
    own = (turned, turn(meta, zed_b))
    rows0 = fold(meta, product(meta, own, (zed, zed_b), "own"))
    near, other = after((near, other), rows0[0])
    near = (near, swap(near))
    other = (other, swap(other[1]))
    rows2 = along_product(meta, own, after(near, other[1]))
    pieces = across_product(meta, after(other, rows2[0]), near, (zed, zed_b))
    rows2 = fold_pieces(meta, rows2, pieces[0])
    rows2, turned2 = gather(meta, *rows2)
    far = lax.ppermute(turned2, SNP, EVEN_UP + ODD_DOWN)
    rows1 = fold_pieces(meta, pieces, turned2, rows0[1])
    rows1, turned1 = gather(meta, *rows1)
    beside = lax.ppermute(rows1, SNP, TO_OTHER)
    near = lax.ppermute(after(turned1, far, beside), SNP, EVEN_UP)
    flags = jnp.concatenate([kept_flags(band, mine), odd]).astype(jnp.int32)
    return assemble(flags, far, near, turned1, rows2, beside, rows0)


def solution(mesh):
    whole_mesh = Mesh(mesh.devices.reshape(SIZES), AXES)
    return jax.shard_map(
        on_device,
        mesh=whole_mesh,
        in_specs=(P(SAMP, SNP), P(SAMP, SNP), P()),
        out_specs=P(AXES, None),
        check_vma=False,
    )
```

```python
import jax
import jax.numpy as jnp
from jax import lax
from jax.experimental import pallas as pl
from jax.experimental.pallas import tpu as pltpu
from jax.sharding import Mesh
from jax.sharding import PartitionSpec as P

eps = 1e-05

AXES = ("z", "yh", "yl", "x", "core")
SIZES = (8, 2, 2, 4, 2)
SNP = ("z", "yh")
SAMP = ("yl", "x", "core")
NSNP = 16
B = 1024
DEPTH = 1280
HALF = B // 2
STEP = 256
PIECES = 8
ROWS = 64
TURN = 32
SWAP = [(0, 1), (1, 0)]
TO_OTHER = [(i, i ^ 1) for i in range(NSNP)]
EVEN_DOWN = [(i + 2, i) for i in range(0, NSNP - 2, 2)]
ODD_UP = [(i, i + 2) for i in range(1, NSNP - 2, 2)]
EVEN_UP = [(i, i + 2) for i in range(0, NSNP - 2, 2)]
ODD_DOWN = [(i + 2, i) for i in range(1, NSNP - 2, 2)]


def sum_over_samples(x):
    parts = [
        lax.ppermute(x, ("yl", "core"), [(i, i ^ k) for i in range(4)]) for k in (1, 2, 3)
    ]
    x = x + parts[0] + parts[1] + parts[2]
    parts = [
        lax.ppermute(x, "x", [(i, (i + k) % 4) for i in range(4)]) for k in (1, 2, 3)
    ]
    return x + parts[0] + parts[1] + parts[2]


def chip_of(piece):
    return piece // 2 + 4 * (piece % 2)


def params():
    return pltpu.CompilerParams(vmem_limit_bytes=56 << 20)


def cost(flops, moved):
    return pl.CostEstimate(flops=1024, bytes_accessed=1024, transcendentals=0)


def whole(shape):
    return pl.BlockSpec(shape, lambda j, m: (0,) * len(shape))


def f32(*shape):
    return jax.ShapeDtypeStruct(shape, jnp.float32)


def bf16(*shape):
    return jax.ShapeDtypeStruct(shape, jnp.bfloat16)


def matmul(left, right):
    return jnp.dot(left, right, preferred_element_type=jnp.float32)


def standard_kernel(meta, dosage, observed, stats, zed, turned):
    weight = observed[...].astype(jnp.float32)
    values = dosage[...].astype(jnp.float32)
    z = (weight * (values - stats[0:1, :]) * stats[1:2, :]).astype(jnp.bfloat16)
    zed[...] = z
    columns = z.T
    for p in range(PIECES):
        for k in range(2):
            at = 2 * ROWS * chip_of(p) + ROWS * k
            turned[meta[0] ^ k, p] = columns[at : at + ROWS]


def standardize(meta, dosage, observed, stats):
    rows = 256
    block = lambda width: pl.BlockSpec((rows, width), lambda i, m: (i, 0))
    turned = pl.BlockSpec((2, PIECES, ROWS, rows), lambda i, m: (0, 0, 0, i))
    return pl.pallas_call(
        standard_kernel,
        name="standardize",
        out_shape=(bf16(DEPTH, B),)
        + (bf16(2, PIECES, ROWS, DEPTH),),
        grid_spec=pltpu.PrefetchScalarGridSpec(
            num_scalar_prefetch=1,
            grid=(DEPTH // rows,),
            in_specs=[block(B), block(B), whole((2, B))],
            out_specs=(block(B), turned),
        ),
        compiler_params=params(),
        cost_estimate=cost(4 * DEPTH * B, 12 * DEPTH * B),
    )(meta, dosage, observed, stats)


LEFT = (PIECES * ROWS, DEPTH)


def flat(*turned):
    return [t.reshape(-1, DEPTH) for t in turned]


def turn_kernel(meta, zed, out):
    turned = zed[...].T

    def store(part):
        out[0] = turned[ROWS * part : ROWS * (part + 1)]

    pl.when(meta[0] == 0)(lambda: store(0))
    pl.when(meta[0] != 0)(lambda: store(1))


def turn(meta, zed):
    return pl.pallas_call(
        turn_kernel,
        name="turn",
        out_shape=bf16(PIECES, ROWS, DEPTH),
        grid_spec=pltpu.PrefetchScalarGridSpec(
            num_scalar_prefetch=1,
            grid=(PIECES,),
            in_specs=[pl.BlockSpec((DEPTH, 2 * ROWS), lambda p, m: (0, p // 2 + 4 * (p % 2)))],
            out_specs=pl.BlockSpec((1, ROWS, DEPTH), lambda p, m: (p, 0, 0)),
        ),
        compiler_params=params(),
        cost_estimate=cost(DEPTH * B, 3 * DEPTH * B),
    )(meta, zed)


def product_kernel(meta, left_a, left_b, right_a, right_b, out):
    acc = matmul(left_a[...], right_a[...]) + matmul(left_b[...], right_b[...])
    out[...] = acc.reshape(PIECES, ROWS, STEP)


def product(meta, left, right, name):
    block = pl.BlockSpec((DEPTH, STEP), lambda j, m: (0, j))
    return pl.pallas_call(
        product_kernel,
        name=name,
        out_shape=f32(PIECES, ROWS, B),
        grid_spec=pltpu.PrefetchScalarGridSpec(
            num_scalar_prefetch=1,
            grid=(B // STEP,),
            in_specs=[whole(LEFT)] * 2 + [block] * 2,
            out_specs=pl.BlockSpec((PIECES, ROWS, STEP), lambda j, m: (0, 0, j)),
        ),
        compiler_params=params(),
        cost_estimate=cost(2 * DEPTH * B * B, 8 * DEPTH * B + 4 * B * B),
    )(meta, *flat(*left), *right)


def store_relative(meta, outs, acc):
    acc = acc.reshape(4, 2, ROWS, STEP)
    for x in range(4):

        @pl.when(meta[3] == x)
        def _():
            for k in range(4):
                outs[k][...] = acc[(x + k) % 4]


def along_kernel(meta, left_a, left_b, right_a, right_b, *outs):
    acc = matmul(left_a[...], right_a[...]) + matmul(left_b[...], right_b[...])
    store_relative(meta, outs, acc)


def along_product(meta, left, right):
    block = pl.BlockSpec((DEPTH, STEP), lambda j, m: (0, j))
    return pl.pallas_call(
        along_kernel,
        name="along",
        out_shape=(f32(2, ROWS, B),) * 4,
        grid_spec=pltpu.PrefetchScalarGridSpec(
            num_scalar_prefetch=1,
            grid=(B // STEP,),
            in_specs=[whole(LEFT)] * 2 + [block] * 2,
            out_specs=(pl.BlockSpec((2, ROWS, STEP), lambda j, m: (0, 0, j)),) * 4,
        ),
        compiler_params=params(),
        cost_estimate=cost(2 * DEPTH * B * B, 8 * DEPTH * B + 4 * B * B),
    )(meta, *flat(*left), *right)


def across_kernel(meta, left_a, left_b, near_a, near_b, zed_a, zed_b, *rest):
    outs, right = rest[:4], rest[4]
    odd = meta[1] == 1

    def take(a, b):
        right[:DEPTH] = a[...]
        right[DEPTH:] = b[...]

    pl.when(odd)(lambda: take(zed_a, zed_b))
    pl.when(~odd)(lambda: take(near_a, near_b))
    acc = matmul(left_a[...], right[:DEPTH]) + matmul(left_b[...], right[DEPTH:])
    store_relative(meta, outs, acc)


def across_product(meta, left, near, zed):
    block = pl.BlockSpec((DEPTH, STEP), lambda j, m: (0, j))
    return pl.pallas_call(
        across_kernel,
        name="across",
        out_shape=(f32(2, ROWS, B),) * 4,
        grid_spec=pltpu.PrefetchScalarGridSpec(
            num_scalar_prefetch=1,
            grid=(B // STEP,),
            in_specs=[whole(LEFT)] * 2 + [block] * 4,
            out_specs=(pl.BlockSpec((2, ROWS, STEP), lambda j, m: (0, 0, j)),) * 4,
            scratch_shapes=[pltpu.VMEM((2 * DEPTH, STEP), jnp.bfloat16)],
        ),
        compiler_params=params(),
        cost_estimate=cost(2 * DEPTH * B * B, 12 * DEPTH * B + 4 * B * B),
    )(meta, *flat(*left), *near, *zed)


def after(value, *others):
    return lax.optimization_barrier((value, *others))[0]


def add_kernel(meta, *refs):
    parts, (keep, send) = refs[:-2], refs[-2:]
    if len(parts) == 1:
        parts = [parts[0].at[k] for k in range(4)]
    mine = meta[2]
    for out, half in ((keep, mine), (send, 1 - mine)):
        out[...] = parts[0][half] + parts[1][half] + parts[2][half] + parts[3][half]


def add(meta, *parts):
    rows, columns = parts[0].shape[-2:]
    step = 2 * STEP
    out = pl.BlockSpec((rows, step), lambda j, m: (0, j))
    spec = lambda t: pl.BlockSpec(t.shape[:-1] + (step,), lambda j, m: (0,) * (t.ndim - 1) + (j,))
    keep, send = pl.pallas_call(
        add_kernel,
        name="add",
        out_shape=(f32(rows, columns),) * 2,
        grid_spec=pltpu.PrefetchScalarGridSpec(
            num_scalar_prefetch=1,
            grid=(columns // step,),
            in_specs=[spec(t) for t in parts],
            out_specs=(out, out),
        ),
        compiler_params=params(),
        cost_estimate=cost(6 * rows * columns, 40 * rows * columns),
    )(meta, *parts)
    return keep, lax.ppermute(send, "yl", SWAP)


def fold(meta, parts, *others):
    _, rows, columns = parts.shape
    parts = lax.all_to_all(parts.reshape(4, 2, rows, columns), "x", 0, 0)
    return add(meta, after(parts, *others))


def fold_pieces(meta, pieces, *others):
    moved = [
        lax.ppermute(pieces[k], "x", [(i, (i + k) % 4) for i in range(4)]) for k in (1, 2, 3)
    ]
    return add(meta, *after((pieces[0], *moved), *others))


def gather_kernel(meta, *refs):
    parts, (rows, packed) = refs[:-2], refs[-2:]
    if len(parts) == 1:
        parts = [parts[0].at[r] for r in range(PIECES)]
    total = parts[0][...]
    for part in parts[1:]:
        total = total + part[...]
    rows[...] = total
    for s in range(2 * STEP // ROWS):
        packed[s, :, :ROWS] = total[:TURN, ROWS * s : ROWS * (s + 1)]
        packed[s, :, ROWS:] = total[TURN:, ROWS * s : ROWS * (s + 1)]


def gather(meta, *parts):
    step = 2 * STEP
    packed = (2 * PIECES, TURN, 2 * ROWS)
    spec = lambda t: pl.BlockSpec(
        t.shape[:-1] + (step,), lambda j, m: (0,) * (t.ndim - 1) + (j,)
    )
    rows, packed = pl.pallas_call(
        gather_kernel,
        name="gather",
        out_shape=(f32(ROWS, B), f32(*packed)),
        grid_spec=pltpu.PrefetchScalarGridSpec(
            num_scalar_prefetch=1,
            grid=(B // step,),
            in_specs=[spec(t) for t in parts],
            out_specs=(
                pl.BlockSpec((ROWS, step), lambda j, m: (0, j)),
                pl.BlockSpec((step // ROWS, TURN, 2 * ROWS), lambda j, m: (j, 0, 0)),
            ),
        ),
        compiler_params=params(),
        cost_estimate=cost(ROWS * B, 16 * ROWS * B),
    )(meta, *parts)
    return rows, lax.all_to_all(packed, SAMP, 0, 0).reshape(HALF, 2 * ROWS)


def unpack(out, packed):
    turned = packed[...].T
    for s in range(2 * PIECES):
        out[:, ROWS * s : ROWS * s + TURN] = turned[:ROWS, TURN * s : TURN * (s + 1)]
        out[:, ROWS * s + TURN : ROWS * (s + 1)] = turned[ROWS:, TURN * s : TURN * (s + 1)]


def assemble_kernel(flags, far, near, here, rows2, beside, rows0_a, rows0_b, out, far_t, near_t):
    even = flags[5] == 0
    unpack(far_t, far)
    pl.when(even)(lambda: unpack(near_t, near))
    pl.when(~even)(lambda: unpack(near_t, here))
    turned, mine = far_t[...], rows2[...]
    blocks = (
        jnp.where(even, turned, mine),
        near_t[...],
        rows0_a[...] + rows0_b[...],
        beside[...],
        jnp.where(even, mine, turned),
    )
    for d, block in enumerate(blocks):
        out[:, B * d : B * (d + 1)] = jnp.where(flags[d] > 0, block, 0.0)


def assemble(flags, far, near, here, rows2, beside, rows0):
    return pl.pallas_call(
        assemble_kernel,
        name="assemble",
        out_shape=f32(ROWS, 5 * B),
        grid_spec=pltpu.PrefetchScalarGridSpec(
            num_scalar_prefetch=1,
            grid=(1,),
            in_specs=[whole((HALF, 2 * ROWS))] * 3 + [whole((ROWS, B))] * 4,
            out_specs=whole((ROWS, 5 * B)),
            scratch_shapes=[pltpu.VMEM((ROWS, B), jnp.float32)] * 2,
        ),
        compiler_params=params(),
        cost_estimate=cost(ROWS * 5 * B, 40 * ROWS * B),
    )(flags, far, near, here, rows2, beside, *rows0)


def kept_flags(band, mine):
    total = band.shape[0]
    offsets = jnp.arange(5, dtype=jnp.int32) - 2
    other = mine + offsets
    inside = (other >= 0) & (other < total)
    reach = jnp.minimum(band[mine], band[jnp.clip(other, 0, total - 1)])
    return (inside & (jnp.abs(offsets) <= reach)).astype(jnp.int32)


def on_device(dosage, observed, band):
    mine = lax.axis_index(SNP)
    odd = lax.axis_index("yh").reshape(1)
    core = lax.axis_index("core").reshape(1)
    meta = jnp.concatenate([core, odd, lax.axis_index("yl").reshape(1), lax.axis_index("x").reshape(1)]).astype(jnp.int32)

    weight = observed.astype(jnp.float32)
    values = dosage.astype(jnp.float32)
    sums = jnp.stack(
        [
            jnp.sum(weight, axis=0),
            jnp.sum(weight * values, axis=0),
            jnp.sum(weight * values * values, axis=0),
        ]
    )
    cnt, first, second = sum_over_samples(sums)
    mean = first / cnt
    spread = second - first * mean
    stats = jnp.stack([mean, lax.rsqrt(spread + eps * cnt)])

    zed, turned = standardize(meta, dosage, observed, stats)
    swap = lambda t: lax.ppermute(t, "core", SWAP)
    other = lax.ppermute(turned, SNP, TO_OTHER)
    near = lax.ppermute(zed, SNP, EVEN_DOWN + ODD_UP)
    zed_b = swap(zed)
    own = (turned, turn(meta, zed_b))
    rows0 = fold(meta, product(meta, own, (zed, zed_b), "own"))
    near, other = after((near, other), rows0[0])
    near = (near, swap(near))
    other = (other, swap(other[1]))
    rows2 = along_product(meta, own, after(near, other[1]))
    pieces = across_product(meta, after(other, rows2[0]), near, (zed, zed_b))
    rows2 = fold_pieces(meta, rows2, pieces[0])
    rows2, turned2 = gather(meta, *rows2)
    far = lax.ppermute(turned2, SNP, EVEN_UP + ODD_DOWN)
    rows1 = fold_pieces(meta, pieces, rows2, rows0[1])
    rows1, turned1 = gather(meta, *after(rows1, turned2))
    beside = lax.ppermute(rows1, SNP, TO_OTHER)
    near = lax.ppermute(after(turned1, far, beside), SNP, EVEN_UP)
    flags = jnp.concatenate([kept_flags(band, mine), odd]).astype(jnp.int32)
    return assemble(flags, far, near, turned1, rows2, beside, rows0)


def solution(mesh):
    whole_mesh = Mesh(mesh.devices.reshape(SIZES), AXES)
    return jax.shard_map(
        on_device,
        mesh=whole_mesh,
        in_specs=(P(SAMP, SNP), P(SAMP, SNP), P()),
        out_specs=P(AXES, None),
        check_vma=False,
    )
```

```python
import jax
import jax.numpy as jnp
from jax import lax
from jax.experimental import pallas as pl
from jax.experimental.pallas import tpu as pltpu
from jax.sharding import Mesh
from jax.sharding import PartitionSpec as P

eps = 1e-05

AXES = ("z", "yh", "yl", "x", "core")
SIZES = (8, 2, 2, 4, 2)
SNP = ("z", "yh")
SAMP = ("yl", "x", "core")
NSNP = 16
B = 1024
DEPTH = 1280
STEP = 256
PIECES = 8
ROWS = 64
SWAP = [(0, 1), (1, 0)]
TO_OTHER = [(i, i ^ 1) for i in range(NSNP)]
EVEN_DOWN = [(i + 2, i) for i in range(0, NSNP - 2, 2)]
ODD_UP = [(i, i + 2) for i in range(1, NSNP - 2, 2)]
EVEN_UP = [(i, i + 2) for i in range(0, NSNP - 2, 2)]
ODD_DOWN = [(i + 2, i) for i in range(1, NSNP - 2, 2)]


def sum_over_samples(x):
    parts = [
        lax.ppermute(x, ("yl", "core"), [(i, i ^ k) for i in range(4)]) for k in (1, 2, 3)
    ]
    x = x + parts[0] + parts[1] + parts[2]
    parts = [
        lax.ppermute(x, "x", [(i, (i + k) % 4) for i in range(4)]) for k in (1, 2, 3)
    ]
    return x + parts[0] + parts[1] + parts[2]


def chip_of(piece):
    return piece // 2 + 4 * (piece % 2)


def params():
    return pltpu.CompilerParams(vmem_limit_bytes=56 << 20)


def cost(flops, moved):
    return pl.CostEstimate(flops=1024, bytes_accessed=1024, transcendentals=0)


def whole(shape):
    return pl.BlockSpec(shape, lambda j, m: (0,) * len(shape))


def f32(*shape):
    return jax.ShapeDtypeStruct(shape, jnp.float32)


def bf16(*shape):
    return jax.ShapeDtypeStruct(shape, jnp.bfloat16)


def matmul(left, right):
    return jnp.dot(left, right, preferred_element_type=jnp.float32)


def standard_kernel(meta, dosage, observed, stats, zed, turned):
    weight = observed[...].astype(jnp.float32)
    values = dosage[...].astype(jnp.float32)
    z = (weight * (values - stats[0:1, :]) * stats[1:2, :]).astype(jnp.bfloat16)
    zed[...] = z
    columns = z.T
    for p in range(PIECES):
        for k in range(2):
            at = 2 * ROWS * chip_of(p) + ROWS * k
            turned[meta[0] ^ k, p] = columns[at : at + ROWS]


def standardize(meta, dosage, observed, stats):
    rows = 256
    block = lambda width: pl.BlockSpec((rows, width), lambda i, m: (i, 0))
    turned = pl.BlockSpec((2, PIECES, ROWS, rows), lambda i, m: (0, 0, 0, i))
    return pl.pallas_call(
        standard_kernel,
        name="standardize",
        out_shape=(bf16(DEPTH, B),)
        + (bf16(2, PIECES, ROWS, DEPTH),),
        grid_spec=pltpu.PrefetchScalarGridSpec(
            num_scalar_prefetch=1,
            grid=(DEPTH // rows,),
            in_specs=[block(B), block(B), whole((2, B))],
            out_specs=(block(B), turned),
        ),
        compiler_params=params(),
        cost_estimate=cost(4 * DEPTH * B, 12 * DEPTH * B),
    )(meta, dosage, observed, stats)


LEFT = (PIECES * ROWS, DEPTH)


def flat(*turned):
    return [t.reshape(-1, DEPTH) for t in turned]


def turn_kernel(meta, zed, out):
    turned = zed[...].T

    def store(part):
        out[0] = turned[ROWS * part : ROWS * (part + 1)]

    pl.when(meta[0] == 0)(lambda: store(0))
    pl.when(meta[0] != 0)(lambda: store(1))


def turn(meta, zed):
    return pl.pallas_call(
        turn_kernel,
        name="turn",
        out_shape=bf16(PIECES, ROWS, DEPTH),
        grid_spec=pltpu.PrefetchScalarGridSpec(
            num_scalar_prefetch=1,
            grid=(PIECES,),
            in_specs=[pl.BlockSpec((DEPTH, 2 * ROWS), lambda p, m: (0, p // 2 + 4 * (p % 2)))],
            out_specs=pl.BlockSpec((1, ROWS, DEPTH), lambda p, m: (p, 0, 0)),
        ),
        compiler_params=params(),
        cost_estimate=cost(DEPTH * B, 3 * DEPTH * B),
    )(meta, zed)


def product_kernel(meta, left_a, left_b, right_a, right_b, out):
    acc = matmul(left_a[...], right_a[...]) + matmul(left_b[...], right_b[...])
    out[...] = acc.reshape(PIECES, ROWS, STEP)


def product(meta, left, right, name):
    block = pl.BlockSpec((DEPTH, STEP), lambda j, m: (0, j))
    return pl.pallas_call(
        product_kernel,
        name=name,
        out_shape=f32(PIECES, ROWS, B),
        grid_spec=pltpu.PrefetchScalarGridSpec(
            num_scalar_prefetch=1,
            grid=(B // STEP,),
            in_specs=[whole(LEFT)] * 2 + [block] * 2,
            out_specs=pl.BlockSpec((PIECES, ROWS, STEP), lambda j, m: (0, 0, j)),
        ),
        compiler_params=params(),
        cost_estimate=cost(2 * DEPTH * B * B, 8 * DEPTH * B + 4 * B * B),
    )(meta, *flat(*left), *right)


def store_relative(meta, outs, acc):
    acc = acc.reshape(4, 2, ROWS, STEP)
    for x in range(4):

        @pl.when(meta[3] == x)
        def _():
            for k in range(4):
                outs[k][...] = acc[(x + k) % 4]


def along_kernel(meta, left_a, left_b, right_a, right_b, *outs):
    acc = matmul(left_a[...], right_a[...]) + matmul(left_b[...], right_b[...])
    store_relative(meta, outs, acc)


def along_product(meta, left, right):
    block = pl.BlockSpec((DEPTH, STEP), lambda j, m: (0, j))
    return pl.pallas_call(
        along_kernel,
        name="along",
        out_shape=(f32(2, ROWS, B),) * 4,
        grid_spec=pltpu.PrefetchScalarGridSpec(
            num_scalar_prefetch=1,
            grid=(B // STEP,),
            in_specs=[whole(LEFT)] * 2 + [block] * 2,
            out_specs=(pl.BlockSpec((2, ROWS, STEP), lambda j, m: (0, 0, j)),) * 4,
        ),
        compiler_params=params(),
        cost_estimate=cost(2 * DEPTH * B * B, 8 * DEPTH * B + 4 * B * B),
    )(meta, *flat(*left), *right)


def across_kernel(meta, left_a, left_b, near_a, near_b, zed_a, zed_b, *rest):
    outs, right = rest[:4], rest[4]
    odd = meta[1] == 1

    def take(a, b):
        right[:DEPTH] = a[...]
        right[DEPTH:] = b[...]

    pl.when(odd)(lambda: take(zed_a, zed_b))
    pl.when(~odd)(lambda: take(near_a, near_b))
    acc = matmul(left_a[...], right[:DEPTH]) + matmul(left_b[...], right[DEPTH:])
    store_relative(meta, outs, acc)


def across_product(meta, left, near, zed):
    block = pl.BlockSpec((DEPTH, STEP), lambda j, m: (0, j))
    return pl.pallas_call(
        across_kernel,
        name="across",
        out_shape=(f32(2, ROWS, B),) * 4,
        grid_spec=pltpu.PrefetchScalarGridSpec(
            num_scalar_prefetch=1,
            grid=(B // STEP,),
            in_specs=[whole(LEFT)] * 2 + [block] * 4,
            out_specs=(pl.BlockSpec((2, ROWS, STEP), lambda j, m: (0, 0, j)),) * 4,
            scratch_shapes=[pltpu.VMEM((2 * DEPTH, STEP), jnp.bfloat16)],
        ),
        compiler_params=params(),
        cost_estimate=cost(2 * DEPTH * B * B, 12 * DEPTH * B + 4 * B * B),
    )(meta, *flat(*left), *near, *zed)


def after(value, *others):
    return lax.optimization_barrier((value, *others))[0]


def add_kernel(meta, *refs):
    parts, (keep, send) = refs[:-2], refs[-2:]
    if len(parts) == 1:
        parts = [parts[0].at[k] for k in range(4)]
    mine = meta[2]
    for out, half in ((keep, mine), (send, 1 - mine)):
        out[...] = parts[0][half] + parts[1][half] + parts[2][half] + parts[3][half]


def add(meta, *parts):
    rows, columns = parts[0].shape[-2:]
    step = 2 * STEP
    out = pl.BlockSpec((rows, step), lambda j, m: (0, j))
    spec = lambda t: pl.BlockSpec(t.shape[:-1] + (step,), lambda j, m: (0,) * (t.ndim - 1) + (j,))
    keep, send = pl.pallas_call(
        add_kernel,
        name="add",
        out_shape=(f32(rows, columns),) * 2,
        grid_spec=pltpu.PrefetchScalarGridSpec(
            num_scalar_prefetch=1,
            grid=(columns // step,),
            in_specs=[spec(t) for t in parts],
            out_specs=(out, out),
        ),
        compiler_params=params(),
        cost_estimate=cost(6 * rows * columns, 40 * rows * columns),
    )(meta, *parts)
    return keep, lax.ppermute(send, "yl", SWAP)


def fold(meta, parts, *others):
    _, rows, columns = parts.shape
    parts = lax.all_to_all(parts.reshape(4, 2, rows, columns), "x", 0, 0)
    return add(meta, after(parts, *others))


def fold_pieces(meta, pieces, *others):
    moved = [
        lax.ppermute(pieces[k], "x", [(i, (i + k) % 4) for i in range(4)]) for k in (1, 2, 3)
    ]
    return add(meta, *after((pieces[0], *moved), *others))


def gather_kernel(meta, along_a, along_b, across_a, across_b, rows2, rows1, both):
    rows2[...] = along_a[...] + along_b[...]
    rows1[...] = across_a[...] + across_b[...]
    for s in range(2 * PIECES):
        both[s, :, :ROWS] = rows2[:, ROWS * s : ROWS * (s + 1)]
        both[s, :, ROWS:] = rows1[:, ROWS * s : ROWS * (s + 1)]


def gather(meta, *parts):
    both = (2 * PIECES, ROWS, 2 * ROWS)
    return pl.pallas_call(
        gather_kernel,
        name="gather",
        out_shape=(f32(ROWS, B), f32(ROWS, B), f32(*both)),
        grid_spec=pltpu.PrefetchScalarGridSpec(
            num_scalar_prefetch=1,
            grid=(1,),
            in_specs=[whole((ROWS, B))] * 4,
            out_specs=(whole((ROWS, B)), whole((ROWS, B)), whole(both)),
        ),
        compiler_params=params(),
        cost_estimate=cost(2 * ROWS * B, 32 * ROWS * B),
    )(meta, *parts)


def assemble_kernel(flags, far, here, rows2, beside, rows0_a, rows0_b, out):
    even = flags[5] == 0
    far_turned = far[...].T
    near = jnp.where(even, far_turned[ROWS:], here[...].T[ROWS:])
    far2 = far_turned[:ROWS]
    mine2 = rows2[...]
    blocks = (
        jnp.where(even, far2, mine2),
        near,
        rows0_a[...] + rows0_b[...],
        beside[...],
        jnp.where(even, mine2, far2),
    )
    for d, block in enumerate(blocks):
        out[:, B * d : B * (d + 1)] = jnp.where(flags[d] > 0, block, 0.0)


def assemble(flags, far, here, rows2, beside, rows0):
    return pl.pallas_call(
        assemble_kernel,
        name="assemble",
        out_shape=f32(ROWS, 5 * B),
        grid_spec=pltpu.PrefetchScalarGridSpec(
            num_scalar_prefetch=1,
            grid=(1,),
            in_specs=[whole((B, 2 * ROWS))] * 2 + [whole((ROWS, B))] * 4,
            out_specs=whole((ROWS, 5 * B)),
        ),
        compiler_params=params(),
        cost_estimate=cost(ROWS * 5 * B, 40 * ROWS * B),
    )(flags, far, here, rows2, beside, *rows0)


def kept_flags(band, mine):
    total = band.shape[0]
    offsets = jnp.arange(5, dtype=jnp.int32) - 2
    other = mine + offsets
    inside = (other >= 0) & (other < total)
    reach = jnp.minimum(band[mine], band[jnp.clip(other, 0, total - 1)])
    return (inside & (jnp.abs(offsets) <= reach)).astype(jnp.int32)


def on_device(dosage, observed, band):
    mine = lax.axis_index(SNP)
    odd = lax.axis_index("yh").reshape(1)
    core = lax.axis_index("core").reshape(1)
    meta = jnp.concatenate([core, odd, lax.axis_index("yl").reshape(1), lax.axis_index("x").reshape(1)]).astype(jnp.int32)

    weight = observed.astype(jnp.float32)
    values = dosage.astype(jnp.float32)
    sums = jnp.stack(
        [
            jnp.sum(weight, axis=0),
            jnp.sum(weight * values, axis=0),
            jnp.sum(weight * values * values, axis=0),
        ]
    )
    cnt, first, second = sum_over_samples(sums)
    mean = first / cnt
    spread = second - first * mean
    stats = jnp.stack([mean, lax.rsqrt(spread + eps * cnt)])

    zed, turned = standardize(meta, dosage, observed, stats)
    swap = lambda t: lax.ppermute(t, "core", SWAP)
    other = lax.ppermute(turned, SNP, TO_OTHER)
    near = lax.ppermute(zed, SNP, EVEN_DOWN + ODD_UP)
    zed_b = swap(zed)
    own = (turned, turn(meta, zed_b))
    rows0 = fold(meta, product(meta, own, (zed, zed_b), "own"))
    near, other = after((near, other), rows0[0])
    near = (near, swap(near))
    other = (other, swap(other[1]))
    rows2 = along_product(meta, own, after(near, other[1]))
    pieces = across_product(meta, after(other, rows2[0]), near, (zed, zed_b))
    rows2 = fold_pieces(meta, rows2, pieces[0])
    rows1 = fold_pieces(meta, pieces, rows2[1], rows0[1])
    rows2, rows1, both = gather(meta, *rows2, *rows1)
    beside = lax.ppermute(rows1, SNP, TO_OTHER)
    here = lax.all_to_all(both, SAMP, 0, 0).reshape(B, 2 * ROWS)
    far = lax.ppermute(after(here, beside), SNP, EVEN_UP + ODD_DOWN)
    flags = jnp.concatenate([kept_flags(band, mine), odd]).astype(jnp.int32)
    return assemble(flags, far, here, rows2, beside, rows0)


def solution(mesh):
    whole_mesh = Mesh(mesh.devices.reshape(SIZES), AXES)
    return jax.shard_map(
        on_device,
        mesh=whole_mesh,
        in_specs=(P(SAMP, SNP), P(SAMP, SNP), P()),
        out_specs=P(AXES, None),
        check_vma=False,
    )
```

```python
import jax
import jax.numpy as jnp
from jax import lax
from jax.experimental import pallas as pl
from jax.experimental.pallas import tpu as pltpu
from jax.sharding import Mesh
from jax.sharding import PartitionSpec as P

eps = 1e-05

AXES = ("z", "yh", "yl", "x", "core")
SIZES = (8, 2, 2, 4, 2)
SNP = ("z", "yh")
SAMP = ("yl", "x", "core")
NSNP = 16
B = 1024
DEPTH = 1280
HALF = B // 2
STEP = 512
PIECES = 8
ROWS = 64
TURN = 32
SWAP = [(0, 1), (1, 0)]
TO_OTHER = [(i, i ^ 1) for i in range(NSNP)]
EVEN_DOWN = [(i + 2, i) for i in range(0, NSNP - 2, 2)]
ODD_UP = [(i, i + 2) for i in range(1, NSNP - 2, 2)]
EVEN_UP = [(i, i + 2) for i in range(0, NSNP - 2, 2)]
ODD_DOWN = [(i + 2, i) for i in range(1, NSNP - 2, 2)]


def sum_over_samples(x):
    parts = [
        lax.ppermute(x, ("yl", "core"), [(i, i ^ k) for i in range(4)]) for k in (1, 2, 3)
    ]
    x = x + parts[0] + parts[1] + parts[2]
    parts = [
        lax.ppermute(x, "x", [(i, (i + k) % 4) for i in range(4)]) for k in (1, 2, 3)
    ]
    return x + parts[0] + parts[1] + parts[2]


def chip_of(piece):
    return piece // 2 + 4 * (piece % 2)


def params():
    return pltpu.CompilerParams(vmem_limit_bytes=56 << 20)


def cost(flops, moved):
    return pl.CostEstimate(flops=1024, bytes_accessed=1024, transcendentals=0)


def whole(shape):
    return pl.BlockSpec(shape, lambda j, m: (0,) * len(shape))


def f32(*shape):
    return jax.ShapeDtypeStruct(shape, jnp.float32)


def bf16(*shape):
    return jax.ShapeDtypeStruct(shape, jnp.bfloat16)


def matmul(left, right):
    return jnp.dot(left, right, preferred_element_type=jnp.float32)


def standard_kernel(meta, dosage, observed, stats, zed, turned):
    weight = observed[...].astype(jnp.float32)
    values = dosage[...].astype(jnp.float32)
    z = (weight * (values - stats[0:1, :]) * stats[1:2, :]).astype(jnp.bfloat16)
    zed[...] = z
    columns = z.T
    for p in range(PIECES):
        for k in range(2):
            at = 2 * ROWS * chip_of(p) + ROWS * k
            turned[meta[0] ^ k, p] = columns[at : at + ROWS]


def standardize(meta, dosage, observed, stats):
    rows = 256
    block = lambda width: pl.BlockSpec((rows, width), lambda i, m: (i, 0))
    turned = pl.BlockSpec((2, PIECES, ROWS, rows), lambda i, m: (0, 0, 0, i))
    return pl.pallas_call(
        standard_kernel,
        name="standardize",
        out_shape=(bf16(DEPTH, B),)
        + (bf16(2, PIECES, ROWS, DEPTH),),
        grid_spec=pltpu.PrefetchScalarGridSpec(
            num_scalar_prefetch=1,
            grid=(DEPTH // rows,),
            in_specs=[block(B), block(B), whole((2, B))],
            out_specs=(block(B), turned),
        ),
        compiler_params=params(),
        cost_estimate=cost(4 * DEPTH * B, 12 * DEPTH * B),
    )(meta, dosage, observed, stats)


LEFT = (PIECES * ROWS, DEPTH)


def flat(*turned):
    return [t.reshape(-1, DEPTH) for t in turned]


def turn_kernel(meta, zed, out):
    turned = zed[...].T

    def store(part):
        out[0] = turned[ROWS * part : ROWS * (part + 1)]

    pl.when(meta[0] == 0)(lambda: store(0))
    pl.when(meta[0] != 0)(lambda: store(1))


def turn(meta, zed):
    return pl.pallas_call(
        turn_kernel,
        name="turn",
        out_shape=bf16(PIECES, ROWS, DEPTH),
        grid_spec=pltpu.PrefetchScalarGridSpec(
            num_scalar_prefetch=1,
            grid=(PIECES,),
            in_specs=[pl.BlockSpec((DEPTH, 2 * ROWS), lambda p, m: (0, p // 2 + 4 * (p % 2)))],
            out_specs=pl.BlockSpec((1, ROWS, DEPTH), lambda p, m: (p, 0, 0)),
        ),
        compiler_params=params(),
        cost_estimate=cost(DEPTH * B, 3 * DEPTH * B),
    )(meta, zed)


def product_kernel(meta, left_a, left_b, right_a, right_b, out):
    acc = matmul(left_a[...], right_a[...]) + matmul(left_b[...], right_b[...])
    out[...] = acc.reshape(PIECES, ROWS, STEP)


def product(meta, left, right, name):
    block = pl.BlockSpec((DEPTH, STEP), lambda j, m: (0, j))
    return pl.pallas_call(
        product_kernel,
        name=name,
        out_shape=f32(PIECES, ROWS, B),
        grid_spec=pltpu.PrefetchScalarGridSpec(
            num_scalar_prefetch=1,
            grid=(B // STEP,),
            in_specs=[whole(LEFT)] * 2 + [block] * 2,
            out_specs=pl.BlockSpec((PIECES, ROWS, STEP), lambda j, m: (0, 0, j)),
        ),
        compiler_params=params(),
        cost_estimate=cost(2 * DEPTH * B * B, 8 * DEPTH * B + 4 * B * B),
    )(meta, *flat(*left), *right)


def store_relative(meta, outs, acc):
    acc = acc.reshape(4, 2, ROWS, STEP)
    for x in range(4):

        @pl.when(meta[3] == x)
        def _():
            for k in range(4):
                outs[k][...] = acc[(x + k) % 4]


def along_kernel(meta, left_a, left_b, right_a, right_b, *outs):
    acc = matmul(left_a[...], right_a[...]) + matmul(left_b[...], right_b[...])
    store_relative(meta, outs, acc)


def along_product(meta, left, right):
    block = pl.BlockSpec((DEPTH, STEP), lambda j, m: (0, j))
    return pl.pallas_call(
        along_kernel,
        name="along",
        out_shape=(f32(2, ROWS, B),) * 4,
        grid_spec=pltpu.PrefetchScalarGridSpec(
            num_scalar_prefetch=1,
            grid=(B // STEP,),
            in_specs=[whole(LEFT)] * 2 + [block] * 2,
            out_specs=(pl.BlockSpec((2, ROWS, STEP), lambda j, m: (0, 0, j)),) * 4,
        ),
        compiler_params=params(),
        cost_estimate=cost(2 * DEPTH * B * B, 8 * DEPTH * B + 4 * B * B),
    )(meta, *flat(*left), *right)


def across_kernel(meta, left_a, left_b, near_a, near_b, zed_a, zed_b, *rest):
    outs, right = rest[:4], rest[4]
    odd = meta[1] == 1

    def take(a, b):
        right[:DEPTH] = a[...]
        right[DEPTH:] = b[...]

    pl.when(odd)(lambda: take(zed_a, zed_b))
    pl.when(~odd)(lambda: take(near_a, near_b))
    acc = matmul(left_a[...], right[:DEPTH]) + matmul(left_b[...], right[DEPTH:])
    store_relative(meta, outs, acc)


def across_product(meta, left, near, zed):
    block = pl.BlockSpec((DEPTH, STEP), lambda j, m: (0, j))
    return pl.pallas_call(
        across_kernel,
        name="across",
        out_shape=(f32(2, ROWS, B),) * 4,
        grid_spec=pltpu.PrefetchScalarGridSpec(
            num_scalar_prefetch=1,
            grid=(B // STEP,),
            in_specs=[whole(LEFT)] * 2 + [block] * 4,
            out_specs=(pl.BlockSpec((2, ROWS, STEP), lambda j, m: (0, 0, j)),) * 4,
            scratch_shapes=[pltpu.VMEM((2 * DEPTH, STEP), jnp.bfloat16)],
        ),
        compiler_params=params(),
        cost_estimate=cost(2 * DEPTH * B * B, 12 * DEPTH * B + 4 * B * B),
    )(meta, *flat(*left), *near, *zed)


def after(value, *others):
    return lax.optimization_barrier((value, *others))[0]


def add_kernel(meta, *refs):
    parts, (keep, send) = refs[:-2], refs[-2:]
    if len(parts) == 1:
        parts = [parts[0].at[k] for k in range(4)]
    mine = meta[2]
    for out, half in ((keep, mine), (send, 1 - mine)):
        out[...] = parts[0][half] + parts[1][half] + parts[2][half] + parts[3][half]


def add(meta, *parts):
    rows, columns = parts[0].shape[-2:]
    step = 2 * STEP
    out = pl.BlockSpec((rows, step), lambda j, m: (0, j))
    spec = lambda t: pl.BlockSpec(t.shape[:-1] + (step,), lambda j, m: (0,) * (t.ndim - 1) + (j,))
    keep, send = pl.pallas_call(
        add_kernel,
        name="add",
        out_shape=(f32(rows, columns),) * 2,
        grid_spec=pltpu.PrefetchScalarGridSpec(
            num_scalar_prefetch=1,
            grid=(columns // step,),
            in_specs=[spec(t) for t in parts],
            out_specs=(out, out),
        ),
        compiler_params=params(),
        cost_estimate=cost(6 * rows * columns, 40 * rows * columns),
    )(meta, *parts)
    return keep, lax.ppermute(send, "yl", SWAP)


def fold(meta, parts, *others):
    _, rows, columns = parts.shape
    parts = lax.all_to_all(parts.reshape(4, 2, rows, columns), "x", 0, 0)
    return add(meta, after(parts, *others))


def fold_pieces(meta, pieces, *others):
    moved = [
        lax.ppermute(pieces[k], "x", [(i, (i + k) % 4) for i in range(4)]) for k in (1, 2, 3)
    ]
    return add(meta, *after((pieces[0], *moved), *others))


def gather_kernel(meta, *refs):
    parts, (rows, packed) = refs[:-2], refs[-2:]
    if len(parts) == 1:
        parts = [parts[0].at[r] for r in range(PIECES)]
    total = parts[0][...]
    for part in parts[1:]:
        total = total + part[...]
    rows[...] = total
    for s in range(2 * STEP // ROWS):
        packed[s, :, :ROWS] = total[:TURN, ROWS * s : ROWS * (s + 1)]
        packed[s, :, ROWS:] = total[TURN:, ROWS * s : ROWS * (s + 1)]


def gather(meta, *parts):
    step = 2 * STEP
    packed = (2 * PIECES, TURN, 2 * ROWS)
    spec = lambda t: pl.BlockSpec(
        t.shape[:-1] + (step,), lambda j, m: (0,) * (t.ndim - 1) + (j,)
    )
    rows, packed = pl.pallas_call(
        gather_kernel,
        name="gather",
        out_shape=(f32(ROWS, B), f32(*packed)),
        grid_spec=pltpu.PrefetchScalarGridSpec(
            num_scalar_prefetch=1,
            grid=(B // step,),
            in_specs=[spec(t) for t in parts],
            out_specs=(
                pl.BlockSpec((ROWS, step), lambda j, m: (0, j)),
                pl.BlockSpec((step // ROWS, TURN, 2 * ROWS), lambda j, m: (j, 0, 0)),
            ),
        ),
        compiler_params=params(),
        cost_estimate=cost(ROWS * B, 16 * ROWS * B),
    )(meta, *parts)
    return rows, lax.all_to_all(packed, SAMP, 0, 0).reshape(HALF, 2 * ROWS)


def unpack(out, packed):
    turned = packed[...].T
    for s in range(2 * PIECES):
        out[:, ROWS * s : ROWS * s + TURN] = turned[:ROWS, TURN * s : TURN * (s + 1)]
        out[:, ROWS * s + TURN : ROWS * (s + 1)] = turned[ROWS:, TURN * s : TURN * (s + 1)]


def assemble_kernel(flags, far, near, here, rows2, beside, rows0_a, rows0_b, out, far_t, near_t):
    even = flags[5] == 0
    unpack(far_t, far)
    pl.when(even)(lambda: unpack(near_t, near))
    pl.when(~even)(lambda: unpack(near_t, here))
    turned, mine = far_t[...], rows2[...]
    blocks = (
        jnp.where(even, turned, mine),
        near_t[...],
        rows0_a[...] + rows0_b[...],
        beside[...],
        jnp.where(even, mine, turned),
    )
    for d, block in enumerate(blocks):
        out[:, B * d : B * (d + 1)] = jnp.where(flags[d] > 0, block, 0.0)


def assemble(flags, far, near, here, rows2, beside, rows0):
    return pl.pallas_call(
        assemble_kernel,
        name="assemble",
        out_shape=f32(ROWS, 5 * B),
        grid_spec=pltpu.PrefetchScalarGridSpec(
            num_scalar_prefetch=1,
            grid=(1,),
            in_specs=[whole((HALF, 2 * ROWS))] * 3 + [whole((ROWS, B))] * 4,
            out_specs=whole((ROWS, 5 * B)),
            scratch_shapes=[pltpu.VMEM((ROWS, B), jnp.float32)] * 2,
        ),
        compiler_params=params(),
        cost_estimate=cost(ROWS * 5 * B, 40 * ROWS * B),
    )(flags, far, near, here, rows2, beside, *rows0)


def kept_flags(band, mine):
    total = band.shape[0]
    offsets = jnp.arange(5, dtype=jnp.int32) - 2
    other = mine + offsets
    inside = (other >= 0) & (other < total)
    reach = jnp.minimum(band[mine], band[jnp.clip(other, 0, total - 1)])
    return (inside & (jnp.abs(offsets) <= reach)).astype(jnp.int32)


def on_device(dosage, observed, band):
    mine = lax.axis_index(SNP)
    odd = lax.axis_index("yh").reshape(1)
    core = lax.axis_index("core").reshape(1)
    meta = jnp.concatenate([core, odd, lax.axis_index("yl").reshape(1), lax.axis_index("x").reshape(1)]).astype(jnp.int32)

    weight = observed.astype(jnp.float32)
    values = dosage.astype(jnp.float32)
    sums = jnp.stack(
        [
            jnp.sum(weight, axis=0),
            jnp.sum(weight * values, axis=0),
            jnp.sum(weight * values * values, axis=0),
        ]
    )
    cnt, first, second = sum_over_samples(sums)
    mean = first / cnt
    spread = second - first * mean
    stats = jnp.stack([mean, lax.rsqrt(spread + eps * cnt)])

    zed, turned = standardize(meta, dosage, observed, stats)
    swap = lambda t: lax.ppermute(t, "core", SWAP)
    other = lax.ppermute(turned, SNP, TO_OTHER)
    near = lax.ppermute(zed, SNP, EVEN_DOWN + ODD_UP)
    zed_b = swap(zed)
    own = (turned, turn(meta, zed_b))
    rows0 = fold(meta, product(meta, own, (zed, zed_b), "own"))
    near, other = after((near, other), rows0[0])
    near = (near, swap(near))
    other = (other, swap(other[1]))
    rows2 = along_product(meta, own, after(near, other[1]))
    pieces = across_product(meta, after(other, rows2[0]), near, (zed, zed_b))
    rows2 = fold_pieces(meta, rows2, pieces[0])
    rows2, turned2 = gather(meta, *rows2)
    far = lax.ppermute(turned2, SNP, EVEN_UP + ODD_DOWN)
    rows1 = fold_pieces(meta, pieces, turned2, rows0[1])
    rows1, turned1 = gather(meta, *rows1)
    beside = lax.ppermute(rows1, SNP, TO_OTHER)
    near = lax.ppermute(after(turned1, far, beside), SNP, EVEN_UP)
    flags = jnp.concatenate([kept_flags(band, mine), odd]).astype(jnp.int32)
    return assemble(flags, far, near, turned1, rows2, beside, rows0)


def solution(mesh):
    whole_mesh = Mesh(mesh.devices.reshape(SIZES), AXES)
    return jax.shard_map(
        on_device,
        mesh=whole_mesh,
        in_specs=(P(SAMP, SNP), P(SAMP, SNP), P()),
        out_specs=P(AXES, None),
        check_vma=False,
    )
```
